32 devices in a mesh: fsdp: 2 (over x), ctx: 4 (over z), tp: 4 (over y, core).
Axes of the slice: x: 2, y: 2, z: 4, core: 2. Of those that a mesh axis runs over, the one named last changes fastest.
Arguments:
- inputs: bfloat16 [2, 1024, 2048], P('fsdp', 'ctx'), may hold values from -6 to 6
- cotangent: bfloat16 [2, 1024, 2048], P('fsdp', 'ctx'), may hold values from -6 to 6
- prefix: int32 [2], P('fsdp'), may hold values from 102 to 512
- attn_gain: bfloat16 [2048], P('fsdp'), may hold values from 0.099609375 to 1.8984375
- w_query: bfloat16 [2048, 2048], P('fsdp', 'tp'), may hold values from -0.125 to 0.125
- key_projection: bfloat16 [2048, 512], P('fsdp', 'tp'), may hold values from -0.125 to 0.125
- value_projection: bfloat16 [2048, 512], P('fsdp', 'tp'), may hold values from -0.125 to 0.125
- w_out: bfloat16 [2048, 2048], P('fsdp', 'tp'), may hold values from -1 to 1
- ffn_gain: bfloat16 [2048], P('fsdp'), may hold values from 0.099609375 to 1.8984375
- w_gate: bfloat16 [2048, 8192], P('fsdp', 'tp'), may hold values from -0.125 to 0.125
- w_up: bfloat16 [2048, 8192], P('fsdp', 'tp'), may hold values from -0.125 to 0.125
- w_down: bfloat16 [2048, 8192], P('fsdp', 'tp'), may hold values from -0.0625 to 0.0625
Outputs:
- output: bfloat16 [2, 1024, 2048], P('fsdp', 'ctx')
- grad_input: bfloat16 [2, 1024, 2048], P('fsdp', 'ctx')
- grad_attn_gain: float32 [2048], P('fsdp')
- grad_query: float32 [2048, 2048], P('fsdp', 'tp')
- grad_key: float32 [2048, 512], P('fsdp', 'tp')
- grad_value: float32 [2048, 512], P('fsdp', 'tp')
- grad_out: float32 [2048, 2048], P('fsdp', 'tp')
- grad_ffn_gain: float32 [2048], P('fsdp')
- grad_gate: float32 [2048, 8192], P('fsdp', 'tp')
- grad_up: float32 [2048, 8192], P('fsdp', 'tp')
- grad_down: float32 [2048, 8192], P('fsdp', 'tp')
The draws below stay inside these ranges and needn't reach their ends.
Inputs may be any that keep to these rules, and one draw needn't show every extreme that they name: prefix holds, for each sequence, how many of its leading positions every position of that sequence may attend.
All inputs are finite; a program needn't handle non-finite values.
Results may differ from the reference program's by a relative error of at most 0.024.
Values may be sent and summed in bfloat16 or wider, within the bound.
A program may use at most 192 MiB of HBM per device.

```python
import math
import jax
import jax.numpy as jnp
from jax import lax

MODEL_DIM = 2048
QUERY_HEAD_COUNT = 32
KEY_VALUE_HEADS = 8
HEAD_SIZE = 64
FF = 8192
SEQ_LEN = 1024
SEQS = 2


def block_levels(stream_key, extent, split, least, top_value):
    gain = 1.0
    for dim, parts in split:
        heights = jax.random.uniform(jax.random.fold_in(jax.random.fold_in(stream_key, 6), dim), (parts,), jnp.float32, least / len(split), top_value / len(split))
        gain = gain * jnp.repeat(jnp.exp(heights), extent[dim] // parts).reshape((-1,) + (1,) * (len(extent) - 1 - dim))
    return gain


def bell_draw(key, shape, width, reach, cuts=(), held_as=jnp.bfloat16):
    array = jax.random.normal(key, shape, jnp.float32) * width
    if len(cuts) > 0:
        array = block_levels(key, shape, cuts, -0.22, 0.18) * array
    return jnp.clip(array, min=-reach, max=reach).astype(held_as)


def setup_inputs(seed: int = 0) -> dict:
    streams_of = jax.random.split(jax.random.key(seed), 13)
    return {
        "inputs": bell_draw(streams_of[0], (SEQS, SEQ_LEN, MODEL_DIM), 1.0, 6.0, ((0, 2), (1, 4))),
        "cotangent": bell_draw(streams_of[1], (SEQS, SEQ_LEN, MODEL_DIM), 1.0, 6.0, ((0, 2), (1, 4))),
        "prefix": jax.random.randint(streams_of[2], (SEQS,), SEQ_LEN // 10, SEQ_LEN // 2 + 1).astype(jnp.int32),
        "attn_gain": jnp.clip(1.0 + 0.18 * jax.random.normal(streams_of[3], (MODEL_DIM,), jnp.float32), 0.099609375, 1.8984375).astype(jnp.bfloat16),
        "w_query": bell_draw(streams_of[4], (MODEL_DIM, QUERY_HEAD_COUNT * HEAD_SIZE), MODEL_DIM ** -0.5, 0.125, ((0, 2), (1, 4))),
        "key_projection": bell_draw(streams_of[5], (MODEL_DIM, KEY_VALUE_HEADS * HEAD_SIZE), MODEL_DIM ** -0.5, 0.125, ((0, 2), (1, 4))),
        "value_projection": bell_draw(streams_of[6], (MODEL_DIM, KEY_VALUE_HEADS * HEAD_SIZE), MODEL_DIM ** -0.5, 0.125, ((0, 2), (1, 4))),
        "w_out": bell_draw(streams_of[7], (MODEL_DIM, QUERY_HEAD_COUNT * HEAD_SIZE), (QUERY_HEAD_COUNT * HEAD_SIZE // 64) ** -0.5, 1.0, ((0, 2), (1, 4))),
        "ffn_gain": jnp.clip(1.0 + 0.18 * jax.random.normal(streams_of[8], (MODEL_DIM,), jnp.float32), 0.099609375, 1.8984375).astype(jnp.bfloat16),
        "w_gate": bell_draw(streams_of[9], (MODEL_DIM, FF), MODEL_DIM ** -0.5, 0.125, ((0, 2), (1, 4))),
        "w_up": bell_draw(streams_of[10], (MODEL_DIM, FF), MODEL_DIM ** -0.5, 0.125, ((0, 2), (1, 4))),
        "w_down": bell_draw(streams_of[11], (MODEL_DIM, FF), FF ** -0.5, 0.0625, ((0, 2), (1, 4))),
    }


EPSILON = 1e-05
THETA = 500000.0
MASKED = -1e+30

@jax.custom_vjp
def lower_triangle(v):
    return lax.optimization_barrier(v.astype(jnp.bfloat16)).astype(jnp.float32)

@jax.custom_vjp
def lower_triangle_back(v):
    return v

def low_keep(v):
    return (lower_triangle(v), None)

def low_pass(kept, grad):
    return (grad,)

def back_keep(v):
    return (v, None)

def back_low(kept, grad):
    return (lower_triangle(grad),)
lower_triangle.defvjp(low_keep, low_pass)
lower_triangle_back.defvjp(back_keep, back_low)

def matrix_product(left, right):
    return jnp.dot(left, right, precision=lax.Precision.HIGHEST)

def tables(length_total):
    position = jnp.arange(length_total, dtype=jnp.int32).astype(jnp.float32)
    exponent = jnp.arange(HEAD_SIZE // 2, dtype=jnp.int32).astype(jnp.float32) * (2.0 / HEAD_SIZE)
    angles = position[:, None] * jnp.power(THETA, -exponent)[None, :]
    return (jnp.cos(angles), jnp.sin(angles))

def apply_rotary(values, cosine_lookup, sine_lookup):
    half_width = values.shape[-1] // 2
    leading = values[..., :half_width]
    trailing = values[..., half_width:]
    cos_wide = cosine_lookup[:, None, :]
    sin_wide = sine_lookup[:, None, :]
    return jnp.concatenate([leading * cos_wide - trailing * sin_wide, trailing * cos_wide + leading * sin_wide], axis=-1)

def block_forward(inputs, prefix_one, attn_gain, w_query, key_projection, value_projection, w_out, ffn_gain, w_gate, w_up, w_down):
    length_total = inputs.shape[0]
    heads_per_group = QUERY_HEAD_COUNT // KEY_VALUE_HEADS
    score_scale = 1.0 / math.sqrt(HEAD_SIZE)
    rms_first = lax.rsqrt(lax.optimization_barrier(jnp.mean(inputs * inputs, axis=-1, keepdims=True)) + EPSILON)
    normalized_rows = lower_triangle(inputs * rms_first * attn_gain)
    query_unrotated = lower_triangle_back(matrix_product(normalized_rows, w_query))
    key_unrotated = lower_triangle_back(matrix_product(normalized_rows, key_projection))
    value_matrix = lower_triangle(lower_triangle_back(matrix_product(normalized_rows, value_projection))).reshape(length_total, KEY_VALUE_HEADS, HEAD_SIZE)
    cosine_lookup, sine_lookup = tables(length_total)
    query_matrix = lower_triangle(apply_rotary(query_unrotated.reshape(length_total, QUERY_HEAD_COUNT, HEAD_SIZE), cosine_lookup, sine_lookup)).reshape(length_total, KEY_VALUE_HEADS, heads_per_group, HEAD_SIZE)
    key_rows_turned = lower_triangle(apply_rotary(key_unrotated.reshape(length_total, KEY_VALUE_HEADS, HEAD_SIZE), cosine_lookup, sine_lookup))
    scores = lower_triangle_back(jnp.einsum('qkgd,pkd->kgqp', query_matrix, key_rows_turned, precision=lax.Precision.HIGHEST) * score_scale)
    position = jnp.arange(length_total, dtype=jnp.int32)
    allowed = (position[None, :] <= position[:, None]) | (position[None, :] < prefix_one)
    scores = jnp.where(allowed, scores, MASKED)
    row_peak = lax.optimization_barrier(jnp.max(scores, axis=-1, keepdims=True))
    weights = jnp.exp(scores - row_peak)
    probabilities = lower_triangle(weights / lax.optimization_barrier(jnp.sum(weights, axis=-1, keepdims=True)))
    attended = jnp.einsum('kgqp,pkd->qkgd', probabilities, value_matrix, precision=lax.Precision.HIGHEST).reshape(length_total, QUERY_HEAD_COUNT * HEAD_SIZE)
    attended = lower_triangle(lower_triangle_back(attended))
    branch = lower_triangle_back(matrix_product(attended, w_out.T))
    middle = inputs + branch
    rms_second = lax.rsqrt(lax.optimization_barrier(jnp.mean(middle * middle, axis=-1, keepdims=True)) + EPSILON)
    normed_mid = lower_triangle(middle * rms_second * ffn_gain)
    gating = lower_triangle_back(matrix_product(normed_mid, w_gate))
    upward = lower_triangle_back(matrix_product(normed_mid, w_up))
    hidden = lower_triangle(jax.nn.silu(gating) * upward)
    return middle + matrix_product(hidden, w_down.T)

def reference(inputs, cotangent, prefix, attn_gain, w_query, key_projection, value_projection, w_out, ffn_gain, w_gate, w_up, w_down):
    params = tuple((weight.astype(jnp.float32) for weight in (attn_gain, w_query, key_projection, value_projection, w_out, ffn_gain, w_gate, w_up, w_down)))

    def per_sequence(totals, sequence_item):
        tokens_seq, cotangent_seq, prefix_seq = sequence_item

        def forward(tokens_in, *weights_in):
            return block_forward(tokens_in, prefix_seq, *weights_in)
        result, pullback = jax.vjp(forward, tokens_seq.astype(jnp.float32), *params)
        gradients = pullback(cotangent_seq.astype(jnp.float32))
        updated = tuple((total + gradient for total, gradient in zip(totals, gradients[1:])))
        return (updated, (result.astype(jnp.bfloat16), gradients[0].astype(jnp.bfloat16)))
    zero_grads = tuple((jnp.zeros(weight.shape, jnp.float32) for weight in params))
    totals, (output, grad_input) = lax.scan(per_sequence, zero_grads, (inputs, cotangent, prefix))
    return (output, grad_input, totals[0], totals[1], totals[2], totals[3], totals[4], totals[5], totals[6], totals[7], totals[8])
```

```python
import math

import jax
import jax.numpy as jnp
from jax import lax
from jax.sharding import PartitionSpec as P

HEAD_SIZE = 64
EPSILON = 1e-05
THETA = 500000.0
MASKED = -1e30
CHUNKS = 2
F32 = jnp.float32
BF16 = jnp.bfloat16


def contract(left, right, left_dim, right_dim):
    return lax.dot_general(
        left, right, (((left_dim,), (right_dim,)), ((), ())), preferred_element_type=F32
    )


def rope_tables(row_start, row_count):
    position = (row_start + jnp.arange(row_count, dtype=jnp.int32)).astype(F32)
    exponent = jnp.arange(HEAD_SIZE // 2, dtype=jnp.int32).astype(F32) * (2.0 / HEAD_SIZE)
    angles = position[:, None] * jnp.power(THETA, -exponent)[None, :]
    return (jnp.cos(angles), jnp.sin(angles))


def apply_rotary(values, cosine_lookup, sine_lookup, direction):
    half_width = values.shape[-1] // 2
    leading = values[..., :half_width]
    trailing = values[..., half_width:]
    cos_wide = cosine_lookup[:, None, :]
    sin_wide = direction * sine_lookup[:, None, :]
    return jnp.concatenate(
        [leading * cos_wide - trailing * sin_wide, trailing * cos_wide + leading * sin_wide],
        axis=-1,
    )


def masked_scores(query_block, key_block, prefix_one, row_start):
    row_count = query_block.shape[0]
    length_total = key_block.shape[0]
    scores = jnp.einsum(
        "qkgd,pkd->kgqp", query_block, key_block, preferred_element_type=F32
    ) * (1.0 / math.sqrt(HEAD_SIZE))
    query_place = row_start + jnp.arange(row_count, dtype=jnp.int32)
    key_place = jnp.arange(length_total, dtype=jnp.int32)
    allowed = (key_place[None, :] <= query_place[:, None]) | (key_place[None, :] < prefix_one)
    return jnp.where(allowed, scores, MASKED)


def attend(query_block, key_block, value_block, prefix_one, row_start):
    scores = masked_scores(query_block, key_block, prefix_one, row_start)
    row_peak = jnp.max(scores, axis=-1, keepdims=True)
    weights = jnp.exp(scores - row_peak)
    row_total = jnp.sum(weights, axis=-1, keepdims=True)
    probabilities = (weights / row_total).astype(BF16)
    attended = jnp.einsum(
        "kgqp,pkd->qkgd", probabilities, value_block, preferred_element_type=F32
    )
    return (attended.astype(BF16), row_peak + jnp.log(row_total))


def attend_back(query_block, key_block, value_block, grad_block, log_total, prefix_one, row_start):
    scores = masked_scores(query_block, key_block, prefix_one, row_start)
    probabilities = jnp.exp(scores - log_total)
    rounded = probabilities.astype(BF16)
    grad_probs = jnp.einsum(
        "qkgd,pkd->kgqp", grad_block, value_block, preferred_element_type=F32
    )
    delta_rows = jnp.sum(probabilities * grad_probs, axis=-1, keepdims=True)
    grad_scores = (probabilities * (grad_probs - delta_rows)).astype(BF16)
    score_scale = 1.0 / math.sqrt(HEAD_SIZE)
    grad_queries = (
        jnp.einsum("kgqp,pkd->qkgd", grad_scores, key_block, preferred_element_type=F32)
        * score_scale
    )
    grad_keys = (
        jnp.einsum("kgqp,qkgd->pkd", grad_scores, query_block, preferred_element_type=F32)
        * score_scale
    )
    grad_values = jnp.einsum(
        "kgqp,qkgd->pkd", rounded, grad_block, preferred_element_type=F32
    )
    return (grad_queries, grad_keys, grad_values)


def make_local(ctx_size):
    swap_x = [(0, 1), (1, 0)]
    swap_z = [(i, i ^ 1) for i in range(ctx_size)]

    def swap_rows(array):
        return lax.ppermute(array, "fsdp", swap_x)

    def local(
        inputs, cotangent, prefix, attn_gain, w_query, key_projection, value_projection, w_out,
        ffn_gain, w_gate, w_up, w_down,
    ):
        side = lax.axis_index("fsdp")
        place = lax.axis_index("ctx")
        part = (place ^ (place >> 1)) & 1
        row_count, model_width = inputs.shape[1:]
        half_width = model_width // 2
        query_width = w_query.shape[1]
        key_width = key_projection.shape[1]
        ffn_width = w_gate.shape[1]
        ffn_half = ffn_width // 2
        chunk = ffn_half // CHUNKS
        query_heads = query_width // HEAD_SIZE
        kv_heads = key_width // HEAD_SIZE
        heads_per_group = query_heads // kv_heads
        row_start = place * row_count
        pair_start = (place // 2) * 2 * row_count

        def own_first(rows):
            a = lax.dynamic_slice_in_dim(rows, side * half_width, half_width, 1)
            b = lax.dynamic_slice_in_dim(rows, (1 - side) * half_width, half_width, 1)
            return jnp.concatenate([a, b], axis=1)

        gains = jnp.stack([attn_gain, ffn_gain])
        gains = jnp.concatenate([gains, swap_rows(gains)], axis=1).astype(F32)
        gain_first, gain_second = gains[0], gains[1]

        qkv_own = jnp.concatenate([w_query, key_projection, value_projection], axis=1)
        qkv_weight = jnp.concatenate([qkv_own, swap_rows(qkv_own)], axis=0)
        out_weight = jnp.concatenate([w_out, swap_rows(w_out)], axis=0)
        ffn_own = []
        for c in range(CHUNKS):
            start = part * ffn_half + c * chunk
            own = tuple(
                lax.dynamic_slice_in_dim(w, start, chunk, 1) for w in (w_gate, w_up, w_down)
            )
            ffn_own.append(own)
        ffn_weights = [
            tuple(jnp.concatenate([w, swap_rows(w)], axis=0) for w in own) for own in ffn_own
        ]

        cosine_lookup, sine_lookup = rope_tables(row_start, row_count)
        residual_low = own_first(inputs[0])
        cot_low = own_first(cotangent[0])
        cot_all = lax.all_gather(cot_low, "ctx", axis=0, tiled=True)
        residual = residual_low.astype(F32)
        rms_first = lax.rsqrt(jnp.mean(residual * residual, axis=-1, keepdims=True) + EPSILON)
        normalized_rows = (residual * rms_first * gain_first).astype(BF16)
        qkv = jnp.dot(normalized_rows, qkv_weight, preferred_element_type=F32)
        query_rot = apply_rotary(
            qkv[:, :query_width].reshape(row_count, query_heads, HEAD_SIZE),
            cosine_lookup, sine_lookup, 1.0,
        ).astype(BF16)
        key_rot = apply_rotary(
            qkv[:, query_width : query_width + key_width].reshape(row_count, kv_heads, HEAD_SIZE),
            cosine_lookup, sine_lookup, 1.0,
        ).astype(BF16).reshape(row_count, key_width)
        value_matrix = qkv[:, query_width + key_width :].astype(BF16)
        kv_whole = lax.all_gather(
            jnp.concatenate([key_rot, value_matrix], axis=1), "ctx", axis=0, tiled=True
        )
        length_total = kv_whole.shape[0]
        key_whole = kv_whole[:, :key_width].reshape(length_total, kv_heads, HEAD_SIZE)
        value_whole = kv_whole[:, key_width:].reshape(length_total, kv_heads, HEAD_SIZE)
        query_groups = query_rot.reshape(row_count, kv_heads, heads_per_group, HEAD_SIZE)
        prefix_one = prefix[0]
        attended, log_total = attend(query_groups, key_whole, value_whole, prefix_one, row_start)
        attended_flat = attended.reshape(row_count, query_width)
        attn_term = contract(attended_flat, out_weight, 1, 1)
        middle = residual + lax.psum(attn_term.astype(BF16), "tp").astype(F32)
        rms_second = lax.rsqrt(jnp.mean(middle * middle, axis=-1, keepdims=True) + EPSILON)
        normed_mid = (middle * rms_second * gain_second).astype(BF16)
        normed_all = lax.all_gather(normed_mid, "ctx", axis=0, tiled=True)

        ffn_term = 0.0
        mid_term = 0.0
        grads = []
        for c in range(CHUNKS):
            gate_w, up_w, down_w = ffn_weights[c]
            gating = jnp.dot(normed_all, gate_w, preferred_element_type=F32)
            upward = jnp.dot(normed_all, up_w, preferred_element_type=F32)
            grad_hidden = jnp.dot(cot_all, down_w, preferred_element_type=F32)
            sigmoid_gate = jax.nn.sigmoid(gating)
            hidden = (gating * sigmoid_gate * upward).astype(BF16)
            grad_gating = (
                grad_hidden * upward * sigmoid_gate * (1.0 + gating * (1.0 - sigmoid_gate))
            ).astype(BF16)
            grad_upward = (grad_hidden * gating * sigmoid_gate).astype(BF16)
            done = []
            for rows, cols in (
                (normed_all, grad_gating), (normed_all, grad_upward), (cot_all, hidden)
            ):
                far = contract(rows[:, half_width:], cols, 0, 0).astype(BF16)
                near = contract(rows[:, :half_width], cols, 0, 0)
                total = (near + swap_rows(far).astype(F32)).astype(BF16)
                done.append((total, lax.ppermute(total, "ctx", swap_z)))
            grads.append(done)

            def pair(rows):
                return lax.dynamic_slice_in_dim(rows, pair_start, 2 * row_count, 0)

            ffn_term += contract(pair(hidden), down_w, 1, 1)
            mid_term += contract(pair(grad_gating), gate_w, 1, 1) + contract(
                pair(grad_upward), up_w, 1, 1
            )

        def pair_reduce(term):
            lower = term[:row_count]
            upper = term[row_count:]
            low = (place % 2) == 0
            mine = jnp.where(low, lower, upper)
            theirs = jnp.where(low, upper, lower).astype(BF16)
            mine = mine + lax.ppermute(theirs, "ctx", swap_z).astype(F32)
            return lax.psum(mine.astype(BF16), "tp").astype(F32)

        grad_mid_norm = pair_reduce(mid_term)
        output_rows = (middle + pair_reduce(ffn_term)).astype(BF16)
        scaled_mid = grad_mid_norm * gain_second
        gain_grad_second = jnp.sum(grad_mid_norm * middle * rms_second, axis=0)
        cube_second = rms_second * rms_second * rms_second
        grad_middle = (
            cot_low.astype(F32)
            + rms_second * scaled_mid
            - middle * cube_second * jnp.mean(scaled_mid * middle, axis=-1, keepdims=True)
        )
        branch_low = grad_middle.astype(BF16)
        grad_out = contract(branch_low, attended_flat, 0, 0)
        grad_attended = jnp.dot(branch_low, out_weight, preferred_element_type=F32).astype(BF16)
        grad_attended = grad_attended.reshape(row_count, kv_heads, heads_per_group, HEAD_SIZE)
        grad_query_rot, grad_key_all, grad_value_all = attend_back(
            query_groups, key_whole, value_whole, grad_attended, log_total, prefix_one, row_start
        )
        grad_kv = jnp.concatenate(
            [
                grad_key_all.reshape(length_total, key_width),
                grad_value_all.reshape(length_total, key_width),
            ],
            axis=1,
        ).astype(BF16)
        grad_kv = lax.psum_scatter(grad_kv, "ctx", scatter_dimension=0, tiled=True).astype(F32)
        grad_query_pre = apply_rotary(
            grad_query_rot.reshape(row_count, query_heads, HEAD_SIZE),
            cosine_lookup, sine_lookup, -1.0,
        ).astype(BF16).reshape(row_count, query_width)
        grad_key_pre = apply_rotary(
            grad_kv[:, :key_width].reshape(row_count, kv_heads, HEAD_SIZE),
            cosine_lookup, sine_lookup, -1.0,
        ).astype(BF16).reshape(row_count, key_width)
        grad_value_pre = grad_kv[:, key_width:].astype(BF16)
        grad_qkv_pre = jnp.concatenate([grad_query_pre, grad_key_pre, grad_value_pre], axis=1)
        grad_qkv = contract(normalized_rows, grad_qkv_pre, 0, 0)
        grad_attn = jnp.concatenate([grad_qkv, grad_out], axis=1)
        grad_attn = grad_attn[:half_width] + swap_rows(grad_attn[half_width:].astype(BF16)).astype(
            F32
        )
        grad_attn = lax.psum(grad_attn.astype(BF16), "ctx").astype(F32)
        grad_normed = lax.psum(contract(grad_qkv_pre, qkv_weight, 1, 1).astype(BF16), "tp").astype(
            F32
        )
        scaled_first = grad_normed * gain_first
        gain_grad_first = jnp.sum(grad_normed * residual * rms_first, axis=0)
        cube_first = rms_first * rms_first * rms_first
        grad_full = (
            grad_middle
            + rms_first * scaled_first
            - residual * cube_first * jnp.mean(scaled_first * residual, axis=-1, keepdims=True)
        )
        gain_grads = jnp.stack([gain_grad_first, gain_grad_second])
        gain_grads = lax.psum(
            gain_grads[:, :half_width] + swap_rows(gain_grads[:, half_width:]), "ctx"
        )

        first_half = part == 0
        result = []
        for i in range(3):
            mine = jnp.concatenate([grads[c][i][0] for c in range(CHUNKS)], axis=1)
            other = jnp.concatenate([grads[c][i][1] for c in range(CHUNKS)], axis=1)
            result.append(
                jnp.concatenate(
                    [jnp.where(first_half, mine, other), jnp.where(first_half, other, mine)],
                    axis=1,
                ).astype(F32)
            )
        end_key = query_width + key_width
        end_value = end_key + key_width
        return (
            own_first(output_rows)[None],
            own_first(grad_full.astype(BF16))[None],
            gain_grads[0],
            grad_attn[:, :query_width],
            grad_attn[:, query_width:end_key],
            grad_attn[:, end_key:end_value],
            grad_attn[:, end_value:],
            gain_grads[1],
            result[0],
            result[1],
            result[2],
        )

    return local


def solution(mesh):
    return jax.shard_map(
        make_local(mesh.shape["ctx"]),
        mesh=mesh,
        in_specs=(
            P("fsdp", "ctx", None), P("fsdp", "ctx", None), P("fsdp"), P("fsdp"),
            P("fsdp", "tp"), P("fsdp", "tp"), P("fsdp", "tp"), P("fsdp", "tp"),
            P("fsdp"), P("fsdp", "tp"), P("fsdp", "tp"), P("fsdp", "tp"),
        ),
        out_specs=(
            P("fsdp", "ctx", None), P("fsdp", "ctx", None), P("fsdp"), P("fsdp", "tp"),
            P("fsdp", "tp"), P("fsdp", "tp"), P("fsdp", "tp"), P("fsdp"),
            P("fsdp", "tp"), P("fsdp", "tp"), P("fsdp", "tp"),
        ),
        check_vma=False,
    )
```

```python
import math

import jax
import jax.numpy as jnp
from jax import lax
from jax.experimental import pallas as pl
from jax.experimental.pallas import tpu as pltpu
from jax.sharding import PartitionSpec as P

HEAD_SIZE = 64
EPSILON = 1e-05
THETA = 500000.0
MASKED = -1e30
CHUNKS = 2
F32 = jnp.float32
BF16 = jnp.bfloat16


def contract(left, right, left_dim, right_dim):
    return lax.dot_general(
        left, right, (((left_dim,), (right_dim,)), ((), ())), preferred_element_type=F32
    )


def rope_tables(row_start, row_count):
    position = (row_start + jnp.arange(row_count, dtype=jnp.int32)).astype(F32)
    exponent = jnp.arange(HEAD_SIZE // 2, dtype=jnp.int32).astype(F32) * (2.0 / HEAD_SIZE)
    angles = position[:, None] * jnp.power(THETA, -exponent)[None, :]
    return (jnp.cos(angles), jnp.sin(angles))


def apply_rotary(values, cosine_lookup, sine_lookup, direction):
    half_width = values.shape[-1] // 2
    leading = values[..., :half_width]
    trailing = values[..., half_width:]
    cos_wide = cosine_lookup[:, None, :]
    sin_wide = direction * sine_lookup[:, None, :]
    return jnp.concatenate(
        [leading * cos_wide - trailing * sin_wide, trailing * cos_wide + leading * sin_wide],
        axis=-1,
    )


def masked_scores(query_block, key_block, prefix_one, row_start):
    row_count = query_block.shape[0]
    length_total = key_block.shape[0]
    scores = jnp.einsum(
        "qkgd,pkd->kgqp", query_block, key_block, preferred_element_type=F32
    ) * (1.0 / math.sqrt(HEAD_SIZE))
    query_place = row_start + jnp.arange(row_count, dtype=jnp.int32)
    key_place = jnp.arange(length_total, dtype=jnp.int32)
    allowed = (key_place[None, :] <= query_place[:, None]) | (key_place[None, :] < prefix_one)
    return jnp.where(allowed, scores, MASKED)


def attend(query_block, key_block, value_block, prefix_one, row_start):
    scores = masked_scores(query_block, key_block, prefix_one, row_start)
    row_peak = jnp.max(scores, axis=-1, keepdims=True)
    weights = jnp.exp(scores - row_peak)
    row_total = jnp.sum(weights, axis=-1, keepdims=True)
    probabilities = (weights / row_total).astype(BF16)
    attended = jnp.einsum(
        "kgqp,pkd->qkgd", probabilities, value_block, preferred_element_type=F32
    )
    return (attended.astype(BF16), row_peak + jnp.log(row_total))


def attend_back(query_block, key_block, value_block, grad_block, log_total, prefix_one, row_start):
    scores = masked_scores(query_block, key_block, prefix_one, row_start)
    probabilities = jnp.exp(scores - log_total)
    rounded = probabilities.astype(BF16)
    grad_probs = jnp.einsum(
        "qkgd,pkd->kgqp", grad_block, value_block, preferred_element_type=F32
    )
    delta_rows = jnp.sum(probabilities * grad_probs, axis=-1, keepdims=True)
    grad_scores = (probabilities * (grad_probs - delta_rows)).astype(BF16)
    score_scale = 1.0 / math.sqrt(HEAD_SIZE)
    grad_queries = (
        jnp.einsum("kgqp,pkd->qkgd", grad_scores, key_block, preferred_element_type=F32)
        * score_scale
    )
    grad_keys = (
        jnp.einsum("kgqp,qkgd->pkd", grad_scores, query_block, preferred_element_type=F32)
        * score_scale
    )
    grad_values = jnp.einsum(
        "kgqp,qkgd->pkd", rounded, grad_block, preferred_element_type=F32
    )
    return (grad_queries, grad_keys, grad_values)


MESH = pl.DeviceIdType.MESH
HBM_SPEC = pl.BlockSpec(memory_space=pl.ANY)
VMEM_SPEC = pl.BlockSpec(memory_space=pltpu.VMEM)
DMA = pltpu.SemaphoreType.DMA


def remote(src, dst, send, recv, peer):
    return pltpu.make_async_remote_copy(
        src_ref=src, dst_ref=dst, send_sem=send, recv_sem=recv, device_id=peer, device_id_type=MESH
    )


def rows_at(ref, start, count):
    return ref.at[pl.ds(pl.multiple_of(start, count), count)]


def guarded(condition, body):
    if condition is None:
        body()
    else:
        pl.when(condition)(body)


def tp_peers(tp_size):
    me = lax.axis_index("tp")
    core = lax.rem(me, 2)
    level = me // 2
    levels = tp_size // 2
    partner = me + 1 - 2 * core
    others = [lax.rem(level + step, levels) * 2 + core for step in range(1, levels)]
    return me, core, level, partner, others


def enter(ctx_size, tp_size, along=False, pair=False, side=False, tensor=True):
    place = lax.axis_index("ctx")
    barrier = pltpu.get_barrier_semaphore()

    def greet(peer):
        pl.semaphore_signal(barrier, inc=1, device_id=peer, device_id_type=MESH)

    count = 0
    if tensor:
        _, _, _, partner, others = tp_peers(tp_size)
        for peer in [partner] + others:
            greet({"tp": peer})
        count = count + 1 + len(others)
    if side:
        greet({"fsdp": 1 - lax.axis_index("fsdp")})
        count = count + 1
    if along:
        up = place + 1 < ctx_size
        down = place > 0

        @pl.when(up)
        def _():
            greet({"ctx": place + 1})

        @pl.when(down)
        def _():
            greet({"ctx": place - 1})

        count = count + up.astype(jnp.int32) + down.astype(jnp.int32)
    if pair:
        greet({"ctx": place + 1 - 2 * lax.rem(place, 2)})
        count = count + 1
    pl.semaphore_wait(barrier, count)


def gather_sems(ctx_size, tp_size):
    spread = 2 * ctx_size - 1
    levels = tp_size // 2
    chips = max(levels - 1, 1)
    return [
        DMA((spread + 1,)), DMA((spread,)), DMA((chips, spread)), DMA((chips, spread)),
        DMA((levels, spread)), DMA((levels, spread)), DMA((1,)),
    ]


def gather_rows(mine, all_ref, ctx_size, tp_size, sems, block=None):
    hop_send, hop_recv, chip_send, chip_recv, core_send, core_recv, own_sem = sems
    place = lax.axis_index("ctx") if ctx_size > 1 else 0
    me, core, level, partner, others = tp_peers(tp_size)
    levels = tp_size // 2
    rows = mine.shape[0]
    middle = ctx_size - 1
    offsets = [0]
    for step in range(1, ctx_size):
        offsets += [-step, step]

    def spot(offset, who):
        return rows_at(all_ref, ((place + offset) * tp_size + who) * rows, rows)

    def hop(offset, step, src):
        slot = 2 * middle + 1 if offset == 0 and step < 0 else middle + offset
        return remote(
            src, spot(offset, me), hop_send.at[slot], hop_recv.at[middle + offset - step],
            {"ctx": place + step},
        )

    def hop_arrival(offset):
        step = -1 if offset < 0 else 1
        return remote(
            spot(offset, me), spot(offset, me), hop_send.at[middle + offset],
            hop_recv.at[middle + offset], {"ctx": place + step},
        )

    def chip(offset, index, src):
        return remote(
            src, spot(offset, me), chip_send.at[index, middle + offset],
            chip_recv.at[levels - 2 - index, middle + offset], {"tp": others[index]},
        )

    def chip_arrival(offset, index):
        where = spot(offset, others[index])
        return remote(
            where, where, chip_send.at[index, middle + offset],
            chip_recv.at[index, middle + offset], {"tp": others[index]},
        )

    def to_core(offset, index, who, src):
        return remote(
            src, spot(offset, who), core_send.at[index, middle + offset],
            core_recv.at[index, middle + offset], {"tp": partner},
        )

    def valid(offset):
        if offset == 0:
            return None
        return place + offset >= 0 if offset < 0 else place + offset < ctx_size

    def onward(offset):
        if offset < 0:
            return 1, jnp.logical_and(place + offset >= 0, place + 1 < ctx_size)
        return -1, jnp.logical_and(place + offset < ctx_size, place > 0)

    def fan_out(offset, src):
        for index in range(levels - 1):
            chip(offset, index, src).start()
        to_core(offset, 0, me, src).start()

    if block is None:
        own = pltpu.make_async_copy(mine, spot(0, me), own_sem.at[0])
    else:
        own = pltpu.make_async_copy(
            block, rows_at(all_ref, place * block.shape[0], block.shape[0]), own_sem.at[0]
        )
    own.start()
    if ctx_size > 1:
        @pl.when(place + 1 < ctx_size)
        def _():
            hop(0, 1, mine).start()

        @pl.when(place > 0)
        def _():
            hop(0, -1, mine).start()

    if block is None:
        fan_out(0, mine)
    for offset in offsets[1:]:
        def arrived(offset=offset):
            hop_arrival(offset).wait_recv()
            fan_out(offset, spot(offset, me))

        guarded(valid(offset), arrived)
        step, more = onward(offset)

        @pl.when(more)
        def _(offset=offset, step=step):
            hop(offset, step, spot(offset, me)).start()

    shared = offsets if block is None else offsets[1:]
    for offset in shared:
        def relay(offset=offset):
            for index in range(levels - 1):
                chip_arrival(offset, index).wait_recv()
                to_core(offset, 1 + index, others[index], spot(offset, others[index])).start()

        guarded(valid(offset), relay)

    for offset in shared:
        def drain(offset=offset):
            for index in range(levels):
                to_core(offset, index, me, spot(offset, me)).wait()
            for index in range(levels - 1):
                chip(offset, index, spot(offset, me)).wait_send()

        guarded(valid(offset), drain)
    own.wait()
    if ctx_size > 1:
        @pl.when(place + 1 < ctx_size)
        def _():
            hop(0, 1, mine).wait_send()

        @pl.when(place > 0)
        def _():
            hop(0, -1, mine).wait_send()

        for offset in offsets[1:]:
            step, more = onward(offset)

            @pl.when(more)
            def _(offset=offset, step=step):
                hop(offset, step, spot(offset, me)).wait_send()


def reduce_gather(term, extras, finish, side_shapes, mesh_shape, identity, blocks, across):
    ctx_size, tp_size = mesh_shape
    levels = tp_size // 2
    width = term.shape[1]
    block_rows = term.shape[0] // blocks
    rows = block_rows // tp_size
    reach = ctx_size if across else 1

    def kernel(term_ref, *refs):
        extra_refs = refs[: len(extras)]
        refs = refs[len(extras) :]
        all_ref = refs[0]
        side_refs = refs[1 : 1 + len(side_shapes)]
        refs = refs[1 + len(side_shapes) :]
        from_core, stage, from_chip, mine = refs[:4]
        refs = refs[4:]
        if blocks == 2:
            pair_stage, from_pair = refs[:2]
            refs = refs[2:]
        sems = refs[:7]
        core_send, core_recv, chip_send, chip_recv, pair_sems = refs[7:]
        place = lax.axis_index("ctx")
        me, core, level, partner, others = tp_peers(tp_size)
        enter(ctx_size, tp_size, along=across, pair=blocks == 2)

        def to_core(block, lev):
            slot = block * levels + lev
            return remote(
                rows_at(term_ref, block * block_rows + (2 * lev + 1 - core) * rows, rows),
                from_core.at[slot], core_send.at[slot], core_recv.at[slot], {"tp": partner},
            )

        def to_chip(index):
            return remote(
                stage.at[index], from_chip.at[levels - 2 - index], chip_send.at[index],
                chip_recv.at[levels - 2 - index], {"tp": others[index]},
            )

        def chip_sum(block, lev):
            own = term_ref[
                pl.ds(pl.multiple_of(block * block_rows + (2 * lev + core) * rows, rows), rows), :
            ]
            return own.astype(F32) + from_core[block * levels + lev].astype(F32)

        for lev in range(levels):
            for block in range(blocks):
                to_core(block, lev).start()
        for lev in range(levels):
            for block in range(blocks):
                to_core(block, lev).wait_recv()
        for index in range(levels - 1):
            lev = lax.rem(level + 1 + index, levels)
            for block in range(blocks):
                stage[index, block * rows : (block + 1) * rows, :] = chip_sum(block, lev).astype(
                    BF16
                )
            to_chip(index).start()
        for index in range(levels - 1):
            to_chip(index).wait_recv()

        def tp_sum(block):
            total = chip_sum(block, level)
            for index in range(levels - 1):
                total += from_chip[
                    index, pl.ds(pl.multiple_of(block * rows, rows), rows), :
                ].astype(F32)
            return total

        if blocks == 2:
            low = lax.rem(place, 2)
            pair_stage[...] = tp_sum(1 - low).astype(BF16)
            swap = remote(
                pair_stage, from_pair, pair_sems.at[0], pair_sems.at[1], {"ctx": place + 1 - 2 * low}
            )
            swap.start()
            total = tp_sum(low)
            swap.wait_recv()
            total += from_pair[...].astype(F32)
        else:
            total = tp_sum(0)
        start = pl.multiple_of(me * rows, rows)
        mine[...] = finish(total, start, *extra_refs, *side_refs)
        gather_rows(mine, all_ref, reach, tp_size, sems)
        for lev in range(levels):
            for block in range(blocks):
                to_core(block, lev).wait_send()
        for index in range(levels - 1):
            to_chip(index).wait_send()
        if blocks == 2:
            swap.wait_send()

    chips = max(levels - 1, 1)
    scratch = [
        pltpu.VMEM((blocks * levels, rows, width), BF16),
        pltpu.VMEM((chips, blocks * rows, width), BF16),
        pltpu.VMEM((chips, blocks * rows, width), BF16),
        pltpu.VMEM((rows, width), BF16),
    ]
    if blocks == 2:
        scratch += [pltpu.VMEM((rows, width), BF16)] * 2
    scratch += gather_sems(reach, tp_size)
    scratch += [
        DMA((blocks * levels,)), DMA((blocks * levels,)), DMA((chips,)), DMA((chips,)), DMA((2,)),
    ]
    return pl.pallas_call(
        kernel,
        out_shape=(
            jax.ShapeDtypeStruct((reach * block_rows, width), BF16),
            *(jax.ShapeDtypeStruct(shape, F32) for shape in side_shapes),
        ),
        in_specs=[VMEM_SPEC] * (1 + len(extras)),
        out_specs=(HBM_SPEC,) + (VMEM_SPEC,) * len(side_shapes),
        scratch_shapes=scratch,
        compiler_params=pltpu.CompilerParams(
            collective_id=identity, has_side_effects=True, vmem_limit_bytes=32 << 20
        ),
    )(term, *extras)


def opening(cot_rows, weights, mesh_shape, identity):
    ctx_size, tp_size = mesh_shape
    block_rows, width = cot_rows.shape
    rows = block_rows // tp_size
    depth = weights[0].shape[0]
    columns = sum(w.shape[1] for w in weights)

    def kernel(cot_ref, *refs):
        weight_refs = refs[: len(weights)]
        all_ref, whole_ref = refs[len(weights) : len(weights) + 2]
        sems = refs[len(weights) + 2 : len(weights) + 9]
        send, recv = refs[len(weights) + 9 :]
        enter(ctx_size, tp_size, along=True, side=True)
        far = {"fsdp": 1 - lax.axis_index("fsdp")}
        swaps = []
        at = 0
        for i, ref in enumerate(weight_refs):
            wide = ref.shape[1]
            swaps.append(
                remote(
                    ref, whole_ref.at[pl.ds(depth, depth), pl.ds(at, wide)], send.at[i], recv.at[i],
                    far,
                )
            )
            swaps[-1].start()
            at += wide
        at = 0
        for ref in weight_refs:
            wide = ref.shape[1]
            whole_ref[0:depth, at : at + wide] = ref[...]
            at += wide
        mine = rows_at(cot_ref, lax.axis_index("tp") * rows, rows)
        gather_rows(mine, all_ref, ctx_size, tp_size, sems, block=cot_ref)
        for swap in swaps:
            swap.wait()

    return pl.pallas_call(
        kernel,
        out_shape=(
            jax.ShapeDtypeStruct((ctx_size * block_rows, width), BF16),
            jax.ShapeDtypeStruct((2 * depth, columns), BF16),
        ),
        in_specs=[VMEM_SPEC] * (1 + len(weights)),
        out_specs=(HBM_SPEC, VMEM_SPEC),
        scratch_shapes=gather_sems(ctx_size, tp_size)
        + [DMA((len(weights),)), DMA((len(weights),))],
        compiler_params=pltpu.CompilerParams(
            collective_id=identity, has_side_effects=True, vmem_limit_bytes=32 << 20
        ),
    )(cot_rows, *weights)


def place_halves(part, mine, other):
    pieces = len(mine)
    depth, wide = mine[0].shape
    tile = min(depth, 256)

    def kernel(part_ref, *refs):
        out_ref = refs[-1]
        step = pl.program_id(1)
        for k in range(2 * pieces):
            @pl.when(step == k)
            def _(k=k):
                out_ref[...] = refs[k][...].astype(F32)

    def target(i, step, part_ref):
        half = jnp.where(step < pieces, part_ref[0], 1 - part_ref[0])
        return i, half * pieces + lax.rem(step, pieces)

    return pl.pallas_call(
        kernel,
        grid_spec=pltpu.PrefetchScalarGridSpec(
            num_scalar_prefetch=1,
            grid=(depth // tile, 2 * pieces),
            in_specs=[pl.BlockSpec((tile, wide), lambda i, step, part_ref: (i, 0))] * (2 * pieces),
            out_specs=pl.BlockSpec((tile, wide), target),
        ),
        out_shape=jax.ShapeDtypeStruct((depth, 2 * pieces * wide), F32),
        cost_estimate=pl.CostEstimate(
            flops=0, bytes_accessed=depth * 2 * pieces * wide * 6, transcendentals=0
        ),
    )(part.reshape(1), *mine, *other)


def mean_square(rows):
    return jnp.mean(rows * rows, axis=-1, keepdims=True)


def finish_middle(total, start, resid_ref, gain_ref, middle_ref):
    rows = total.shape[0]
    middle = resid_ref[pl.ds(start, rows), :].astype(F32) + total
    middle_ref[...] = middle
    return (middle * lax.rsqrt(mean_square(middle) + EPSILON) * gain_ref[...]).astype(BF16)


def norm_back(grad, base, values, gain):
    rms = lax.rsqrt(mean_square(values) + EPSILON)
    scaled = grad * gain
    gain_grad = jnp.sum(grad * values * rms, axis=0, keepdims=True)
    cube = rms * rms * rms
    full = base + rms * scaled - values * cube * jnp.mean(scaled * values, axis=-1, keepdims=True)
    return full, gain_grad


def finish_grad_middle(total, start, middle_ref, cot_ref, gain_ref, grad_ref, gain_grad_ref):
    base = cot_ref[pl.ds(start, total.shape[0]), :].astype(F32)
    full, gain_grad = norm_back(total, base, middle_ref[...], gain_ref[...])
    grad_ref[...] = full
    gain_grad_ref[...] = gain_grad
    return full.astype(BF16)


def finish_grad_input(total, start, grad_ref, resid_ref, gain_ref, gain_grad_ref):
    values = resid_ref[pl.ds(start, total.shape[0]), :].astype(F32)
    full, gain_grad = norm_back(total, grad_ref[...], values, gain_ref[...])
    gain_grad_ref[...] = gain_grad
    return full.astype(BF16)


def finish_output(total, start, middle_ref):
    return (middle_ref[...] + total).astype(BF16)


def make_local(ctx_size, tp_size):
    mesh_shape = (ctx_size, tp_size)
    swap_x = [(0, 1), (1, 0)]
    swap_z = [(i, i ^ 1) for i in range(ctx_size)]

    def swap_rows(array):
        return lax.ppermute(array, "fsdp", swap_x)

    def local(
        inputs, cotangent, prefix, attn_gain, w_query, key_projection, value_projection, w_out,
        ffn_gain, w_gate, w_up, w_down,
    ):
        side = lax.axis_index("fsdp")
        place = lax.axis_index("ctx")
        part = (place ^ (place >> 1)) & 1
        row_count, model_width = inputs.shape[1:]
        half_width = model_width // 2
        query_width = w_query.shape[1]
        key_width = key_projection.shape[1]
        ffn_width = w_gate.shape[1]
        ffn_half = ffn_width // 2
        chunk = ffn_half // CHUNKS
        query_heads = query_width // HEAD_SIZE
        kv_heads = key_width // HEAD_SIZE
        heads_per_group = query_heads // kv_heads
        row_start = place * row_count
        pair_start = (place // 2) * 2 * row_count

        def own_first(rows):
            a = lax.dynamic_slice_in_dim(rows, side * half_width, half_width, 1)
            b = lax.dynamic_slice_in_dim(rows, (1 - side) * half_width, half_width, 1)
            return jnp.concatenate([a, b], axis=1)

        gains = jnp.stack([attn_gain, ffn_gain])
        gains = jnp.concatenate([gains, swap_rows(gains)], axis=1).astype(F32)
        gain_first, gain_second = gains[0], gains[1]

        residual_low = own_first(inputs[0])
        cot_low = own_first(cotangent[0])
        cot_all, qkv_weight = opening(
            cot_low,
            (w_query, jnp.concatenate([key_projection, value_projection], axis=1)),
            mesh_shape, 0,
        )
        w_out, w_gate, w_up, w_down, _ = lax.optimization_barrier(
            (w_out, w_gate, w_up, w_down, qkv_weight)
        )
        out_weight = jnp.concatenate([w_out, swap_rows(w_out)], axis=0)
        ffn_own = []
        for c in range(CHUNKS):
            start = part * ffn_half + c * chunk
            own = tuple(
                lax.dynamic_slice_in_dim(w, start, chunk, 1) for w in (w_gate, w_up, w_down)
            )
            ffn_own.append(own)
        ffn_weights = [
            tuple(jnp.concatenate([w, swap_rows(w)], axis=0) for w in own) for own in ffn_own
        ]

        cosine_lookup, sine_lookup = rope_tables(row_start, row_count)
        residual = residual_low.astype(F32)
        rms_first = lax.rsqrt(jnp.mean(residual * residual, axis=-1, keepdims=True) + EPSILON)
        normalized_rows = (residual * rms_first * gain_first).astype(BF16)
        qkv = jnp.dot(normalized_rows, qkv_weight, preferred_element_type=F32)
        query_rot = apply_rotary(
            qkv[:, :query_width].reshape(row_count, query_heads, HEAD_SIZE),
            cosine_lookup, sine_lookup, 1.0,
        ).astype(BF16)
        key_rot = apply_rotary(
            qkv[:, query_width : query_width + key_width].reshape(row_count, kv_heads, HEAD_SIZE),
            cosine_lookup, sine_lookup, 1.0,
        ).astype(BF16).reshape(row_count, key_width)
        value_matrix = qkv[:, query_width + key_width :].astype(BF16)
        kv_whole = lax.all_gather(
            jnp.concatenate([key_rot, value_matrix], axis=1), "ctx", axis=0, tiled=True
        )
        length_total = kv_whole.shape[0]
        key_whole = kv_whole[:, :key_width].reshape(length_total, kv_heads, HEAD_SIZE)
        value_whole = kv_whole[:, key_width:].reshape(length_total, kv_heads, HEAD_SIZE)
        query_groups = query_rot.reshape(row_count, kv_heads, heads_per_group, HEAD_SIZE)
        prefix_one = prefix[0]
        attended, log_total = attend(query_groups, key_whole, value_whole, prefix_one, row_start)
        attended_flat = attended.reshape(row_count, query_width)
        attn_term = contract(attended_flat, out_weight, 1, 1)
        slice_shape = (row_count // tp_size, model_width)
        normed_all, middle = reduce_gather(
            attn_term.astype(BF16), (residual_low, gain_second[None]), finish_middle,
            (slice_shape,), mesh_shape, 1, 1, True,
        )

        ffn_term = 0.0
        mid_term = 0.0
        grads = []
        for c in range(CHUNKS):
            gate_w, up_w, down_w = ffn_weights[c]
            gating = jnp.dot(normed_all, gate_w, preferred_element_type=F32)
            upward = jnp.dot(normed_all, up_w, preferred_element_type=F32)
            grad_hidden = jnp.dot(cot_all, down_w, preferred_element_type=F32)
            sigmoid_gate = jax.nn.sigmoid(gating)
            hidden = (gating * sigmoid_gate * upward).astype(BF16)
            grad_gating = (
                grad_hidden * upward * sigmoid_gate * (1.0 + gating * (1.0 - sigmoid_gate))
            ).astype(BF16)
            grad_upward = (grad_hidden * gating * sigmoid_gate).astype(BF16)
            done = []
            for rows, cols in (
                (normed_all, grad_gating), (normed_all, grad_upward), (cot_all, hidden)
            ):
                far = contract(rows[:, half_width:], cols, 0, 0).astype(BF16)
                near = contract(rows[:, :half_width], cols, 0, 0)
                total = (near + swap_rows(far).astype(F32)).astype(BF16)
                done.append((total, lax.ppermute(total, "ctx", swap_z)))
            grads.append(done)

            def pair(rows):
                return lax.dynamic_slice_in_dim(rows, pair_start, 2 * row_count, 0)

            ffn_term += contract(pair(hidden), down_w, 1, 1)
            mid_term += contract(pair(grad_gating), gate_w, 1, 1) + contract(
                pair(grad_upward), up_w, 1, 1
            )

        branch_low, grad_middle, gain_grad_second = reduce_gather(
            mid_term.astype(BF16), (middle, cot_low, gain_second[None]), finish_grad_middle,
            (slice_shape, (1, model_width)), mesh_shape, 2, 2, False,
        )
        (output_rows,) = reduce_gather(
            ffn_term.astype(BF16), (middle,), finish_output, (), mesh_shape, 3, 2, False
        )
        grad_out = contract(branch_low, attended_flat, 0, 0)
        grad_attended = jnp.dot(branch_low, out_weight, preferred_element_type=F32).astype(BF16)
        grad_attended = grad_attended.reshape(row_count, kv_heads, heads_per_group, HEAD_SIZE)
        grad_query_rot, grad_key_all, grad_value_all = attend_back(
            query_groups, key_whole, value_whole, grad_attended, log_total, prefix_one, row_start
        )
        grad_kv = jnp.concatenate(
            [
                grad_key_all.reshape(length_total, key_width),
                grad_value_all.reshape(length_total, key_width),
            ],
            axis=1,
        ).astype(BF16)
        grad_kv = lax.psum_scatter(grad_kv, "ctx", scatter_dimension=0, tiled=True).astype(F32)
        grad_query_pre = apply_rotary(
            grad_query_rot.reshape(row_count, query_heads, HEAD_SIZE),
            cosine_lookup, sine_lookup, -1.0,
        ).astype(BF16).reshape(row_count, query_width)
        grad_key_pre = apply_rotary(
            grad_kv[:, :key_width].reshape(row_count, kv_heads, HEAD_SIZE),
            cosine_lookup, sine_lookup, -1.0,
        ).astype(BF16).reshape(row_count, key_width)
        grad_value_pre = grad_kv[:, key_width:].astype(BF16)
        grad_qkv_pre = jnp.concatenate([grad_query_pre, grad_key_pre, grad_value_pre], axis=1)
        grad_qkv = contract(normalized_rows, grad_qkv_pre, 0, 0)
        grad_attn = jnp.concatenate([grad_qkv, grad_out], axis=1)
        grad_attn = grad_attn[:half_width] + swap_rows(grad_attn[half_width:].astype(BF16)).astype(
            F32
        )
        grad_attn = lax.psum(grad_attn.astype(BF16), "ctx").astype(F32)
        input_rows, gain_grad_first = reduce_gather(
            contract(grad_qkv_pre, qkv_weight, 1, 1).astype(BF16),
            (grad_middle, residual_low, gain_first[None]), finish_grad_input,
            ((1, model_width),), mesh_shape, 4, 1, False,
        )
        gain_grads = jnp.concatenate([gain_grad_first, gain_grad_second], axis=0)
        gain_grads = lax.psum(
            gain_grads[:, :half_width] + swap_rows(gain_grads[:, half_width:]), ("ctx", "tp")
        )

        result = [
            place_halves(part, [done[i][0] for done in grads], [done[i][1] for done in grads])
            for i in range(3)
        ]
        end_key = query_width + key_width
        end_value = end_key + key_width
        return (
            own_first(output_rows)[None],
            own_first(input_rows)[None],
            gain_grads[0],
            grad_attn[:, :query_width],
            grad_attn[:, query_width:end_key],
            grad_attn[:, end_key:end_value],
            grad_attn[:, end_value:],
            gain_grads[1],
            result[0],
            result[1],
            result[2],
        )

    return local


def solution(mesh):
    return jax.shard_map(
        make_local(mesh.shape["ctx"], mesh.shape["tp"]),
        mesh=mesh,
        in_specs=(
            P("fsdp", "ctx", None), P("fsdp", "ctx", None), P("fsdp"), P("fsdp"),
            P("fsdp", "tp"), P("fsdp", "tp"), P("fsdp", "tp"), P("fsdp", "tp"),
            P("fsdp"), P("fsdp", "tp"), P("fsdp", "tp"), P("fsdp", "tp"),
        ),
        out_specs=(
            P("fsdp", "ctx", None), P("fsdp", "ctx", None), P("fsdp"), P("fsdp", "tp"),
            P("fsdp", "tp"), P("fsdp", "tp"), P("fsdp", "tp"), P("fsdp"),
            P("fsdp", "tp"), P("fsdp", "tp"), P("fsdp", "tp"),
        ),
        check_vma=False,
    )
```

```python
import math

import jax
import jax.numpy as jnp
from jax import lax
from jax.experimental import pallas as pl
from jax.experimental.pallas import tpu as pltpu
from jax.sharding import PartitionSpec as P

HEAD_SIZE = 64
EPSILON = 1e-05
THETA = 500000.0
MASKED = -1e30
CHUNKS = 2
F32 = jnp.float32
BF16 = jnp.bfloat16


def contract(left, right, left_dim, right_dim):
    return lax.dot_general(
        left, right, (((left_dim,), (right_dim,)), ((), ())), preferred_element_type=F32
    )


def rope_tables(row_start, row_count):
    position = (row_start + jnp.arange(row_count, dtype=jnp.int32)).astype(F32)
    exponent = jnp.arange(HEAD_SIZE // 2, dtype=jnp.int32).astype(F32) * (2.0 / HEAD_SIZE)
    angles = position[:, None] * jnp.power(THETA, -exponent)[None, :]
    return (jnp.cos(angles), jnp.sin(angles))


def apply_rotary(values, cosine_lookup, sine_lookup, direction):
    half_width = values.shape[-1] // 2
    leading = values[..., :half_width]
    trailing = values[..., half_width:]
    cos_wide = cosine_lookup[:, None, :]
    sin_wide = direction * sine_lookup[:, None, :]
    return jnp.concatenate(
        [leading * cos_wide - trailing * sin_wide, trailing * cos_wide + leading * sin_wide],
        axis=-1,
    )


def masked_scores(query_block, key_block, prefix_one, row_start):
    row_count = query_block.shape[0]
    length_total = key_block.shape[0]
    scores = jnp.einsum(
        "qkgd,pkd->kgqp", query_block, key_block, preferred_element_type=F32
    ) * (1.0 / math.sqrt(HEAD_SIZE))
    query_place = row_start + jnp.arange(row_count, dtype=jnp.int32)
    key_place = jnp.arange(length_total, dtype=jnp.int32)
    allowed = (key_place[None, :] <= query_place[:, None]) | (key_place[None, :] < prefix_one)
    return jnp.where(allowed, scores, MASKED)


def attend(query_block, key_block, value_block, prefix_one, row_start):
    scores = masked_scores(query_block, key_block, prefix_one, row_start)
    row_peak = jnp.max(scores, axis=-1, keepdims=True)
    weights = jnp.exp(scores - row_peak)
    row_total = jnp.sum(weights, axis=-1, keepdims=True)
    probabilities = (weights / row_total).astype(BF16)
    attended = jnp.einsum(
        "kgqp,pkd->qkgd", probabilities, value_block, preferred_element_type=F32
    )
    return (attended.astype(BF16), row_peak + jnp.log(row_total))


def attend_back(query_block, key_block, value_block, grad_block, log_total, prefix_one, row_start):
    scores = masked_scores(query_block, key_block, prefix_one, row_start)
    probabilities = jnp.exp(scores - log_total)
    rounded = probabilities.astype(BF16)
    grad_probs = jnp.einsum(
        "qkgd,pkd->kgqp", grad_block, value_block, preferred_element_type=F32
    )
    delta_rows = jnp.sum(probabilities * grad_probs, axis=-1, keepdims=True)
    grad_scores = (probabilities * (grad_probs - delta_rows)).astype(BF16)
    score_scale = 1.0 / math.sqrt(HEAD_SIZE)
    grad_queries = (
        jnp.einsum("kgqp,pkd->qkgd", grad_scores, key_block, preferred_element_type=F32)
        * score_scale
    )
    grad_keys = (
        jnp.einsum("kgqp,qkgd->pkd", grad_scores, query_block, preferred_element_type=F32)
        * score_scale
    )
    grad_values = jnp.einsum(
        "kgqp,qkgd->pkd", rounded, grad_block, preferred_element_type=F32
    )
    return (grad_queries, grad_keys, grad_values)


MESH = pl.DeviceIdType.MESH
HBM_SPEC = pl.BlockSpec(memory_space=pl.ANY)
VMEM_SPEC = pl.BlockSpec(memory_space=pltpu.VMEM)
DMA = pltpu.SemaphoreType.DMA


def remote(src, dst, send, recv, peer):
    return pltpu.make_async_remote_copy(
        src_ref=src, dst_ref=dst, send_sem=send, recv_sem=recv, device_id=peer, device_id_type=MESH
    )


def rows_at(ref, start, count):
    return ref.at[pl.ds(pl.multiple_of(start, count), count)]


def guarded(condition, body):
    if condition is None:
        body()
    else:
        pl.when(condition)(body)


def tp_peers(tp_size):
    me = lax.axis_index("tp")
    core = lax.rem(me, 2)
    level = me // 2
    levels = tp_size // 2
    partner = me + 1 - 2 * core
    others = [lax.rem(level + step, levels) * 2 + core for step in range(1, levels)]
    return me, core, level, partner, others


def enter(ctx_size, tp_size, along=False, pair=False, side=False, tensor=True, line=False):
    place = lax.axis_index("ctx")
    barrier = pltpu.get_barrier_semaphore()

    def greet(peer):
        pl.semaphore_signal(barrier, inc=1, device_id=peer, device_id_type=MESH)

    count = 0
    if tensor:
        _, _, _, partner, others = tp_peers(tp_size)
        for peer in [partner] + others:
            greet({"tp": peer})
        count = count + 1 + len(others)
    if side:
        greet({"fsdp": 1 - lax.axis_index("fsdp")})
        count = count + 1
    if along:
        up = place + 1 < ctx_size
        down = place > 0

        @pl.when(up)
        def _():
            greet({"ctx": place + 1})

        @pl.when(down)
        def _():
            greet({"ctx": place - 1})

        count = count + up.astype(jnp.int32) + down.astype(jnp.int32)
    if pair:
        greet({"ctx": place + 1 - 2 * lax.rem(place, 2)})
        count = count + 1
    if line:
        for step in range(1, ctx_size):
            greet({"ctx": lax.rem(place + step, ctx_size)})
        count = count + ctx_size - 1
    pl.semaphore_wait(barrier, count)


def gather_sems(ctx_size, tp_size):
    spread = 2 * ctx_size - 1
    levels = tp_size // 2
    chips = max(levels - 1, 1)
    return [
        DMA((spread + 1,)), DMA((spread,)), DMA((chips, spread)), DMA((chips, spread)),
        DMA((levels, spread)), DMA((levels, spread)), DMA((1,)),
    ]


def gather_rows(mine, all_ref, ctx_size, tp_size, sems, block=None):
    hop_send, hop_recv, chip_send, chip_recv, core_send, core_recv, own_sem = sems
    place = lax.axis_index("ctx") if ctx_size > 1 else 0
    me, core, level, partner, others = tp_peers(tp_size)
    levels = tp_size // 2
    rows = mine.shape[0]
    middle = ctx_size - 1
    offsets = [0]
    for step in range(1, ctx_size):
        offsets += [-step, step]

    def spot(offset, who):
        return rows_at(all_ref, ((place + offset) * tp_size + who) * rows, rows)

    def hop(offset, step, src):
        slot = 2 * middle + 1 if offset == 0 and step < 0 else middle + offset
        return remote(
            src, spot(offset, me), hop_send.at[slot], hop_recv.at[middle + offset - step],
            {"ctx": place + step},
        )

    def hop_arrival(offset):
        step = -1 if offset < 0 else 1
        return remote(
            spot(offset, me), spot(offset, me), hop_send.at[middle + offset],
            hop_recv.at[middle + offset], {"ctx": place + step},
        )

    def chip(offset, index, src):
        return remote(
            src, spot(offset, me), chip_send.at[index, middle + offset],
            chip_recv.at[levels - 2 - index, middle + offset], {"tp": others[index]},
        )

    def chip_arrival(offset, index):
        where = spot(offset, others[index])
        return remote(
            where, where, chip_send.at[index, middle + offset],
            chip_recv.at[index, middle + offset], {"tp": others[index]},
        )

    def to_core(offset, index, who, src):
        return remote(
            src, spot(offset, who), core_send.at[index, middle + offset],
            core_recv.at[index, middle + offset], {"tp": partner},
        )

    def valid(offset):
        if offset == 0:
            return None
        return place + offset >= 0 if offset < 0 else place + offset < ctx_size

    def onward(offset):
        if offset < 0:
            return 1, jnp.logical_and(place + offset >= 0, place + 1 < ctx_size)
        return -1, jnp.logical_and(place + offset < ctx_size, place > 0)

    def fan_out(offset, src):
        for index in range(levels - 1):
            chip(offset, index, src).start()
        to_core(offset, 0, me, src).start()

    if block is None:
        own = pltpu.make_async_copy(mine, spot(0, me), own_sem.at[0])
    else:
        own = pltpu.make_async_copy(
            block, rows_at(all_ref, place * block.shape[0], block.shape[0]), own_sem.at[0]
        )
    own.start()
    if ctx_size > 1:
        @pl.when(place + 1 < ctx_size)
        def _():
            hop(0, 1, mine).start()

        @pl.when(place > 0)
        def _():
            hop(0, -1, mine).start()

    if block is None:
        fan_out(0, mine)
    for offset in offsets[1:]:
        def arrived(offset=offset):
            hop_arrival(offset).wait_recv()
            fan_out(offset, spot(offset, me))

        guarded(valid(offset), arrived)
        step, more = onward(offset)

        @pl.when(more)
        def _(offset=offset, step=step):
            hop(offset, step, spot(offset, me)).start()

    shared = offsets if block is None else offsets[1:]
    for offset in shared:
        def relay(offset=offset):
            for index in range(levels - 1):
                chip_arrival(offset, index).wait_recv()
                to_core(offset, 1 + index, others[index], spot(offset, others[index])).start()

        guarded(valid(offset), relay)

    for offset in shared:
        def drain(offset=offset):
            for index in range(levels):
                to_core(offset, index, me, spot(offset, me)).wait()
            for index in range(levels - 1):
                chip(offset, index, spot(offset, me)).wait_send()

        guarded(valid(offset), drain)
    own.wait()
    if ctx_size > 1:
        @pl.when(place + 1 < ctx_size)
        def _():
            hop(0, 1, mine).wait_send()

        @pl.when(place > 0)
        def _():
            hop(0, -1, mine).wait_send()

        for offset in offsets[1:]:
            step, more = onward(offset)

            @pl.when(more)
            def _(offset=offset, step=step):
                hop(offset, step, spot(offset, me)).wait_send()


def line_sems(ctx_size):
    spread = 2 * ctx_size - 1
    return [DMA((spread + 1,)), DMA((spread,)), DMA((1,))]


def line_gather(mine, all_ref, ctx_size, sems):
    hop_send, hop_recv, own_sem = sems
    place = lax.axis_index("ctx")
    rows = mine.shape[0]
    middle = ctx_size - 1
    offsets = [o for step in range(1, ctx_size) for o in (-step, step)]

    def spot(offset):
        return rows_at(all_ref, (place + offset) * rows, rows)

    def hop(offset, step, src):
        slot = 2 * middle + 1 if offset == 0 and step < 0 else middle + offset
        return remote(
            src, spot(offset), hop_send.at[slot], hop_recv.at[middle + offset - step],
            {"ctx": place + step},
        )

    def arrival(offset):
        step = -1 if offset < 0 else 1
        return remote(
            spot(offset), spot(offset), hop_send.at[middle + offset],
            hop_recv.at[middle + offset], {"ctx": place + step},
        )

    def valid(offset):
        return place + offset >= 0 if offset < 0 else place + offset < ctx_size

    def onward(offset):
        if offset < 0:
            return 1, jnp.logical_and(place + offset >= 0, place + 1 < ctx_size)
        return -1, jnp.logical_and(place + offset < ctx_size, place > 0)

    own = pltpu.make_async_copy(mine, spot(0), own_sem.at[0])
    ends = ((1, place + 1 < ctx_size), (-1, place > 0))

    def begin():
        for step, there in ends:
            @pl.when(there)
            def _(step=step):
                hop(0, step, mine).start()

        own.start()

    def finish():
        for offset in offsets:
            @pl.when(valid(offset))
            def _(offset=offset):
                arrival(offset).wait_recv()

            step, more = onward(offset)

            @pl.when(more)
            def _(offset=offset, step=step):
                hop(offset, step, spot(offset)).start()

        own.wait()
        for step, there in ends:
            @pl.when(there)
            def _(step=step):
                hop(0, step, mine).wait_send()

        for offset in offsets:
            step, more = onward(offset)

            @pl.when(more)
            def _(offset=offset, step=step):
                hop(offset, step, spot(offset)).wait_send()

    return begin, finish


class AttnTail:
    def __init__(self, pre_slabs, norm_all, gain_second, mesh_shape):
        self.ctx_size, self.tp_size = mesh_shape
        self.inputs = (pre_slabs, norm_all, gain_second)
        self.wide, self.rows = pre_slabs.shape[1:]
        self.half = norm_all.shape[1] // 2
        levels = self.tp_size // 2
        self.levels = levels
        self.outs = (
            jax.ShapeDtypeStruct((self.ctx_size * self.wide, self.half), BF16),
            jax.ShapeDtypeStruct((2, self.half), F32),
        )
        self.out_specs = (HBM_SPEC, VMEM_SPEC)
        chips = max(levels - 1, 1)
        self.scratch = [
            pltpu.VMEM(pre_slabs.shape, BF16),
            pltpu.VMEM((self.wide, self.half), F32),
            pltpu.VMEM((self.wide, self.half), BF16),
            pltpu.VMEM((self.wide, self.half), BF16),
            pltpu.VMEM((self.wide, self.half), BF16),
            pltpu.VMEM((4, 2, self.half), F32),
            pltpu.VMEM((levels, 2, self.half), F32),
            pltpu.VMEM((self.ctx_size, 2, self.half), F32),
            DMA((self.ctx_size,)), DMA((self.ctx_size,)),
            DMA((6,)),
            DMA((chips,)), DMA((chips,)),
            DMA((self.ctx_size,)), DMA((self.ctx_size,)),
        ] + line_sems(self.ctx_size)

    def bind(self, in_refs, out_refs, side_refs, scratch):
        pre_ref, norm_ref, gain_second_ref = in_refs
        all_ref, gains_ref = out_refs
        slabs, own_half, far_half, from_far, quarter, swaps, by_level, by_place = scratch[:8]
        all_send, all_recv, duo, lev_send, lev_recv, ctx_send, ctx_recv = scratch[8:15]
        ctx_size, levels, half, rows = self.ctx_size, self.levels, self.half, self.rows
        place = lax.axis_index("ctx")
        _, _, level, partner, others = tp_peers(self.tp_size)
        far = {"fsdp": 1 - lax.axis_index("fsdp")}
        tile = min(512, half)
        line_begin, line_finish = line_gather(quarter, all_ref, ctx_size, scratch[15:18])

        def slab(step):
            peer = lax.rem(place + step, ctx_size)
            return remote(
                pre_ref.at[peer], slabs.at[place], all_send.at[step], all_recv.at[step], {"ctx": peer}
            )

        def slab_arrival(step):
            src = lax.rem(place + ctx_size - step, ctx_size)
            return remote(
                slabs.at[src], slabs.at[src], all_send.at[step], all_recv.at[step], {"ctx": src}
            )

        grads = remote(far_half, from_far, duo.at[0], duo.at[1], far)
        gain_x = remote(swaps.at[0], swaps.at[1], duo.at[2], duo.at[3], far)
        gain_core = remote(swaps.at[2], swaps.at[3], duo.at[4], duo.at[5], {"tp": partner})

        def gain_level(index):
            return remote(
                by_level.at[level], by_level.at[level], lev_send.at[index],
                lev_recv.at[levels - 2 - index], {"tp": others[index]},
            )

        def gain_level_arrival(index):
            where = by_level.at[lax.rem(level + 1 + index, levels)]
            return remote(where, where, lev_send.at[index], lev_recv.at[index], {"tp": others[index]})

        def gain_place(step):
            peer = lax.rem(place + step, ctx_size)
            return remote(
                by_place.at[place], by_place.at[place], ctx_send.at[step], ctx_recv.at[step],
                {"ctx": peer},
            )

        def gain_place_arrival(step):
            src = lax.rem(place + ctx_size - step, ctx_size)
            where = by_place.at[src]
            return remote(where, where, ctx_send.at[step], ctx_recv.at[step], {"ctx": src})

        def product(at):
            columns = pl.ds(pl.multiple_of(at, tile), tile)
            total = jnp.dot(
                slabs[0], norm_ref[0:rows, columns], preferred_element_type=F32
            )
            for z in range(1, ctx_size):
                total += jnp.dot(
                    slabs[z], norm_ref[z * rows : (z + 1) * rows, columns],
                    preferred_element_type=F32,
                )
            return total

        def begin():
            for step in range(1, ctx_size):
                slab(step).start()
            slabs[place] = pre_ref[place]

        def middle():
            for step in range(1, ctx_size):
                slab_arrival(step).wait_recv()

            @pl.loop(0, half // tile)
            def _(i):
                far_half[:, pl.ds(pl.multiple_of(i * tile, tile), tile)] = product(
                    half + i * tile
                ).astype(BF16)

            grads.start()

            @pl.loop(0, half // tile)
            def _(i):
                own_half[:, pl.ds(pl.multiple_of(i * tile, tile), tile)] = product(i * tile)

        def end():
            gain_first = side_refs[0]
            swaps[0, 0:1, :] = gain_first[:, half:]
            swaps[0, 1:2, :] = gain_second_ref[:, half:]
            gain_x.start()
            grads.wait_recv()
            quarter[...] = (own_half[...] + from_far[...].astype(F32)).astype(BF16)
            line_begin()
            gain_x.wait_recv()
            swaps[2, 0:1, :] = gain_first[:, :half] + swaps[1, 0:1, :]
            swaps[2, 1:2, :] = gain_second_ref[:, :half] + swaps[1, 1:2, :]
            gain_core.start()
            gain_core.wait_recv()
            by_level[level] = swaps[2] + swaps[3]
            for index in range(levels - 1):
                gain_level(index).start()
            for index in range(levels - 1):
                gain_level_arrival(index).wait_recv()
            total = by_level[0]
            for lev in range(1, levels):
                total += by_level[lev]
            by_place[place] = total
            for step in range(1, ctx_size):
                gain_place(step).start()
            for step in range(1, ctx_size):
                gain_place_arrival(step).wait_recv()
            total = by_place[0]
            for z in range(1, ctx_size):
                total += by_place[z]
            gains_ref[...] = total
            line_finish()
            for step in range(1, ctx_size):
                slab(step).wait_send()
                gain_place(step).wait_send()
            for index in range(levels - 1):
                gain_level(index).wait_send()
            grads.wait_send()
            gain_x.wait_send()
            gain_core.wait_send()

        return begin, middle, end


def reduce_gather(term, extras, finish, side_shapes, mesh_shape, identity, blocks, across, aside=None):
    ctx_size, tp_size = mesh_shape
    levels = tp_size // 2
    width = term.shape[1]
    block_rows = term.shape[0] // blocks
    rows = block_rows // tp_size
    reach = ctx_size if across else 1
    beside = aside is not None
    aside_inputs = aside.inputs if beside else ()
    aside_outs = aside.outs if beside else ()
    aside_scratch = aside.scratch if beside else []

    def kernel(term_ref, *refs):
        extra_refs = refs[: len(extras)]
        refs = refs[len(extras) :]
        aside_in = refs[: len(aside_inputs)]
        refs = refs[len(aside_inputs) :]
        all_ref = refs[0]
        side_refs = refs[1 : 1 + len(side_shapes)]
        refs = refs[1 + len(side_shapes) :]
        aside_out = refs[: len(aside_outs)]
        refs = refs[len(aside_outs) :]
        from_core, stage, from_chip, mine = refs[:4]
        refs = refs[4:]
        if blocks == 2:
            pair_stage, from_pair = refs[:2]
            refs = refs[2:]
        sems = refs[:7]
        core_send, core_recv, chip_send, chip_recv, pair_sems = refs[7:12]
        place = lax.axis_index("ctx")
        me, core, level, partner, others = tp_peers(tp_size)
        enter(ctx_size, tp_size, along=across, pair=blocks == 2, side=beside, line=beside)
        if beside:
            aside_begin, aside_middle, aside_end = aside.bind(
                aside_in, aside_out, side_refs, refs[12:]
            )
            aside_begin()

        def to_core(block, lev):
            slot = block * levels + lev
            return remote(
                rows_at(term_ref, block * block_rows + (2 * lev + 1 - core) * rows, rows),
                from_core.at[slot], core_send.at[slot], core_recv.at[slot], {"tp": partner},
            )

        def to_chip(index):
            return remote(
                stage.at[index], from_chip.at[levels - 2 - index], chip_send.at[index],
                chip_recv.at[levels - 2 - index], {"tp": others[index]},
            )

        def chip_sum(block, lev):
            own = term_ref[
                pl.ds(pl.multiple_of(block * block_rows + (2 * lev + core) * rows, rows), rows), :
            ]
            return own.astype(F32) + from_core[block * levels + lev].astype(F32)

        for lev in range(levels):
            for block in range(blocks):
                to_core(block, lev).start()
        for lev in range(levels):
            for block in range(blocks):
                to_core(block, lev).wait_recv()
        for index in range(levels - 1):
            lev = lax.rem(level + 1 + index, levels)
            for block in range(blocks):
                stage[index, block * rows : (block + 1) * rows, :] = chip_sum(block, lev).astype(
                    BF16
                )
            to_chip(index).start()
        if beside:
            aside_middle()
        for index in range(levels - 1):
            to_chip(index).wait_recv()

        def tp_sum(block):
            total = chip_sum(block, level)
            for index in range(levels - 1):
                total += from_chip[
                    index, pl.ds(pl.multiple_of(block * rows, rows), rows), :
                ].astype(F32)
            return total

        if blocks == 2:
            low = lax.rem(place, 2)
            pair_stage[...] = tp_sum(1 - low).astype(BF16)
            swap = remote(
                pair_stage, from_pair, pair_sems.at[0], pair_sems.at[1], {"ctx": place + 1 - 2 * low}
            )
            swap.start()
            total = tp_sum(low)
            swap.wait_recv()
            total += from_pair[...].astype(F32)
        else:
            total = tp_sum(0)
        start = pl.multiple_of(me * rows, rows)
        mine[...] = finish(total, start, *extra_refs, *side_refs)
        gather_rows(mine, all_ref, reach, tp_size, sems)
        if beside:
            aside_end()
        for lev in range(levels):
            for block in range(blocks):
                to_core(block, lev).wait_send()
        for index in range(levels - 1):
            to_chip(index).wait_send()
        if blocks == 2:
            swap.wait_send()

    chips = max(levels - 1, 1)
    scratch = [
        pltpu.VMEM((blocks * levels, rows, width), BF16),
        pltpu.VMEM((chips, blocks * rows, width), BF16),
        pltpu.VMEM((chips, blocks * rows, width), BF16),
        pltpu.VMEM((rows, width), BF16),
    ]
    if blocks == 2:
        scratch += [pltpu.VMEM((rows, width), BF16)] * 2
    scratch += gather_sems(reach, tp_size)
    scratch += [
        DMA((blocks * levels,)), DMA((blocks * levels,)), DMA((chips,)), DMA((chips,)), DMA((2,)),
    ]
    scratch += aside_scratch
    return pl.pallas_call(
        kernel,
        out_shape=(
            jax.ShapeDtypeStruct((reach * block_rows, width), BF16),
            *(jax.ShapeDtypeStruct(shape, F32) for shape in side_shapes),
            *aside_outs,
        ),
        in_specs=[VMEM_SPEC] * (1 + len(extras) + len(aside_inputs)),
        out_specs=(HBM_SPEC,) + (VMEM_SPEC,) * len(side_shapes)
        + (aside.out_specs if beside else ()),
        scratch_shapes=scratch,
        compiler_params=pltpu.CompilerParams(
            collective_id=identity, has_side_effects=True, vmem_limit_bytes=32 << 20
        ),
    )(term, *extras, *aside_inputs)


def opening(cot_rows, groups, gains, mesh_shape, identity):
    ctx_size, tp_size = mesh_shape
    block_rows, width = cot_rows.shape
    rows = block_rows // tp_size
    weights = [w for group in groups for w in group]
    depth = weights[0].shape[0]
    places = []
    for g, group in enumerate(groups):
        at = 0
        for w in group:
            places.append((g, at, w.shape[1]))
            at += w.shape[1]
    wholes = [
        jax.ShapeDtypeStruct((2 * depth, sum(w.shape[1] for w in group)), BF16) for group in groups
    ]

    def kernel(cot_ref, *refs):
        weight_refs = refs[: len(weights)]
        gain_ref = refs[len(weights)]
        refs = refs[len(weights) + 1 :]
        all_ref, gain_far_ref = refs[:2]
        whole_refs = refs[2 : 2 + len(groups)]
        refs = refs[2 + len(groups) :]
        sems = refs[:7]
        send, recv = refs[7:]
        enter(ctx_size, tp_size, along=True, side=True)
        far = {"fsdp": 1 - lax.axis_index("fsdp")}
        last = len(weights)
        swaps = [remote(gain_ref, gain_far_ref, send.at[last], recv.at[last], far)]
        for i, (g, at, wide) in enumerate(places):
            swaps.append(
                remote(
                    weight_refs[i], whole_refs[g].at[pl.ds(depth, depth), pl.ds(at, wide)],
                    send.at[i], recv.at[i], far,
                )
            )
        for swap in swaps:
            swap.start()
        for i, (g, at, wide) in enumerate(places):
            whole_refs[g][0:depth, at : at + wide] = weight_refs[i][...]
        mine = rows_at(cot_ref, lax.axis_index("tp") * rows, rows)
        gather_rows(mine, all_ref, ctx_size, tp_size, sems, block=cot_ref)
        for swap in swaps:
            swap.wait()

    return pl.pallas_call(
        kernel,
        out_shape=(
            jax.ShapeDtypeStruct((ctx_size * block_rows, width), BF16),
            jax.ShapeDtypeStruct(gains.shape, F32),
            *wholes,
        ),
        in_specs=[VMEM_SPEC] * (2 + len(weights)),
        out_specs=(HBM_SPEC,) + (VMEM_SPEC,) * (1 + len(groups)),
        scratch_shapes=gather_sems(ctx_size, tp_size)
        + [DMA((len(weights) + 1,)), DMA((len(weights) + 1,))],
        compiler_params=pltpu.CompilerParams(
            collective_id=identity, has_side_effects=True, vmem_limit_bytes=40 << 20
        ),
    )(cot_rows, *weights, gains)


def place_halves(part, mine, other, wide):
    pieces = len(mine)
    depth = mine[0][0].shape[0]
    tile = min(depth, 512)
    parts = list(mine) + list(other)

    def kernel(part_ref, *refs):
        out_ref = refs[-1]
        step = pl.program_id(1)
        for k in range(2 * pieces):
            @pl.when(step == k)
            def _(k=k):
                out_ref[...] = refs[k][...].astype(F32)

    def target(i, step, part_ref):
        half = jnp.where(step < pieces, part_ref[0], 1 - part_ref[0])
        return i, half * pieces + lax.rem(step, pieces)

    return pl.pallas_call(
        kernel,
        grid_spec=pltpu.PrefetchScalarGridSpec(
            num_scalar_prefetch=1,
            grid=(depth // tile, 2 * pieces),
            in_specs=[
                pl.BlockSpec((tile, wide), lambda i, step, part_ref, at=at: (i, at))
                for _, at in parts
            ],
            out_specs=pl.BlockSpec((tile, wide), target),
        ),
        out_shape=jax.ShapeDtypeStruct((depth, 2 * pieces * wide), F32),
        cost_estimate=pl.CostEstimate(
            flops=0, bytes_accessed=depth * 2 * pieces * wide * 6, transcendentals=0
        ),
    )(part.reshape(1), *(array for array, _ in parts))


def mean_square(rows):
    return jnp.mean(rows * rows, axis=-1, keepdims=True)


def finish_middle(total, start, resid_ref, gain_ref, middle_ref):
    rows = total.shape[0]
    middle = resid_ref[pl.ds(start, rows), :].astype(F32) + total
    middle_ref[...] = middle
    return (middle * lax.rsqrt(mean_square(middle) + EPSILON) * gain_ref[...]).astype(BF16)


def norm_back(grad, base, values, gain):
    rms = lax.rsqrt(mean_square(values) + EPSILON)
    scaled = grad * gain
    gain_grad = jnp.sum(grad * values * rms, axis=0, keepdims=True)
    cube = rms * rms * rms
    full = base + rms * scaled - values * cube * jnp.mean(scaled * values, axis=-1, keepdims=True)
    return full, gain_grad


def finish_grad_middle(total, start, middle_ref, cot_ref, gain_ref, grad_ref, gain_grad_ref):
    base = cot_ref[pl.ds(start, total.shape[0]), :].astype(F32)
    full, gain_grad = norm_back(total, base, middle_ref[...], gain_ref[...])
    grad_ref[...] = full
    gain_grad_ref[...] = gain_grad
    return full.astype(BF16)


def finish_grad_input(total, start, grad_ref, resid_ref, gain_ref, gain_grad_ref):
    values = resid_ref[pl.ds(start, total.shape[0]), :].astype(F32)
    full, gain_grad = norm_back(total, grad_ref[...], values, gain_ref[...])
    gain_grad_ref[...] = gain_grad
    return full.astype(BF16)


def finish_output(total, start, middle_ref):
    return (middle_ref[...] + total).astype(BF16)


def make_local(ctx_size, tp_size):
    mesh_shape = (ctx_size, tp_size)
    swap_x = [(0, 1), (1, 0)]
    swap_z = [(i, i ^ 1) for i in range(ctx_size)]

    def swap_rows(array):
        return lax.ppermute(array, "fsdp", swap_x)

    def local(
        inputs, cotangent, prefix, attn_gain, w_query, key_projection, value_projection, w_out,
        ffn_gain, w_gate, w_up, w_down,
    ):
        side = lax.axis_index("fsdp")
        place = lax.axis_index("ctx")
        part = (place ^ (place >> 1)) & 1
        row_count, model_width = inputs.shape[1:]
        half_width = model_width // 2
        query_width = w_query.shape[1]
        key_width = key_projection.shape[1]
        ffn_width = w_gate.shape[1]
        ffn_half = ffn_width // 2
        chunk = ffn_half // CHUNKS
        query_heads = query_width // HEAD_SIZE
        kv_heads = key_width // HEAD_SIZE
        heads_per_group = query_heads // kv_heads
        row_start = place * row_count
        pair_start = (place // 2) * 2 * row_count

        def own_first(rows):
            a = lax.dynamic_slice_in_dim(rows, side * half_width, half_width, 1)
            b = lax.dynamic_slice_in_dim(rows, (1 - side) * half_width, half_width, 1)
            return jnp.concatenate([a, b], axis=1)

        gains = jnp.stack([attn_gain, ffn_gain]).astype(F32)
        residual_low = own_first(inputs[0])
        cot_low = own_first(cotangent[0])
        rows_all, gains_far, qkv_weight, out_weight = opening(
            jnp.concatenate([cot_low, residual_low], axis=1),
            ((w_query, jnp.concatenate([key_projection, value_projection], axis=1)), (w_out,)),
            gains, mesh_shape, 0,
        )
        cot_all = rows_all[:, :model_width]
        residual_all = rows_all[:, model_width:].astype(F32)
        gains = jnp.concatenate([gains, gains_far], axis=1)
        gain_first, gain_second = gains[0], gains[1]
        w_gate, w_up, w_down, _ = lax.optimization_barrier((w_gate, w_up, w_down, qkv_weight))
        ffn_own = []
        for c in range(CHUNKS):
            start = part * ffn_half + c * chunk
            gate_own, up_own, down_own = (
                lax.dynamic_slice_in_dim(w, start, chunk, 1) for w in (w_gate, w_up, w_down)
            )
            ffn_own.append((jnp.concatenate([gate_own, up_own], axis=1), down_own))
        ffn_far = [[swap_rows(w) for w in ffn_own[0]]]
        for c in range(1, CHUNKS):
            ffn_own[c], ffn_far[c - 1] = lax.optimization_barrier((ffn_own[c], ffn_far[c - 1]))
            ffn_far.append([swap_rows(w) for w in ffn_own[c]])

        cosine_lookup, sine_lookup = rope_tables(row_start, row_count)
        residual = residual_low.astype(F32)
        rms_first = lax.rsqrt(jnp.mean(residual * residual, axis=-1, keepdims=True) + EPSILON)
        normalized_rows = (residual * rms_first * gain_first).astype(BF16)
        qkv = jnp.dot(normalized_rows, qkv_weight, preferred_element_type=F32)
        query_rot = apply_rotary(
            qkv[:, :query_width].reshape(row_count, query_heads, HEAD_SIZE),
            cosine_lookup, sine_lookup, 1.0,
        ).astype(BF16)
        key_rot = apply_rotary(
            qkv[:, query_width : query_width + key_width].reshape(row_count, kv_heads, HEAD_SIZE),
            cosine_lookup, sine_lookup, 1.0,
        ).astype(BF16).reshape(row_count, key_width)
        value_matrix = qkv[:, query_width + key_width :].astype(BF16)
        kv_whole = lax.all_gather(
            jnp.concatenate([key_rot, value_matrix], axis=1), "ctx", axis=0, tiled=True
        )
        length_total = kv_whole.shape[0]
        key_whole = kv_whole[:, :key_width].reshape(length_total, kv_heads, HEAD_SIZE)
        value_whole = kv_whole[:, key_width:].reshape(length_total, kv_heads, HEAD_SIZE)
        query_groups = query_rot.reshape(row_count, kv_heads, heads_per_group, HEAD_SIZE)
        prefix_one = prefix[0]
        attended, log_total = attend(query_groups, key_whole, value_whole, prefix_one, row_start)
        attended_flat = attended.reshape(row_count, query_width)
        attn_term = contract(attended_flat, out_weight, 1, 1).astype(BF16)
        attn_term, ffn_far[0] = lax.optimization_barrier((attn_term, ffn_far[0]))
        slice_shape = (row_count // tp_size, model_width)
        normed_all, middle = reduce_gather(
            attn_term, (residual_low, gain_second[None]), finish_middle,
            (slice_shape,), mesh_shape, 1, 1, True,
        )

        ffn_term = 0.0
        mid_term = 0.0
        sides = []
        fars = []
        for c in range(CHUNKS):
            if c:
                ffn_far[c], fars[-1] = lax.optimization_barrier((ffn_far[c], fars[-1]))
            pair_w, down_w = (
                jnp.concatenate([w, far], axis=0) for w, far in zip(ffn_own[c], ffn_far[c])
            )
            both = jnp.dot(normed_all, pair_w, preferred_element_type=F32)
            gating, upward = both[:, :chunk], both[:, chunk:]
            grad_hidden = jnp.dot(cot_all, down_w, preferred_element_type=F32)
            sigmoid_gate = jax.nn.sigmoid(gating)
            hidden = (gating * sigmoid_gate * upward).astype(BF16)
            grad_gating = (
                grad_hidden * upward * sigmoid_gate * (1.0 + gating * (1.0 - sigmoid_gate))
            ).astype(BF16)
            grad_upward = (grad_hidden * gating * sigmoid_gate).astype(BF16)
            grad_both = jnp.concatenate([grad_gating, grad_upward], axis=1)
            sides.append(((normed_all, grad_both), (cot_all, hidden)))
            fars.append(
                [contract(rows[:, half_width:], cols, 0, 0).astype(BF16) for rows, cols in sides[c]]
            )

            def pair(rows):
                return lax.dynamic_slice_in_dim(rows, pair_start, 2 * row_count, 0)

            ffn_term += contract(pair(hidden), down_w, 1, 1)
            mid_term += contract(pair(grad_both), pair_w, 1, 1)

        mid_low, fars[-1] = lax.optimization_barrier((mid_term.astype(BF16), fars[-1]))
        received = [[swap_rows(far) for far in chunk_fars] for chunk_fars in fars]

        def summed(c):
            return [
                (contract(rows[:, :half_width], cols, 0, 0) + far.astype(F32)).astype(BF16)
                for (rows, cols), far in zip(sides[c], received[c])
            ]

        branch_low, grad_middle, gain_grad_second = reduce_gather(
            mid_low, (middle, cot_low, gain_second[None]), finish_grad_middle,
            (slice_shape, (1, model_width)), mesh_shape, 2, 2, False,
        )
        totals = [None] * CHUNKS
        branch_low, received[0] = lax.optimization_barrier((branch_low, received[0]))
        totals[0] = summed(0)
        branch_low, totals[0] = lax.optimization_barrier((branch_low, totals[0]))
        swapped = [None] * CHUNKS
        swapped[0] = [lax.ppermute(total, "ctx", swap_z) for total in totals[0]]
        grad_out = contract(branch_low, attended_flat, 0, 0)
        grad_out_far = swap_rows(grad_out[half_width:].astype(BF16))
        grad_attended = jnp.dot(branch_low, out_weight, preferred_element_type=F32).astype(BF16)
        grad_attended = grad_attended.reshape(row_count, kv_heads, heads_per_group, HEAD_SIZE)
        grad_query_rot, grad_key_all, grad_value_all = attend_back(
            query_groups, key_whole, value_whole, grad_attended, log_total, prefix_one, row_start
        )
        grad_kv = jnp.concatenate(
            [
                grad_key_all.reshape(length_total, key_width),
                grad_value_all.reshape(length_total, key_width),
            ],
            axis=1,
        ).astype(BF16)
        grad_kv = lax.psum_scatter(grad_kv, "ctx", scatter_dimension=0, tiled=True)
        ffn_low, grad_kv = lax.optimization_barrier((ffn_term.astype(BF16), grad_kv))
        grad_kv = grad_kv.astype(F32)
        (output_rows,) = reduce_gather(
            ffn_low, (middle,), finish_output, (), mesh_shape, 3, 2, False
        )
        grad_out = grad_out[:half_width] + grad_out_far.astype(F32)
        grad_out = lax.psum(grad_out.astype(BF16), "ctx").astype(F32)
        grad_query_pre = apply_rotary(
            grad_query_rot.reshape(row_count, query_heads, HEAD_SIZE),
            cosine_lookup, sine_lookup, -1.0,
        ).astype(BF16).reshape(row_count, query_width)
        grad_key_pre = apply_rotary(
            grad_kv[:, :key_width].reshape(row_count, kv_heads, HEAD_SIZE),
            cosine_lookup, sine_lookup, -1.0,
        ).astype(BF16).reshape(row_count, key_width)
        grad_value_pre = grad_kv[:, key_width:].astype(BF16)
        grad_qkv_pre = jnp.concatenate([grad_query_pre, grad_key_pre, grad_value_pre], axis=1)
        attn_width = grad_qkv_pre.shape[1]
        pre_slabs = grad_qkv_pre.T.reshape(ctx_size, attn_width // ctx_size, row_count)
        normed_term = contract(grad_qkv_pre, qkv_weight, 1, 1).astype(BF16)
        normed_term, received[1], output_rows = lax.optimization_barrier(
            (normed_term, received[1], output_rows)
        )
        totals[1] = summed(1)
        normed_term, totals[1] = lax.optimization_barrier((normed_term, totals[1]))
        swapped[1] = [lax.ppermute(total, "ctx", swap_z) for total in totals[1]]
        rms_all = lax.rsqrt(jnp.mean(residual_all * residual_all, axis=-1, keepdims=True) + EPSILON)
        norm_all = (residual_all * rms_all * gain_first).astype(BF16)
        input_rows, _, grad_attn, gain_grads = reduce_gather(
            normed_term,
            (grad_middle, residual_low, gain_first[None]), finish_grad_input,
            ((1, model_width),), mesh_shape, 4, 1, False,
            AttnTail(pre_slabs, norm_all, gain_grad_second, mesh_shape),
        )
        grad_attn = grad_attn.T.astype(F32)

        def result(which, block):
            return place_halves(
                part,
                [(totals[c][which], block) for c in range(CHUNKS)],
                [(swapped[c][which], block) for c in range(CHUNKS)],
                chunk,
            )

        end_key = query_width + key_width
        end_value = end_key + key_width
        return (
            own_first(output_rows)[None],
            own_first(input_rows)[None],
            gain_grads[0],
            grad_attn[:, :query_width],
            grad_attn[:, query_width:end_key],
            grad_attn[:, end_key:end_value],
            grad_out,
            gain_grads[1],
            result(0, 0),
            result(0, 1),
            result(1, 0),
        )

    return local


def solution(mesh):
    return jax.shard_map(
        make_local(mesh.shape["ctx"], mesh.shape["tp"]),
        mesh=mesh,
        in_specs=(
            P("fsdp", "ctx", None), P("fsdp", "ctx", None), P("fsdp"), P("fsdp"),
            P("fsdp", "tp"), P("fsdp", "tp"), P("fsdp", "tp"), P("fsdp", "tp"),
            P("fsdp"), P("fsdp", "tp"), P("fsdp", "tp"), P("fsdp", "tp"),
        ),
        out_specs=(
            P("fsdp", "ctx", None), P("fsdp", "ctx", None), P("fsdp"), P("fsdp", "tp"),
            P("fsdp", "tp"), P("fsdp", "tp"), P("fsdp", "tp"), P("fsdp"),
            P("fsdp", "tp"), P("fsdp", "tp"), P("fsdp", "tp"),
        ),
        check_vma=False,
    )
```

```python
import math

import jax
import jax.numpy as jnp
from jax import lax
from jax.experimental import pallas as pl
from jax.experimental.pallas import tpu as pltpu
from jax.sharding import PartitionSpec as P

HEAD_SIZE = 64
EPSILON = 1e-05
THETA = 500000.0
MASKED = -1e30
F32 = jnp.float32
BF16 = jnp.bfloat16


def contract(left, right, left_dim, right_dim):
    return lax.dot_general(
        left, right, (((left_dim,), (right_dim,)), ((), ())), preferred_element_type=F32
    )


def rope_tables(row_start, row_count):
    position = (row_start + jnp.arange(row_count, dtype=jnp.int32)).astype(F32)
    exponent = jnp.arange(HEAD_SIZE // 2, dtype=jnp.int32).astype(F32) * (2.0 / HEAD_SIZE)
    angles = position[:, None] * jnp.power(THETA, -exponent)[None, :]
    return (jnp.cos(angles), jnp.sin(angles))


def apply_rotary(values, cosine_lookup, sine_lookup, direction):
    half_width = values.shape[1] // 2
    leading = values[:, :half_width]
    trailing = values[:, half_width:]
    sin = direction * sine_lookup
    return jnp.concatenate(
        [leading * cosine_lookup - trailing * sin, trailing * cosine_lookup + leading * sin],
        axis=1,
    )


def allowed_pairs(bounds_ref, shape):
    key_place = lax.broadcasted_iota(jnp.int32, shape, 0)
    query_place = bounds_ref[1] + lax.broadcasted_iota(jnp.int32, shape, 1)
    return (key_place <= query_place) | (key_place < bounds_ref[0])


SCORE_SCALE = 1.0 / math.sqrt(HEAD_SIZE)
SMEM_SPEC = pl.BlockSpec(memory_space=pltpu.SMEM)


def attend(bounds, queries, keys, values_flat):
    heads, _, rows = queries.shape
    places = keys.shape[1]
    group = heads // keys.shape[0]

    def kernel(bounds_ref, query_ref, key_ref, value_ref, out_ref, log_ref):
        @pl.loop(0, heads)
        def _(h):
            k = h // group
            scores = jnp.dot(key_ref[k], query_ref[h], preferred_element_type=F32) * SCORE_SCALE
            scores = jnp.where(allowed_pairs(bounds_ref, (places, rows)), scores, MASKED)
            peak = jnp.max(scores, axis=0, keepdims=True)
            weights = jnp.exp(scores - peak)
            total = jnp.sum(weights, axis=0, keepdims=True)
            probabilities = (weights * (1.0 / total)).astype(BF16)
            out_ref[h] = jnp.dot(
                value_ref[k], probabilities, preferred_element_type=F32
            ).astype(BF16)
            log_ref[h] = peak + jnp.log(total)

    return pl.pallas_call(
        kernel,
        out_shape=(
            jax.ShapeDtypeStruct(queries.shape, BF16),
            jax.ShapeDtypeStruct((heads, 1, rows), F32),
        ),
        in_specs=[SMEM_SPEC] + [pl.BlockSpec(memory_space=pltpu.VMEM)] * 3,
        out_specs=(pl.BlockSpec(memory_space=pltpu.VMEM),) * 2,
        compiler_params=pltpu.CompilerParams(vmem_limit_bytes=24 << 20),
    )(bounds, queries, keys, values_flat)


def attend_back(bounds, queries, keys, keys_flat, values, grads, log_total):
    heads, size, rows = queries.shape
    key_heads, places, _ = keys.shape
    group = heads // key_heads

    def kernel(
        bounds_ref, query_ref, key_ref, key_flat_ref, value_ref, grad_ref, log_ref, query_grad_ref,
        both_grad_ref, totals,
    ):
        totals[...] = jnp.zeros_like(totals)

        @pl.loop(0, heads)
        def _(h):
            k = h // group
            scores = jnp.dot(key_ref[k], query_ref[h], preferred_element_type=F32) * SCORE_SCALE
            scores = jnp.where(allowed_pairs(bounds_ref, (places, rows)), scores, MASKED)
            probabilities = jnp.exp(scores - log_ref[h])
            grad_probs = jnp.dot(value_ref[k], grad_ref[h], preferred_element_type=F32)
            delta = jnp.sum(probabilities * grad_probs, axis=0, keepdims=True)
            grad_scores = (probabilities * (grad_probs - delta)).astype(BF16)
            query_grad_ref[h] = SCORE_SCALE * jnp.dot(
                key_flat_ref[k], grad_scores, preferred_element_type=F32
            )
            totals[k] += SCORE_SCALE * contract(query_ref[h], grad_scores, 1, 1)
            totals[key_heads + k] += contract(grad_ref[h], probabilities.astype(BF16), 1, 1)

        both_grad_ref[...] = totals[...].astype(BF16)

    return pl.pallas_call(
        kernel,
        out_shape=(
            jax.ShapeDtypeStruct(queries.shape, F32),
            jax.ShapeDtypeStruct((2 * key_heads, size, places), BF16),
        ),
        in_specs=[SMEM_SPEC] + [pl.BlockSpec(memory_space=pltpu.VMEM)] * 6,
        out_specs=(pl.BlockSpec(memory_space=pltpu.VMEM),) * 2,
        scratch_shapes=[pltpu.VMEM((2 * key_heads, size, places), F32)],
        compiler_params=pltpu.CompilerParams(vmem_limit_bytes=32 << 20),
    )(bounds, queries, keys, keys_flat, values, grads, log_total)


MESH = pl.DeviceIdType.MESH
HBM_SPEC = pl.BlockSpec(memory_space=pl.ANY)
VMEM_SPEC = pl.BlockSpec(memory_space=pltpu.VMEM)
DMA = pltpu.SemaphoreType.DMA


def remote(src, dst, send, recv, peer):
    return pltpu.make_async_remote_copy(
        src_ref=src, dst_ref=dst, send_sem=send, recv_sem=recv, device_id=peer, device_id_type=MESH
    )


def rows_at(ref, start, count):
    return ref.at[pl.ds(pl.multiple_of(start, count), count)]


def guarded(condition, body):
    if condition is None:
        body()
    else:
        pl.when(condition)(body)


def tp_peers(tp_size):
    me = lax.axis_index("tp")
    core = lax.rem(me, 2)
    level = me // 2
    levels = tp_size // 2
    partner = me + 1 - 2 * core
    others = [lax.rem(level + step, levels) * 2 + core for step in range(1, levels)]
    return me, core, level, partner, others


def enter(ctx_size, tp_size, along=False, pair=False, side=False, tensor=True, line=False):
    place = lax.axis_index("ctx")
    barrier = pltpu.get_barrier_semaphore()

    def greet(peer):
        pl.semaphore_signal(barrier, inc=1, device_id=peer, device_id_type=MESH)

    count = 0
    if tensor:
        _, _, _, partner, others = tp_peers(tp_size)
        for peer in [partner] + others:
            greet({"tp": peer})
        count = count + 1 + len(others)
    if side:
        greet({"fsdp": 1 - lax.axis_index("fsdp")})
        count = count + 1
    if along:
        up = place + 1 < ctx_size
        down = place > 0

        @pl.when(up)
        def _():
            greet({"ctx": place + 1})

        @pl.when(down)
        def _():
            greet({"ctx": place - 1})

        count = count + up.astype(jnp.int32) + down.astype(jnp.int32)
    if pair:
        greet({"ctx": place + 1 - 2 * lax.rem(place, 2)})
        count = count + 1
    if line:
        for step in range(1, ctx_size):
            greet({"ctx": lax.rem(place + step, ctx_size)})
        count = count + ctx_size - 1
    pl.semaphore_wait(barrier, count)


def gather_sems(ctx_size, tp_size):
    spread = 2 * ctx_size - 1
    levels = tp_size // 2
    chips = max(levels - 1, 1)
    return [
        DMA((spread + 1,)), DMA((spread,)), DMA((chips, spread)), DMA((chips, spread)),
        DMA((levels, spread)), DMA((levels, spread)), DMA((1,)),
    ]


def gather_rows(mine, all_ref, ctx_size, tp_size, sems, block=None):
    hop_send, hop_recv, chip_send, chip_recv, core_send, core_recv, own_sem = sems
    place = lax.axis_index("ctx") if ctx_size > 1 else 0
    me, core, level, partner, others = tp_peers(tp_size)
    levels = tp_size // 2
    rows = mine.shape[0]
    middle = ctx_size - 1
    offsets = [0]
    for step in range(1, ctx_size):
        offsets += [-step, step]

    def spot(offset, who):
        return rows_at(all_ref, ((place + offset) * tp_size + who) * rows, rows)

    def hop(offset, step, src):
        slot = 2 * middle + 1 if offset == 0 and step < 0 else middle + offset
        return remote(
            src, spot(offset, me), hop_send.at[slot], hop_recv.at[middle + offset - step],
            {"ctx": place + step},
        )

    def hop_arrival(offset):
        step = -1 if offset < 0 else 1
        return remote(
            spot(offset, me), spot(offset, me), hop_send.at[middle + offset],
            hop_recv.at[middle + offset], {"ctx": place + step},
        )

    def chip(offset, index, src):
        return remote(
            src, spot(offset, me), chip_send.at[index, middle + offset],
            chip_recv.at[levels - 2 - index, middle + offset], {"tp": others[index]},
        )

    def chip_arrival(offset, index):
        where = spot(offset, others[index])
        return remote(
            where, where, chip_send.at[index, middle + offset],
            chip_recv.at[index, middle + offset], {"tp": others[index]},
        )

    def to_core(offset, index, who, src):
        return remote(
            src, spot(offset, who), core_send.at[index, middle + offset],
            core_recv.at[index, middle + offset], {"tp": partner},
        )

    def valid(offset):
        if offset == 0:
            return None
        return place + offset >= 0 if offset < 0 else place + offset < ctx_size

    def onward(offset):
        if offset < 0:
            return 1, jnp.logical_and(place + offset >= 0, place + 1 < ctx_size)
        return -1, jnp.logical_and(place + offset < ctx_size, place > 0)

    def fan_out(offset, src):
        for index in range(levels - 1):
            chip(offset, index, src).start()
        to_core(offset, 0, me, src).start()

    if block is None:
        own = pltpu.make_async_copy(mine, spot(0, me), own_sem.at[0])
    else:
        own = pltpu.make_async_copy(
            block, rows_at(all_ref, place * block.shape[0], block.shape[0]), own_sem.at[0]
        )
    own.start()
    if ctx_size > 1:
        @pl.when(place + 1 < ctx_size)
        def _():
            hop(0, 1, mine).start()

        @pl.when(place > 0)
        def _():
            hop(0, -1, mine).start()

    if block is None:
        fan_out(0, mine)
    for offset in offsets[1:]:
        def arrived(offset=offset):
            hop_arrival(offset).wait_recv()
            fan_out(offset, spot(offset, me))

        guarded(valid(offset), arrived)
        step, more = onward(offset)

        @pl.when(more)
        def _(offset=offset, step=step):
            hop(offset, step, spot(offset, me)).start()

    shared = offsets if block is None else offsets[1:]
    for offset in shared:
        def relay(offset=offset):
            for index in range(levels - 1):
                chip_arrival(offset, index).wait_recv()
                to_core(offset, 1 + index, others[index], spot(offset, others[index])).start()

        guarded(valid(offset), relay)

    for offset in shared:
        def drain(offset=offset):
            for index in range(levels):
                to_core(offset, index, me, spot(offset, me)).wait()
            for index in range(levels - 1):
                chip(offset, index, spot(offset, me)).wait_send()

        guarded(valid(offset), drain)
    own.wait()
    if ctx_size > 1:
        @pl.when(place + 1 < ctx_size)
        def _():
            hop(0, 1, mine).wait_send()

        @pl.when(place > 0)
        def _():
            hop(0, -1, mine).wait_send()

        for offset in offsets[1:]:
            step, more = onward(offset)

            @pl.when(more)
            def _(offset=offset, step=step):
                hop(offset, step, spot(offset, me)).wait_send()


def line_sems(ctx_size):
    spread = 2 * ctx_size - 1
    return [DMA((spread + 1,)), DMA((spread,)), DMA((1,))]


def line_gather(mine, all_ref, ctx_size, sems):
    hop_send, hop_recv, own_sem = sems
    place = lax.axis_index("ctx")
    rows = mine.shape[0]
    middle = ctx_size - 1
    offsets = [o for step in range(1, ctx_size) for o in (-step, step)]

    def spot(offset):
        return rows_at(all_ref, (place + offset) * rows, rows)

    def hop(offset, step, src):
        slot = 2 * middle + 1 if offset == 0 and step < 0 else middle + offset
        return remote(
            src, spot(offset), hop_send.at[slot], hop_recv.at[middle + offset - step],
            {"ctx": place + step},
        )

    def arrival(offset):
        step = -1 if offset < 0 else 1
        return remote(
            spot(offset), spot(offset), hop_send.at[middle + offset],
            hop_recv.at[middle + offset], {"ctx": place + step},
        )

    def valid(offset):
        return place + offset >= 0 if offset < 0 else place + offset < ctx_size

    def onward(offset):
        if offset < 0:
            return 1, jnp.logical_and(place + offset >= 0, place + 1 < ctx_size)
        return -1, jnp.logical_and(place + offset < ctx_size, place > 0)

    own = pltpu.make_async_copy(mine, spot(0), own_sem.at[0])
    ends = ((1, place + 1 < ctx_size), (-1, place > 0))

    def begin():
        for step, there in ends:
            @pl.when(there)
            def _(step=step):
                hop(0, step, mine).start()

        own.start()

    def finish():
        for offset in offsets:
            @pl.when(valid(offset))
            def _(offset=offset):
                arrival(offset).wait_recv()

            step, more = onward(offset)

            @pl.when(more)
            def _(offset=offset, step=step):
                hop(offset, step, spot(offset)).start()

        own.wait()
        for step, there in ends:
            @pl.when(there)
            def _(step=step):
                hop(0, step, mine).wait_send()

        for offset in offsets:
            step, more = onward(offset)

            @pl.when(more)
            def _(offset=offset, step=step):
                hop(offset, step, spot(offset)).wait_send()

    return begin, finish


class KvSum:
    side = False

    def __init__(self, grad_kv, ctx_size):
        self.ctx_size = ctx_size
        self.inputs = (grad_kv,)
        self.rows = grad_kv.shape[1] // ctx_size
        self.block = (grad_kv.shape[0], self.rows)
        self.outs = (jax.ShapeDtypeStruct(self.block, F32),)
        self.out_specs = (VMEM_SPEC,)
        self.scratch = [
            pltpu.VMEM((ctx_size, *self.block), BF16), DMA((ctx_size,)), DMA((ctx_size,)),
        ]

    def bind(self, in_refs, out_refs, side_refs, scratch):
        (grad_ref,) = in_refs
        (sum_ref,) = out_refs
        slots, send, recv = scratch
        ctx_size, rows = self.ctx_size, self.rows
        place = lax.axis_index("ctx")

        def to(step):
            peer = lax.rem(place + step, ctx_size)
            return remote(
                grad_ref.at[:, pl.ds(pl.multiple_of(peer * rows, rows), rows)], slots.at[place],
                send.at[step], recv.at[step], {"ctx": peer},
            )

        def arrival(step):
            src = lax.rem(place + ctx_size - step, ctx_size)
            return remote(slots.at[src], slots.at[src], send.at[step], recv.at[step], {"ctx": src})

        def begin():
            for step in range(1, ctx_size):
                to(step).start()
            slots[place] = grad_ref[:, pl.ds(pl.multiple_of(place * rows, rows), rows)]

        def middle():
            pass

        def end():
            for step in range(1, ctx_size):
                arrival(step).wait_recv()
            total = slots[0].astype(F32)
            for z in range(1, ctx_size):
                total += slots[z].astype(F32)
            sum_ref[...] = total
            for step in range(1, ctx_size):
                to(step).wait_send()

        return begin, middle, end


class AttnTail:
    side = True

    def __init__(self, pre_slabs, norm_all, gain_second, out_rows, mesh_shape):
        self.ctx_size, self.tp_size = mesh_shape
        self.inputs = (pre_slabs, norm_all, gain_second, out_rows)
        self.wide, self.rows = pre_slabs.shape[1:]
        self.out_wide = out_rows.shape[0] // self.ctx_size
        self.half = norm_all.shape[1] // 2
        levels = self.tp_size // 2
        self.levels = levels
        self.outs = (
            jax.ShapeDtypeStruct((self.ctx_size * (self.wide + self.out_wide), self.half), BF16),
            jax.ShapeDtypeStruct((2, self.half), F32),
        )
        self.out_specs = (HBM_SPEC, VMEM_SPEC)
        chips = max(levels - 1, 1)
        self.scratch = [
            pltpu.VMEM(pre_slabs.shape, BF16),
            pltpu.VMEM((self.wide, self.half), F32),
            pltpu.VMEM((self.wide, self.half), BF16),
            pltpu.VMEM((self.wide, self.half), BF16),
            pltpu.VMEM((self.wide + self.out_wide, self.half), BF16),
            pltpu.VMEM((4, 2, self.half), F32),
            pltpu.VMEM((levels, 2, self.half), F32),
            pltpu.VMEM((self.ctx_size, 2, self.half), F32),
            DMA((self.ctx_size,)), DMA((self.ctx_size,)),
            DMA((6,)),
            DMA((chips,)), DMA((chips,)),
            DMA((self.ctx_size,)), DMA((self.ctx_size,)),
        ] + line_sems(self.ctx_size) + [
            pltpu.VMEM((self.ctx_size, self.out_wide, self.half), BF16),
            DMA((self.ctx_size,)), DMA((self.ctx_size,)),
        ]

    def bind(self, in_refs, out_refs, side_refs, scratch):
        pre_ref, norm_ref, gain_second_ref, out_ref = in_refs
        all_ref, gains_ref = out_refs
        slabs, own_half, far_half, from_far, quarter, swaps, by_level, by_place = scratch[:8]
        all_send, all_recv, duo, lev_send, lev_recv, ctx_send, ctx_recv = scratch[8:15]
        ctx_size, levels, half, rows = self.ctx_size, self.levels, self.half, self.rows
        place = lax.axis_index("ctx")
        _, _, level, partner, others = tp_peers(self.tp_size)
        far = {"fsdp": 1 - lax.axis_index("fsdp")}
        tile = min(512, half)
        line_begin, line_finish = line_gather(quarter, all_ref, ctx_size, scratch[15:18])
        out_slots, out_send, out_recv = scratch[18:21]
        wide, out_wide = self.wide, self.out_wide

        def out_slab(step):
            peer = lax.rem(place + step, ctx_size)
            return remote(
                rows_at(out_ref, peer * out_wide, out_wide), out_slots.at[place],
                out_send.at[step], out_recv.at[step], {"ctx": peer},
            )

        def out_arrival(step):
            src = lax.rem(place + ctx_size - step, ctx_size)
            where = out_slots.at[src]
            return remote(where, where, out_send.at[step], out_recv.at[step], {"ctx": src})

        def slab(step):
            peer = lax.rem(place + step, ctx_size)
            return remote(
                pre_ref.at[peer], slabs.at[place], all_send.at[step], all_recv.at[step], {"ctx": peer}
            )

        def slab_arrival(step):
            src = lax.rem(place + ctx_size - step, ctx_size)
            return remote(
                slabs.at[src], slabs.at[src], all_send.at[step], all_recv.at[step], {"ctx": src}
            )

        grads = remote(far_half, from_far, duo.at[0], duo.at[1], far)
        gain_x = remote(swaps.at[0], swaps.at[1], duo.at[2], duo.at[3], far)
        gain_core = remote(swaps.at[2], swaps.at[3], duo.at[4], duo.at[5], {"tp": partner})

        def gain_level(index):
            return remote(
                by_level.at[level], by_level.at[level], lev_send.at[index],
                lev_recv.at[levels - 2 - index], {"tp": others[index]},
            )

        def gain_level_arrival(index):
            where = by_level.at[lax.rem(level + 1 + index, levels)]
            return remote(where, where, lev_send.at[index], lev_recv.at[index], {"tp": others[index]})

        def gain_place(step):
            peer = lax.rem(place + step, ctx_size)
            return remote(
                by_place.at[place], by_place.at[place], ctx_send.at[step], ctx_recv.at[step],
                {"ctx": peer},
            )

        def gain_place_arrival(step):
            src = lax.rem(place + ctx_size - step, ctx_size)
            where = by_place.at[src]
            return remote(where, where, ctx_send.at[step], ctx_recv.at[step], {"ctx": src})

        def product(at):
            columns = pl.ds(pl.multiple_of(at, tile), tile)
            total = jnp.dot(
                slabs[0], norm_ref[0:rows, columns], preferred_element_type=F32
            )
            for z in range(1, ctx_size):
                total += jnp.dot(
                    slabs[z], norm_ref[z * rows : (z + 1) * rows, columns],
                    preferred_element_type=F32,
                )
            return total

        def begin():
            for step in range(1, ctx_size):
                slab(step).start()
            for step in range(1, ctx_size):
                out_slab(step).start()
            slabs[place] = pre_ref[place]
            out_slots[place] = out_ref[pl.ds(pl.multiple_of(place * out_wide, out_wide), out_wide), :]

        def middle():
            for step in range(1, ctx_size):
                slab_arrival(step).wait_recv()

            @pl.loop(0, half // tile)
            def _(i):
                far_half[:, pl.ds(pl.multiple_of(i * tile, tile), tile)] = product(
                    half + i * tile
                ).astype(BF16)

            grads.start()

            @pl.loop(0, half // tile)
            def _(i):
                own_half[:, pl.ds(pl.multiple_of(i * tile, tile), tile)] = product(i * tile)

        def end():
            gain_first = side_refs[0]
            swaps[0, 0:1, :] = gain_first[:, half:]
            swaps[0, 1:2, :] = gain_second_ref[:, half:]
            gain_x.start()
            for step in range(1, ctx_size):
                out_arrival(step).wait_recv()
            total = out_slots[0].astype(F32)
            for z in range(1, ctx_size):
                total += out_slots[z].astype(F32)
            quarter[wide : wide + out_wide, :] = total.astype(BF16)
            grads.wait_recv()
            quarter[0:wide, :] = (own_half[...] + from_far[...].astype(F32)).astype(BF16)
            line_begin()
            gain_x.wait_recv()
            swaps[2, 0:1, :] = gain_first[:, :half] + swaps[1, 0:1, :]
            swaps[2, 1:2, :] = gain_second_ref[:, :half] + swaps[1, 1:2, :]
            gain_core.start()
            gain_core.wait_recv()
            by_level[level] = swaps[2] + swaps[3]
            for index in range(levels - 1):
                gain_level(index).start()
            for index in range(levels - 1):
                gain_level_arrival(index).wait_recv()
            total = by_level[0]
            for lev in range(1, levels):
                total += by_level[lev]
            by_place[place] = total
            for step in range(1, ctx_size):
                gain_place(step).start()
            for step in range(1, ctx_size):
                gain_place_arrival(step).wait_recv()
            total = by_place[0]
            for z in range(1, ctx_size):
                total += by_place[z]
            gains_ref[...] = total
            line_finish()
            for step in range(1, ctx_size):
                slab(step).wait_send()
                out_slab(step).wait_send()
                gain_place(step).wait_send()
            for index in range(levels - 1):
                gain_level(index).wait_send()
            grads.wait_send()
            gain_x.wait_send()
            gain_core.wait_send()

        return begin, middle, end


def reduce_gather(term, extras, finish, side_shapes, mesh_shape, identity, blocks, across, aside=None):
    ctx_size, tp_size = mesh_shape
    levels = tp_size // 2
    width = term.shape[1]
    block_rows = term.shape[0] // blocks
    rows = block_rows // tp_size
    reach = ctx_size if across else 1
    beside = aside is not None
    aside_inputs = aside.inputs if beside else ()
    aside_outs = aside.outs if beside else ()
    aside_scratch = aside.scratch if beside else []

    def kernel(term_ref, *refs):
        extra_refs = refs[: len(extras)]
        refs = refs[len(extras) :]
        aside_in = refs[: len(aside_inputs)]
        refs = refs[len(aside_inputs) :]
        all_ref = refs[0]
        side_refs = refs[1 : 1 + len(side_shapes)]
        refs = refs[1 + len(side_shapes) :]
        aside_out = refs[: len(aside_outs)]
        refs = refs[len(aside_outs) :]
        from_core, stage, from_chip, mine = refs[:4]
        refs = refs[4:]
        if blocks == 2:
            pair_stage, from_pair = refs[:2]
            refs = refs[2:]
        sems = refs[:7]
        core_send, core_recv, chip_send, chip_recv, pair_sems = refs[7:12]
        place = lax.axis_index("ctx")
        me, core, level, partner, others = tp_peers(tp_size)
        enter(
            ctx_size, tp_size, along=across, pair=blocks == 2 and not beside,
            side=beside and aside.side, line=beside,
        )
        if beside:
            aside_begin, aside_middle, aside_end = aside.bind(
                aside_in, aside_out, side_refs, refs[12:]
            )
            aside_begin()

        def to_core(block, lev):
            slot = block * levels + lev
            return remote(
                rows_at(term_ref, block * block_rows + (2 * lev + 1 - core) * rows, rows),
                from_core.at[slot], core_send.at[slot], core_recv.at[slot], {"tp": partner},
            )

        def to_chip(index):
            return remote(
                stage.at[index], from_chip.at[levels - 2 - index], chip_send.at[index],
                chip_recv.at[levels - 2 - index], {"tp": others[index]},
            )

        def chip_sum(block, lev):
            own = term_ref[
                pl.ds(pl.multiple_of(block * block_rows + (2 * lev + core) * rows, rows), rows), :
            ]
            return own.astype(F32) + from_core[block * levels + lev].astype(F32)

        for lev in range(levels):
            for block in range(blocks):
                to_core(block, lev).start()
        for lev in range(levels):
            for block in range(blocks):
                to_core(block, lev).wait_recv()
        for index in range(levels - 1):
            lev = lax.rem(level + 1 + index, levels)
            for block in range(blocks):
                stage[index, block * rows : (block + 1) * rows, :] = chip_sum(block, lev).astype(
                    BF16
                )
            to_chip(index).start()
        if beside:
            aside_middle()
        for index in range(levels - 1):
            to_chip(index).wait_recv()

        def tp_sum(block):
            total = chip_sum(block, level)
            for index in range(levels - 1):
                total += from_chip[
                    index, pl.ds(pl.multiple_of(block * rows, rows), rows), :
                ].astype(F32)
            return total

        if blocks == 2:
            low = lax.rem(place, 2)
            pair_stage[...] = tp_sum(1 - low).astype(BF16)
            swap = remote(
                pair_stage, from_pair, pair_sems.at[0], pair_sems.at[1], {"ctx": place + 1 - 2 * low}
            )
            swap.start()
            total = tp_sum(low)
            swap.wait_recv()
            total += from_pair[...].astype(F32)
        else:
            total = tp_sum(0)
        start = pl.multiple_of(me * rows, rows)
        mine[...] = finish(total, start, *extra_refs, *side_refs)
        gather_rows(mine, all_ref, reach, tp_size, sems)
        if beside:
            aside_end()
        for lev in range(levels):
            for block in range(blocks):
                to_core(block, lev).wait_send()
        for index in range(levels - 1):
            to_chip(index).wait_send()
        if blocks == 2:
            swap.wait_send()

    chips = max(levels - 1, 1)
    scratch = [
        pltpu.VMEM((blocks * levels, rows, width), BF16),
        pltpu.VMEM((chips, blocks * rows, width), BF16),
        pltpu.VMEM((chips, blocks * rows, width), BF16),
        pltpu.VMEM((rows, width), BF16),
    ]
    if blocks == 2:
        scratch += [pltpu.VMEM((rows, width), BF16)] * 2
    scratch += gather_sems(reach, tp_size)
    scratch += [
        DMA((blocks * levels,)), DMA((blocks * levels,)), DMA((chips,)), DMA((chips,)), DMA((2,)),
    ]
    scratch += aside_scratch
    return pl.pallas_call(
        kernel,
        out_shape=(
            jax.ShapeDtypeStruct((reach * block_rows, width), BF16),
            *(jax.ShapeDtypeStruct(shape, F32) for shape in side_shapes),
            *aside_outs,
        ),
        in_specs=[VMEM_SPEC] * (1 + len(extras) + len(aside_inputs)),
        out_specs=(HBM_SPEC,) + (VMEM_SPEC,) * len(side_shapes)
        + (aside.out_specs if beside else ()),
        scratch_shapes=scratch,
        compiler_params=pltpu.CompilerParams(
            collective_id=identity, has_side_effects=True, vmem_limit_bytes=32 << 20
        ),
    )(term, *extras, *aside_inputs)


def opening(cot_rows, groups, gains, mesh_shape, identity):
    ctx_size, tp_size = mesh_shape
    block_rows, width = cot_rows.shape
    rows = block_rows // tp_size
    weights = [w for group in groups for w in group]
    depth = weights[0].shape[0]
    places = []
    for g, group in enumerate(groups):
        at = 0
        for w in group:
            places.append((g, at, w.shape[1]))
            at += w.shape[1]
    wholes = [
        jax.ShapeDtypeStruct((2 * depth, sum(w.shape[1] for w in group)), BF16) for group in groups
    ]

    def kernel(cot_ref, *refs):
        weight_refs = refs[: len(weights)]
        gain_ref = refs[len(weights)]
        refs = refs[len(weights) + 1 :]
        all_ref, gain_far_ref = refs[:2]
        whole_refs = refs[2 : 2 + len(groups)]
        refs = refs[2 + len(groups) :]
        sems = refs[:7]
        send, recv = refs[7:]
        enter(ctx_size, tp_size, along=True, side=True)
        far = {"fsdp": 1 - lax.axis_index("fsdp")}
        last = len(weights)
        swaps = [remote(gain_ref, gain_far_ref, send.at[last], recv.at[last], far)]
        for i, (g, at, wide) in enumerate(places):
            swaps.append(
                remote(
                    weight_refs[i], whole_refs[g].at[pl.ds(depth, depth), pl.ds(at, wide)],
                    send.at[i], recv.at[i], far,
                )
            )
        for swap in swaps:
            swap.start()
        for i, (g, at, wide) in enumerate(places):
            whole_refs[g][0:depth, at : at + wide] = weight_refs[i][...]
        mine = rows_at(cot_ref, lax.axis_index("tp") * rows, rows)
        gather_rows(mine, all_ref, ctx_size, tp_size, sems, block=cot_ref)
        for swap in swaps:
            swap.wait()

    return pl.pallas_call(
        kernel,
        out_shape=(
            jax.ShapeDtypeStruct((ctx_size * block_rows, width), BF16),
            jax.ShapeDtypeStruct(gains.shape, F32),
            *wholes,
        ),
        in_specs=[VMEM_SPEC] * (2 + len(weights)),
        out_specs=(HBM_SPEC,) + (VMEM_SPEC,) * (1 + len(groups)),
        scratch_shapes=gather_sems(ctx_size, tp_size)
        + [DMA((len(weights) + 1,)), DMA((len(weights) + 1,))],
        compiler_params=pltpu.CompilerParams(
            collective_id=identity, has_side_effects=True, vmem_limit_bytes=40 << 20
        ),
    )(cot_rows, *weights, gains)


def place_blocks(table, pieces, wide):
    count = len(pieces)
    depth = pieces[0][0].shape[0]
    tile = min(depth, 1024)

    def kernel(table_ref, *refs):
        out_ref = refs[-1]
        step = pl.program_id(1)
        for k in range(count):
            @pl.when(step == k)
            def _(k=k):
                out_ref[...] = refs[k][...].astype(F32)

    return pl.pallas_call(
        kernel,
        grid_spec=pltpu.PrefetchScalarGridSpec(
            num_scalar_prefetch=1,
            grid=(depth // tile, count),
            in_specs=[
                pl.BlockSpec((tile, wide), lambda i, step, table_ref, at=at: (i, at))
                for _, at in pieces
            ],
            out_specs=pl.BlockSpec((tile, wide), lambda i, step, table_ref: (i, table_ref[step])),
        ),
        out_shape=jax.ShapeDtypeStruct((depth, count * wide), F32),
        cost_estimate=pl.CostEstimate(
            flops=0, bytes_accessed=depth * count * wide * 6, transcendentals=0
        ),
    )(table, *(array for array, _ in pieces))


def mean_square(rows):
    return jnp.mean(rows * rows, axis=-1, keepdims=True)


def finish_middle(total, start, resid_ref, gain_ref, middle_ref):
    rows = total.shape[0]
    middle = resid_ref[pl.ds(start, rows), :].astype(F32) + total
    middle_ref[...] = middle
    return (middle * lax.rsqrt(mean_square(middle) + EPSILON) * gain_ref[...]).astype(BF16)


def norm_back(grad, base, values, gain):
    rms = lax.rsqrt(mean_square(values) + EPSILON)
    scaled = grad * gain
    gain_grad = jnp.sum(grad * values * rms, axis=0, keepdims=True)
    cube = rms * rms * rms
    full = base + rms * scaled - values * cube * jnp.mean(scaled * values, axis=-1, keepdims=True)
    return full, gain_grad


def finish_grad_middle(total, start, middle_ref, cot_ref, gain_ref, grad_ref, gain_grad_ref):
    base = cot_ref[pl.ds(start, total.shape[0]), :].astype(F32)
    full, gain_grad = norm_back(total, base, middle_ref[...], gain_ref[...])
    grad_ref[...] = full
    gain_grad_ref[...] = gain_grad
    return full.astype(BF16)


def finish_grad_input(total, start, grad_ref, resid_ref, gain_ref, gain_grad_ref):
    values = resid_ref[pl.ds(start, total.shape[0]), :].astype(F32)
    full, gain_grad = norm_back(total, grad_ref[...], values, gain_ref[...])
    gain_grad_ref[...] = gain_grad
    return full.astype(BF16)


def finish_output(total, start, middle_ref):
    return (middle_ref[...] + total).astype(BF16)


def make_local(ctx_size, tp_size):
    mesh_shape = (ctx_size, tp_size)
    swap_x = [(0, 1), (1, 0)]
    swap_z = [(i, i ^ 1) for i in range(ctx_size)]

    def swap_rows(array):
        return lax.ppermute(array, "fsdp", swap_x)

    def local(
        inputs, cotangent, prefix, attn_gain, w_query, key_projection, value_projection, w_out,
        ffn_gain, w_gate, w_up, w_down,
    ):
        side = lax.axis_index("fsdp")
        place = lax.axis_index("ctx")
        part = (place ^ (place >> 1)) & 1
        row_count, model_width = inputs.shape[1:]
        half_width = model_width // 2
        query_width = w_query.shape[1]
        key_width = key_projection.shape[1]
        ffn_width = w_gate.shape[1]
        unit = ffn_width // 8
        query_heads = query_width // HEAD_SIZE
        kv_heads = key_width // HEAD_SIZE
        row_start = place * row_count
        pair_start = (place // 2) * 2 * row_count

        def own_first(rows):
            a = lax.dynamic_slice_in_dim(rows, side * half_width, half_width, 1)
            b = lax.dynamic_slice_in_dim(rows, (1 - side) * half_width, half_width, 1)
            return jnp.concatenate([a, b], axis=1)

        gains = jnp.stack([attn_gain, ffn_gain]).astype(F32)
        residual_low = own_first(inputs[0])
        cot_low = own_first(cotangent[0])
        rows_all, gains_far, qkv_weight, out_weight = opening(
            jnp.concatenate([cot_low, residual_low], axis=1),
            ((w_query, jnp.concatenate([key_projection, value_projection], axis=1)), (w_out,)),
            gains, mesh_shape, 0,
        )
        cot_all = rows_all[:, :model_width]
        residual_all = rows_all[:, model_width:].astype(F32)
        gains = jnp.concatenate([gains, gains_far], axis=1)
        gain_first, gain_second = gains[0], gains[1]
        low = place & 1
        base = 2 + 3 * part
        units = [base, base + 1, base + 2, low, 1 - low]
        def own_columns(weights, at):
            return jnp.concatenate(
                [lax.dynamic_slice_in_dim(w, at * unit, unit, 1) for w in weights], axis=1
            )

        ffn_weights = (w_gate, w_up, w_down)
        ffn_weights, _ = lax.optimization_barrier((ffn_weights, qkv_weight))
        owns = [own_columns(ffn_weights, units[0])]
        ffn_weights, owns[0] = lax.optimization_barrier((ffn_weights, owns[0]))
        owns += [own_columns(ffn_weights, at) for at in units[1:]]
        others = [swap_rows(owns[0]), swap_rows(owns[1]), None, None, None]

        cosine_lookup, sine_lookup = (table.T for table in rope_tables(row_start, row_count))
        residual = residual_low.astype(F32)
        rms_first = lax.rsqrt(jnp.mean(residual * residual, axis=-1, keepdims=True) + EPSILON)
        normalized_rows = (residual * rms_first * gain_first).astype(BF16)
        qkv = contract(qkv_weight, normalized_rows, 0, 1)
        queries = apply_rotary(
            qkv[:query_width].reshape(query_heads, HEAD_SIZE, row_count),
            cosine_lookup, sine_lookup, 1.0,
        ).astype(BF16)
        key_rot = apply_rotary(
            qkv[query_width : query_width + key_width].reshape(kv_heads, HEAD_SIZE, row_count),
            cosine_lookup, sine_lookup, 1.0,
        ).astype(BF16)
        value_rows = qkv[query_width + key_width :].astype(BF16)
        kv_own = jnp.concatenate([key_rot, value_rows.reshape(kv_heads, HEAD_SIZE, row_count)], axis=0)
        kv_whole = lax.all_gather(
            kv_own.reshape(2 * key_width, row_count).T, "ctx", axis=0, tiled=True
        )
        length_total = kv_whole.shape[0]
        by_place = kv_whole.reshape(length_total, 2 * kv_heads, HEAD_SIZE).transpose(1, 0, 2)
        by_feature = kv_whole.T.reshape(2 * kv_heads, HEAD_SIZE, length_total)
        bounds = jnp.stack([prefix[0], row_start.astype(jnp.int32)])
        attended, log_total = attend(
            bounds, queries, by_place[:kv_heads], by_feature[kv_heads:]
        )
        attended_flat = attended.reshape(query_width, row_count)
        attn_term = contract(attended_flat, out_weight, 0, 1).astype(BF16)
        attn_term, owns[2], others[0] = lax.optimization_barrier((attn_term, owns[2], others[0]))
        others[2] = swap_rows(owns[2])
        slice_shape = (row_count // tp_size, model_width)
        normed_all, middle = reduce_gather(
            attn_term, (residual_low, gain_second[None]), finish_middle,
            (slice_shape,), mesh_shape, 1, 1, True,
        )

        ffn_term = 0.0
        mid_term = 0.0
        sides = []
        fars = []
        received = []

        def pair(rows):
            return lax.dynamic_slice_in_dim(rows, pair_start, 2 * row_count, 0)

        def outer(sides_of, part_of):
            return [contract(part_of(rows), cols, 0, 0) for rows, cols in sides_of]

        def summed(c):
            near = jnp.concatenate(outer(sides[c], lambda rows: rows[:, :half_width]), axis=1)
            return (near + received[c].astype(F32)).astype(BF16)

        def forward(c):
            both_w = jnp.concatenate([owns[c], others[c]], axis=0)
            pair_w, down_w = both_w[:, : 2 * unit], both_w[:, 2 * unit :]
            both = jnp.dot(normed_all, pair_w, preferred_element_type=F32)
            gating, upward = both[:, :unit], both[:, unit:]
            grad_hidden = jnp.dot(cot_all, down_w, preferred_element_type=F32)
            sigmoid_gate = jax.nn.sigmoid(gating)
            hidden = (gating * sigmoid_gate * upward).astype(BF16)
            grad_gating = (
                grad_hidden * upward * sigmoid_gate * (1.0 + gating * (1.0 - sigmoid_gate))
            ).astype(BF16)
            grad_upward = (grad_hidden * gating * sigmoid_gate).astype(BF16)
            grad_both = jnp.concatenate([grad_gating, grad_upward], axis=1)
            sides.append(((normed_all, grad_both), (cot_all, hidden)))
            far = outer(sides[c], lambda rows: rows[:, half_width:])
            fars.append(jnp.concatenate([f.astype(BF16) for f in far], axis=1))
            return pair_w, down_w, grad_both, hidden

        for c in range(4):
            if c:
                others[c], fars[-1] = lax.optimization_barrier((others[c], fars[-1]))
            if c == 1:
                owns[3], others[1] = lax.optimization_barrier((owns[3], others[1]))
                others[3] = swap_rows(owns[3])
            pair_w, down_w, grad_both, hidden = forward(c)
            ffn_term += contract(pair(hidden), down_w, 1, 1)
            mid_term += contract(pair(grad_both), pair_w, 1, 1)

        def swap_ctx(total):
            return lax.ppermute(total, "ctx", swap_z)

        others[4] = lax.ppermute(others[3], "ctx", swap_z)
        received = [swap_rows(fars[0]), swap_rows(fars[1])]
        mid_low, fars[2], fars[3] = lax.optimization_barrier(
            (mid_term.astype(BF16), fars[2], fars[3])
        )
        received.append(swap_rows(fars[2]))
        branch_low, grad_middle, gain_grad_second = reduce_gather(
            mid_low, (middle, cot_low, gain_second[None]), finish_grad_middle,
            (slice_shape, (1, model_width)), mesh_shape, 2, 2, False,
        )
        branch_low, others[4], received[0], received[1], fars[3] = lax.optimization_barrier(
            (branch_low, others[4], received[0], received[1], fars[3])
        )
        totals = [summed(0), summed(1)]
        branch_low, totals = lax.optimization_barrier((branch_low, totals))
        swapped = [swap_ctx(total) for total in totals]
        grad_out = jnp.dot(attended_flat, branch_low, preferred_element_type=F32)
        grad_out_far = swap_rows(grad_out[:, half_width:].astype(BF16))
        received.append(swap_rows(fars[3]))
        forward(4)
        grad_attended = contract(out_weight, branch_low, 0, 1).astype(BF16)
        grad_query_rot, grad_kv = attend_back(
            bounds, queries, by_place[:kv_heads], by_feature[:kv_heads], by_place[kv_heads:],
            grad_attended.reshape(query_heads, HEAD_SIZE, row_count), log_total,
        )
        grad_kv = grad_kv.reshape(2 * key_width, length_total)
        grad_kv, fars[4], received[2] = lax.optimization_barrier((grad_kv, fars[4], received[2]))
        totals.append(summed(2))
        grad_kv, totals[2] = lax.optimization_barrier((grad_kv, totals[2]))
        swapped.append(swap_ctx(totals[2]))
        received.append(swap_rows(fars[4]))
        output_rows, grad_kv = reduce_gather(
            ffn_term.astype(BF16), (middle,), finish_output, (), mesh_shape, 3, 2, False,
            KvSum(grad_kv, ctx_size),
        )
        output_rows, grad_kv, grad_out_far, received[3], swapped[0] = lax.optimization_barrier(
            (output_rows, grad_kv, grad_out_far, received[3], swapped[0])
        )
        grad_query_pre = apply_rotary(
            grad_query_rot, cosine_lookup, sine_lookup, -1.0
        ).astype(BF16).reshape(query_width, row_count)
        grad_key_pre = apply_rotary(
            grad_kv[:key_width].reshape(kv_heads, HEAD_SIZE, row_count),
            cosine_lookup, sine_lookup, -1.0,
        ).astype(BF16).reshape(key_width, row_count)
        grad_value_pre = grad_kv[key_width:].astype(BF16)
        grad_qkv_pre = jnp.concatenate([grad_query_pre, grad_key_pre, grad_value_pre], axis=0)
        attn_width = grad_qkv_pre.shape[0]
        pre_slabs = grad_qkv_pre.reshape(ctx_size, attn_width // ctx_size, row_count)
        normed_term = contract(grad_qkv_pre, qkv_weight, 0, 1).astype(BF16)
        grad_out_rows = (grad_out[:, :half_width] + grad_out_far.astype(F32)).astype(BF16)
        totals.append(summed(3))
        normed_term, totals[3] = lax.optimization_barrier((normed_term, totals[3]))
        rms_all = lax.rsqrt(jnp.mean(residual_all * residual_all, axis=-1, keepdims=True) + EPSILON)
        norm_all = (residual_all * rms_all * gain_first).astype(BF16)
        input_rows, _, grad_attn, gain_grads = reduce_gather(
            normed_term,
            (grad_middle, residual_low, gain_first[None]), finish_grad_input,
            ((1, model_width),), mesh_shape, 4, 1, False,
            AttnTail(pre_slabs, norm_all, gain_grad_second, grad_out_rows, mesh_shape),
        )
        grad_attn, received[4], swapped[1], swapped[2] = lax.optimization_barrier(
            (grad_attn, received[4], swapped[1], swapped[2])
        )
        grad_attn = grad_attn.reshape(ctx_size, -1, half_width)
        part_width = attn_width // ctx_size
        grad_out = grad_attn[:, part_width:].reshape(query_width, half_width).T.astype(F32)
        grad_attn = grad_attn[:, :part_width].reshape(attn_width, half_width).T.astype(F32)

        totals.append(summed(4))
        far_base = 2 + 3 * (1 - part)
        table = jnp.stack(units + [far_base, far_base + 1, far_base + 2])

        def result(block):
            return place_blocks(table, [(piece, block) for piece in totals + swapped], unit)

        end_key = query_width + key_width
        end_value = end_key + key_width
        return (
            own_first(output_rows)[None],
            own_first(input_rows)[None],
            gain_grads[0],
            grad_attn[:, :query_width],
            grad_attn[:, query_width:end_key],
            grad_attn[:, end_key:end_value],
            grad_out,
            gain_grads[1],
            result(0),
            result(1),
            result(2),
        )

    return local


def solution(mesh):
    return jax.shard_map(
        make_local(mesh.shape["ctx"], mesh.shape["tp"]),
        mesh=mesh,
        in_specs=(
            P("fsdp", "ctx", None), P("fsdp", "ctx", None), P("fsdp"), P("fsdp"),
            P("fsdp", "tp"), P("fsdp", "tp"), P("fsdp", "tp"), P("fsdp", "tp"),
            P("fsdp"), P("fsdp", "tp"), P("fsdp", "tp"), P("fsdp", "tp"),
        ),
        out_specs=(
            P("fsdp", "ctx", None), P("fsdp", "ctx", None), P("fsdp"), P("fsdp", "tp"),
            P("fsdp", "tp"), P("fsdp", "tp"), P("fsdp", "tp"), P("fsdp"),
            P("fsdp", "tp"), P("fsdp", "tp"), P("fsdp", "tp"),
        ),
        check_vma=False,
    )
```

```python
import math

import jax
import jax.numpy as jnp
from jax import lax
from jax.experimental import pallas as pl
from jax.experimental.pallas import tpu as pltpu
from jax.sharding import PartitionSpec as P

HEAD_SIZE = 64
EPSILON = 1e-05
THETA = 500000.0
MASKED = -1e30
F32 = jnp.float32
BF16 = jnp.bfloat16


def contract(left, right, left_dim, right_dim):
    return lax.dot_general(
        left, right, (((left_dim,), (right_dim,)), ((), ())), preferred_element_type=F32
    )


def rope_tables(row_start, row_count):
    position = (row_start + jnp.arange(row_count, dtype=jnp.int32)).astype(F32)
    exponent = jnp.arange(HEAD_SIZE // 2, dtype=jnp.int32).astype(F32) * (2.0 / HEAD_SIZE)
    angles = position[:, None] * jnp.power(THETA, -exponent)[None, :]
    return (jnp.cos(angles), jnp.sin(angles))


def apply_rotary(values, cosine_lookup, sine_lookup, direction):
    half_width = values.shape[1] // 2
    leading = values[:, :half_width]
    trailing = values[:, half_width:]
    sin = direction * sine_lookup
    return jnp.concatenate(
        [leading * cosine_lookup - trailing * sin, trailing * cosine_lookup + leading * sin],
        axis=1,
    )


def allowed_pairs(bounds_ref, shape):
    key_place = lax.broadcasted_iota(jnp.int32, shape, 0)
    query_place = bounds_ref[1] + lax.broadcasted_iota(jnp.int32, shape, 1)
    return (key_place <= query_place) | (key_place < bounds_ref[0])


SCORE_SCALE = 1.0 / math.sqrt(HEAD_SIZE)
SMEM_SPEC = pl.BlockSpec(memory_space=pltpu.SMEM)


def attend(bounds, queries, keys, values_flat):
    heads, _, rows = queries.shape
    places = keys.shape[1]
    group = heads // keys.shape[0]

    def kernel(bounds_ref, query_ref, key_ref, value_ref, out_ref, log_ref):
        @pl.loop(0, heads)
        def _(h):
            k = h // group
            scores = jnp.dot(key_ref[k], query_ref[h], preferred_element_type=F32) * SCORE_SCALE
            scores = jnp.where(allowed_pairs(bounds_ref, (places, rows)), scores, MASKED)
            peak = jnp.max(scores, axis=0, keepdims=True)
            weights = jnp.exp(scores - peak)
            total = jnp.sum(weights, axis=0, keepdims=True)
            probabilities = (weights * (1.0 / total)).astype(BF16)
            out_ref[h] = jnp.dot(
                value_ref[k], probabilities, preferred_element_type=F32
            ).astype(BF16)
            log_ref[h] = peak + jnp.log(total)

    return pl.pallas_call(
        kernel,
        out_shape=(
            jax.ShapeDtypeStruct(queries.shape, BF16),
            jax.ShapeDtypeStruct((heads, 1, rows), F32),
        ),
        in_specs=[SMEM_SPEC] + [pl.BlockSpec(memory_space=pltpu.VMEM)] * 3,
        out_specs=(pl.BlockSpec(memory_space=pltpu.VMEM),) * 2,
        compiler_params=pltpu.CompilerParams(vmem_limit_bytes=24 << 20),
    )(bounds, queries, keys, values_flat)


def attend_back(bounds, queries, keys, keys_flat, values, grads, log_total):
    heads, size, rows = queries.shape
    key_heads, places, _ = keys.shape
    group = heads // key_heads

    def kernel(
        bounds_ref, query_ref, key_ref, key_flat_ref, value_ref, grad_ref, log_ref, query_grad_ref,
        both_grad_ref, totals,
    ):
        totals[...] = jnp.zeros_like(totals)

        @pl.loop(0, heads)
        def _(h):
            k = h // group
            scores = jnp.dot(key_ref[k], query_ref[h], preferred_element_type=F32) * SCORE_SCALE
            scores = jnp.where(allowed_pairs(bounds_ref, (places, rows)), scores, MASKED)
            probabilities = jnp.exp(scores - log_ref[h])
            grad_probs = jnp.dot(value_ref[k], grad_ref[h], preferred_element_type=F32)
            delta = jnp.sum(probabilities * grad_probs, axis=0, keepdims=True)
            grad_scores = (probabilities * (grad_probs - delta)).astype(BF16)
            query_grad_ref[h] = SCORE_SCALE * jnp.dot(
                key_flat_ref[k], grad_scores, preferred_element_type=F32
            )
            totals[k] += SCORE_SCALE * contract(query_ref[h], grad_scores, 1, 1)
            totals[key_heads + k] += contract(grad_ref[h], probabilities.astype(BF16), 1, 1)

        both_grad_ref[...] = totals[...].astype(BF16)

    return pl.pallas_call(
        kernel,
        out_shape=(
            jax.ShapeDtypeStruct(queries.shape, F32),
            jax.ShapeDtypeStruct((2 * key_heads, size, places), BF16),
        ),
        in_specs=[SMEM_SPEC] + [pl.BlockSpec(memory_space=pltpu.VMEM)] * 6,
        out_specs=(pl.BlockSpec(memory_space=pltpu.VMEM),) * 2,
        scratch_shapes=[pltpu.VMEM((2 * key_heads, size, places), F32)],
        compiler_params=pltpu.CompilerParams(vmem_limit_bytes=32 << 20),
    )(bounds, queries, keys, keys_flat, values, grads, log_total)


MESH = pl.DeviceIdType.MESH
HBM_SPEC = pl.BlockSpec(memory_space=pl.ANY)
VMEM_SPEC = pl.BlockSpec(memory_space=pltpu.VMEM)
DMA = pltpu.SemaphoreType.DMA


def remote(src, dst, send, recv, peer):
    return pltpu.make_async_remote_copy(
        src_ref=src, dst_ref=dst, send_sem=send, recv_sem=recv, device_id=peer, device_id_type=MESH
    )


def rows_at(ref, start, count):
    return ref.at[pl.ds(pl.multiple_of(start, count), count)]


def guarded(condition, body):
    if condition is None:
        body()
    else:
        pl.when(condition)(body)


def tp_peers(tp_size):
    me = lax.axis_index("tp")
    core = lax.rem(me, 2)
    level = me // 2
    levels = tp_size // 2
    partner = me + 1 - 2 * core
    others = [lax.rem(level + step, levels) * 2 + core for step in range(1, levels)]
    return me, core, level, partner, others


def enter(ctx_size, tp_size, along=False, pair=False, side=False, tensor=True, line=False):
    place = lax.axis_index("ctx")
    barrier = pltpu.get_barrier_semaphore()

    def greet(peer):
        pl.semaphore_signal(barrier, inc=1, device_id=peer, device_id_type=MESH)

    count = 0
    if tensor:
        _, _, _, partner, others = tp_peers(tp_size)
        for peer in [partner] + others:
            greet({"tp": peer})
        count = count + 1 + len(others)
    if side:
        greet({"fsdp": 1 - lax.axis_index("fsdp")})
        count = count + 1
    if along:
        up = place + 1 < ctx_size
        down = place > 0

        @pl.when(up)
        def _():
            greet({"ctx": place + 1})

        @pl.when(down)
        def _():
            greet({"ctx": place - 1})

        count = count + up.astype(jnp.int32) + down.astype(jnp.int32)
    if pair:
        greet({"ctx": place + 1 - 2 * lax.rem(place, 2)})
        count = count + 1
    if line:
        for step in range(1, ctx_size):
            greet({"ctx": lax.rem(place + step, ctx_size)})
        count = count + ctx_size - 1
    pl.semaphore_wait(barrier, count)


def gather_sems(ctx_size, tp_size):
    spread = 2 * ctx_size - 1
    levels = tp_size // 2
    chips = max(levels - 1, 1)
    return [
        DMA((spread + 1,)), DMA((spread,)), DMA((chips, spread)), DMA((chips, spread)),
        DMA((levels, spread)), DMA((levels, spread)), DMA((1,)),
    ]


def gather_rows(mine, all_ref, ctx_size, tp_size, sems, block=None):
    hop_send, hop_recv, chip_send, chip_recv, core_send, core_recv, own_sem = sems
    place = lax.axis_index("ctx") if ctx_size > 1 else 0
    me, core, level, partner, others = tp_peers(tp_size)
    levels = tp_size // 2
    rows = mine.shape[0]
    middle = ctx_size - 1
    offsets = [0]
    for step in range(1, ctx_size):
        offsets += [-step, step]

    def spot(offset, who):
        return rows_at(all_ref, ((place + offset) * tp_size + who) * rows, rows)

    def hop(offset, step, src):
        slot = 2 * middle + 1 if offset == 0 and step < 0 else middle + offset
        return remote(
            src, spot(offset, me), hop_send.at[slot], hop_recv.at[middle + offset - step],
            {"ctx": place + step},
        )

    def hop_arrival(offset):
        step = -1 if offset < 0 else 1
        return remote(
            spot(offset, me), spot(offset, me), hop_send.at[middle + offset],
            hop_recv.at[middle + offset], {"ctx": place + step},
        )

    def chip(offset, index, src):
        return remote(
            src, spot(offset, me), chip_send.at[index, middle + offset],
            chip_recv.at[levels - 2 - index, middle + offset], {"tp": others[index]},
        )

    def chip_arrival(offset, index):
        where = spot(offset, others[index])
        return remote(
            where, where, chip_send.at[index, middle + offset],
            chip_recv.at[index, middle + offset], {"tp": others[index]},
        )

    def to_core(offset, index, who, src):
        return remote(
            src, spot(offset, who), core_send.at[index, middle + offset],
            core_recv.at[index, middle + offset], {"tp": partner},
        )

    def valid(offset):
        if offset == 0:
            return None
        return place + offset >= 0 if offset < 0 else place + offset < ctx_size

    def onward(offset):
        if offset < 0:
            return 1, jnp.logical_and(place + offset >= 0, place + 1 < ctx_size)
        return -1, jnp.logical_and(place + offset < ctx_size, place > 0)

    def fan_out(offset, src):
        for index in range(levels - 1):
            chip(offset, index, src).start()
        to_core(offset, 0, me, src).start()

    if block is None:
        own = pltpu.make_async_copy(mine, spot(0, me), own_sem.at[0])
    else:
        own = pltpu.make_async_copy(
            block, rows_at(all_ref, place * block.shape[0], block.shape[0]), own_sem.at[0]
        )
    own.start()
    if ctx_size > 1:
        @pl.when(place + 1 < ctx_size)
        def _():
            hop(0, 1, mine).start()

        @pl.when(place > 0)
        def _():
            hop(0, -1, mine).start()

    if block is None:
        fan_out(0, mine)
    for offset in offsets[1:]:
        def arrived(offset=offset):
            hop_arrival(offset).wait_recv()
            fan_out(offset, spot(offset, me))

        guarded(valid(offset), arrived)
        step, more = onward(offset)

        @pl.when(more)
        def _(offset=offset, step=step):
            hop(offset, step, spot(offset, me)).start()

    shared = offsets if block is None else offsets[1:]
    for offset in shared:
        def relay(offset=offset):
            for index in range(levels - 1):
                chip_arrival(offset, index).wait_recv()
                to_core(offset, 1 + index, others[index], spot(offset, others[index])).start()

        guarded(valid(offset), relay)

    for offset in shared:
        def drain(offset=offset):
            for index in range(levels):
                to_core(offset, index, me, spot(offset, me)).wait()
            for index in range(levels - 1):
                chip(offset, index, spot(offset, me)).wait_send()

        guarded(valid(offset), drain)
    own.wait()
    if ctx_size > 1:
        @pl.when(place + 1 < ctx_size)
        def _():
            hop(0, 1, mine).wait_send()

        @pl.when(place > 0)
        def _():
            hop(0, -1, mine).wait_send()

        for offset in offsets[1:]:
            step, more = onward(offset)

            @pl.when(more)
            def _(offset=offset, step=step):
                hop(offset, step, spot(offset, me)).wait_send()


def line_sems(ctx_size):
    spread = 2 * ctx_size - 1
    return [DMA((spread + 1,)), DMA((spread,)), DMA((1,))]


def line_gather(mine, all_ref, ctx_size, sems):
    hop_send, hop_recv, own_sem = sems
    place = lax.axis_index("ctx")
    rows = mine.shape[0]
    middle = ctx_size - 1
    offsets = [o for step in range(1, ctx_size) for o in (-step, step)]

    def spot(offset):
        return rows_at(all_ref, (place + offset) * rows, rows)

    def hop(offset, step, src):
        slot = 2 * middle + 1 if offset == 0 and step < 0 else middle + offset
        return remote(
            src, spot(offset), hop_send.at[slot], hop_recv.at[middle + offset - step],
            {"ctx": place + step},
        )

    def arrival(offset):
        step = -1 if offset < 0 else 1
        return remote(
            spot(offset), spot(offset), hop_send.at[middle + offset],
            hop_recv.at[middle + offset], {"ctx": place + step},
        )

    def valid(offset):
        return place + offset >= 0 if offset < 0 else place + offset < ctx_size

    def onward(offset):
        if offset < 0:
            return 1, jnp.logical_and(place + offset >= 0, place + 1 < ctx_size)
        return -1, jnp.logical_and(place + offset < ctx_size, place > 0)

    own = pltpu.make_async_copy(mine, spot(0), own_sem.at[0])
    ends = ((1, place + 1 < ctx_size), (-1, place > 0))

    def begin():
        for step, there in ends:
            @pl.when(there)
            def _(step=step):
                hop(0, step, mine).start()

        own.start()

    def finish():
        for offset in offsets:
            @pl.when(valid(offset))
            def _(offset=offset):
                arrival(offset).wait_recv()

            step, more = onward(offset)

            @pl.when(more)
            def _(offset=offset, step=step):
                hop(offset, step, spot(offset)).start()

        own.wait()
        for step, there in ends:
            @pl.when(there)
            def _(step=step):
                hop(0, step, mine).wait_send()

        for offset in offsets:
            step, more = onward(offset)

            @pl.when(more)
            def _(offset=offset, step=step):
                hop(offset, step, spot(offset)).wait_send()

    return begin, finish


class KvSum:
    side = False

    def __init__(self, grad_kv, ctx_size):
        self.ctx_size = ctx_size
        self.inputs = (grad_kv,)
        self.rows = grad_kv.shape[1] // ctx_size
        self.block = (grad_kv.shape[0], self.rows)
        self.outs = (jax.ShapeDtypeStruct(self.block, F32),)
        self.out_specs = (VMEM_SPEC,)
        self.scratch = [
            pltpu.VMEM((ctx_size, *self.block), BF16), DMA((ctx_size,)), DMA((ctx_size,)),
        ]

    def bind(self, in_refs, out_refs, side_refs, scratch):
        (grad_ref,) = in_refs
        (sum_ref,) = out_refs
        slots, send, recv = scratch
        ctx_size, rows = self.ctx_size, self.rows
        place = lax.axis_index("ctx")

        def to(step):
            peer = lax.rem(place + step, ctx_size)
            return remote(
                grad_ref.at[:, pl.ds(pl.multiple_of(peer * rows, rows), rows)], slots.at[place],
                send.at[step], recv.at[step], {"ctx": peer},
            )

        def arrival(step):
            src = lax.rem(place + ctx_size - step, ctx_size)
            return remote(slots.at[src], slots.at[src], send.at[step], recv.at[step], {"ctx": src})

        def begin():
            for step in range(1, ctx_size):
                to(step).start()
            slots[place] = grad_ref[:, pl.ds(pl.multiple_of(place * rows, rows), rows)]

        def middle():
            pass

        def end():
            for step in range(1, ctx_size):
                arrival(step).wait_recv()
            total = slots[0].astype(F32)
            for z in range(1, ctx_size):
                total += slots[z].astype(F32)
            sum_ref[...] = total
            for step in range(1, ctx_size):
                to(step).wait_send()

        return begin, middle, end


class AttnTail:
    side = True

    def __init__(self, pre_slabs, norm_all, gain_second, out_rows, mesh_shape):
        self.ctx_size, self.tp_size = mesh_shape
        self.inputs = (pre_slabs, norm_all, gain_second, out_rows)
        self.wide, self.rows = pre_slabs.shape[1:]
        self.out_wide = out_rows.shape[0] // self.ctx_size
        self.half = norm_all.shape[1] // 2
        levels = self.tp_size // 2
        self.levels = levels
        self.outs = (
            jax.ShapeDtypeStruct((self.ctx_size * (self.wide + self.out_wide), self.half), BF16),
            jax.ShapeDtypeStruct((2, self.half), F32),
        )
        self.out_specs = (HBM_SPEC, VMEM_SPEC)
        chips = max(levels - 1, 1)
        self.scratch = [
            pltpu.VMEM(pre_slabs.shape, BF16),
            pltpu.VMEM((self.wide, self.half), F32),
            pltpu.VMEM((self.wide, self.half), BF16),
            pltpu.VMEM((self.wide, self.half), BF16),
            pltpu.VMEM((self.wide + self.out_wide, self.half), BF16),
            pltpu.VMEM((4, 2, self.half), F32),
            pltpu.VMEM((levels, 2, self.half), F32),
            pltpu.VMEM((self.ctx_size, 2, self.half), F32),
            DMA((self.ctx_size,)), DMA((self.ctx_size,)),
            DMA((6,)),
            DMA((chips,)), DMA((chips,)),
            DMA((self.ctx_size,)), DMA((self.ctx_size,)),
        ] + line_sems(self.ctx_size) + [
            pltpu.VMEM((self.ctx_size, self.out_wide, self.half), BF16),
            DMA((self.ctx_size,)), DMA((self.ctx_size,)),
        ]

    def bind(self, in_refs, out_refs, side_refs, scratch):
        pre_ref, norm_ref, gain_second_ref, out_ref = in_refs
        all_ref, gains_ref = out_refs
        slabs, own_half, far_half, from_far, quarter, swaps, by_level, by_place = scratch[:8]
        all_send, all_recv, duo, lev_send, lev_recv, ctx_send, ctx_recv = scratch[8:15]
        ctx_size, levels, half, rows = self.ctx_size, self.levels, self.half, self.rows
        place = lax.axis_index("ctx")
        _, _, level, partner, others = tp_peers(self.tp_size)
        far = {"fsdp": 1 - lax.axis_index("fsdp")}
        tile = min(512, half)
        line_begin, line_finish = line_gather(quarter, all_ref, ctx_size, scratch[15:18])
        out_slots, out_send, out_recv = scratch[18:21]
        wide, out_wide = self.wide, self.out_wide

        def out_slab(step):
            peer = lax.rem(place + step, ctx_size)
            return remote(
                rows_at(out_ref, peer * out_wide, out_wide), out_slots.at[place],
                out_send.at[step], out_recv.at[step], {"ctx": peer},
            )

        def out_arrival(step):
            src = lax.rem(place + ctx_size - step, ctx_size)
            where = out_slots.at[src]
            return remote(where, where, out_send.at[step], out_recv.at[step], {"ctx": src})

        def slab(step):
            peer = lax.rem(place + step, ctx_size)
            return remote(
                pre_ref.at[peer], slabs.at[place], all_send.at[step], all_recv.at[step], {"ctx": peer}
            )

        def slab_arrival(step):
            src = lax.rem(place + ctx_size - step, ctx_size)
            return remote(
                slabs.at[src], slabs.at[src], all_send.at[step], all_recv.at[step], {"ctx": src}
            )

        grads = remote(far_half, from_far, duo.at[0], duo.at[1], far)
        gain_x = remote(swaps.at[0], swaps.at[1], duo.at[2], duo.at[3], far)
        gain_core = remote(swaps.at[2], swaps.at[3], duo.at[4], duo.at[5], {"tp": partner})

        def gain_level(index):
            return remote(
                by_level.at[level], by_level.at[level], lev_send.at[index],
                lev_recv.at[levels - 2 - index], {"tp": others[index]},
            )

        def gain_level_arrival(index):
            where = by_level.at[lax.rem(level + 1 + index, levels)]
            return remote(where, where, lev_send.at[index], lev_recv.at[index], {"tp": others[index]})

        def gain_place(step):
            peer = lax.rem(place + step, ctx_size)
            return remote(
                by_place.at[place], by_place.at[place], ctx_send.at[step], ctx_recv.at[step],
                {"ctx": peer},
            )

        def gain_place_arrival(step):
            src = lax.rem(place + ctx_size - step, ctx_size)
            where = by_place.at[src]
            return remote(where, where, ctx_send.at[step], ctx_recv.at[step], {"ctx": src})

        def product(at):
            columns = pl.ds(pl.multiple_of(at, tile), tile)
            total = jnp.dot(
                slabs[0], norm_ref[0:rows, columns], preferred_element_type=F32
            )
            for z in range(1, ctx_size):
                total += jnp.dot(
                    slabs[z], norm_ref[z * rows : (z + 1) * rows, columns],
                    preferred_element_type=F32,
                )
            return total

        def begin():
            for step in range(1, ctx_size):
                slab(step).start()
            for step in range(1, ctx_size):
                out_slab(step).start()
            slabs[place] = pre_ref[place]
            out_slots[place] = out_ref[pl.ds(pl.multiple_of(place * out_wide, out_wide), out_wide), :]

        def middle():
            for step in range(1, ctx_size):
                slab_arrival(step).wait_recv()

            @pl.loop(0, half // tile)
            def _(i):
                far_half[:, pl.ds(pl.multiple_of(i * tile, tile), tile)] = product(
                    half + i * tile
                ).astype(BF16)

            grads.start()

            @pl.loop(0, half // tile)
            def _(i):
                own_half[:, pl.ds(pl.multiple_of(i * tile, tile), tile)] = product(i * tile)

        def end():
            gain_first = side_refs[0]
            swaps[0, 0:1, :] = gain_first[:, half:]
            swaps[0, 1:2, :] = gain_second_ref[:, half:]
            gain_x.start()
            for step in range(1, ctx_size):
                out_arrival(step).wait_recv()
            total = out_slots[0].astype(F32)
            for z in range(1, ctx_size):
                total += out_slots[z].astype(F32)
            quarter[wide : wide + out_wide, :] = total.astype(BF16)
            grads.wait_recv()
            quarter[0:wide, :] = (own_half[...] + from_far[...].astype(F32)).astype(BF16)
            line_begin()
            gain_x.wait_recv()
            swaps[2, 0:1, :] = gain_first[:, :half] + swaps[1, 0:1, :]
            swaps[2, 1:2, :] = gain_second_ref[:, :half] + swaps[1, 1:2, :]
            gain_core.start()
            gain_core.wait_recv()
            by_level[level] = swaps[2] + swaps[3]
            for index in range(levels - 1):
                gain_level(index).start()
            for index in range(levels - 1):
                gain_level_arrival(index).wait_recv()
            total = by_level[0]
            for lev in range(1, levels):
                total += by_level[lev]
            by_place[place] = total
            for step in range(1, ctx_size):
                gain_place(step).start()
            for step in range(1, ctx_size):
                gain_place_arrival(step).wait_recv()
            total = by_place[0]
            for z in range(1, ctx_size):
                total += by_place[z]
            gains_ref[...] = total
            line_finish()
            for step in range(1, ctx_size):
                slab(step).wait_send()
                out_slab(step).wait_send()
                gain_place(step).wait_send()
            for index in range(levels - 1):
                gain_level(index).wait_send()
            grads.wait_send()
            gain_x.wait_send()
            gain_core.wait_send()

        return begin, middle, end


def reduce_gather(term, extras, finish, side_shapes, mesh_shape, identity, blocks, across, aside=None):
    ctx_size, tp_size = mesh_shape
    levels = tp_size // 2
    width = term.shape[1]
    block_rows = term.shape[0] // blocks
    rows = block_rows // tp_size
    reach = ctx_size if across else 1
    beside = aside is not None
    aside_inputs = aside.inputs if beside else ()
    aside_outs = aside.outs if beside else ()
    aside_scratch = aside.scratch if beside else []

    def kernel(term_ref, *refs):
        extra_refs = refs[: len(extras)]
        refs = refs[len(extras) :]
        aside_in = refs[: len(aside_inputs)]
        refs = refs[len(aside_inputs) :]
        all_ref = refs[0]
        side_refs = refs[1 : 1 + len(side_shapes)]
        refs = refs[1 + len(side_shapes) :]
        aside_out = refs[: len(aside_outs)]
        refs = refs[len(aside_outs) :]
        from_core, stage, from_chip, mine = refs[:4]
        refs = refs[4:]
        if blocks == 2:
            pair_stage, from_pair = refs[:2]
            refs = refs[2:]
        sems = refs[:7]
        core_send, core_recv, chip_send, chip_recv, pair_sems = refs[7:12]
        place = lax.axis_index("ctx")
        me, core, level, partner, others = tp_peers(tp_size)
        enter(
            ctx_size, tp_size, along=across, pair=blocks == 2 and not beside,
            side=beside and aside.side, line=beside,
        )
        if beside:
            aside_begin, aside_middle, aside_end = aside.bind(
                aside_in, aside_out, side_refs, refs[12:]
            )
            aside_begin()

        def to_core(block, lev):
            slot = block * levels + lev
            return remote(
                rows_at(term_ref, block * block_rows + (2 * lev + 1 - core) * rows, rows),
                from_core.at[slot], core_send.at[slot], core_recv.at[slot], {"tp": partner},
            )

        def to_chip(index):
            return remote(
                stage.at[index], from_chip.at[levels - 2 - index], chip_send.at[index],
                chip_recv.at[levels - 2 - index], {"tp": others[index]},
            )

        def chip_sum(block, lev):
            own = term_ref[
                pl.ds(pl.multiple_of(block * block_rows + (2 * lev + core) * rows, rows), rows), :
            ]
            return own.astype(F32) + from_core[block * levels + lev].astype(F32)

        for lev in range(levels):
            for block in range(blocks):
                to_core(block, lev).start()
        for lev in range(levels):
            for block in range(blocks):
                to_core(block, lev).wait_recv()
        for index in range(levels - 1):
            lev = lax.rem(level + 1 + index, levels)
            for block in range(blocks):
                stage[index, block * rows : (block + 1) * rows, :] = chip_sum(block, lev).astype(
                    BF16
                )
            to_chip(index).start()
        if beside:
            aside_middle()
        for index in range(levels - 1):
            to_chip(index).wait_recv()

        def tp_sum(block):
            total = chip_sum(block, level)
            for index in range(levels - 1):
                total += from_chip[
                    index, pl.ds(pl.multiple_of(block * rows, rows), rows), :
                ].astype(F32)
            return total

        if blocks == 2:
            low = lax.rem(place, 2)
            pair_stage[...] = tp_sum(1 - low).astype(BF16)
            swap = remote(
                pair_stage, from_pair, pair_sems.at[0], pair_sems.at[1], {"ctx": place + 1 - 2 * low}
            )
            swap.start()
            total = tp_sum(low)
            swap.wait_recv()
            total += from_pair[...].astype(F32)
        else:
            total = tp_sum(0)
        start = pl.multiple_of(me * rows, rows)
        mine[...] = finish(total, start, *extra_refs, *side_refs)
        gather_rows(mine, all_ref, reach, tp_size, sems)
        if beside:
            aside_end()
        for lev in range(levels):
            for block in range(blocks):
                to_core(block, lev).wait_send()
        for index in range(levels - 1):
            to_chip(index).wait_send()
        if blocks == 2:
            swap.wait_send()

    chips = max(levels - 1, 1)
    scratch = [
        pltpu.VMEM((blocks * levels, rows, width), BF16),
        pltpu.VMEM((chips, blocks * rows, width), BF16),
        pltpu.VMEM((chips, blocks * rows, width), BF16),
        pltpu.VMEM((rows, width), BF16),
    ]
    if blocks == 2:
        scratch += [pltpu.VMEM((rows, width), BF16)] * 2
    scratch += gather_sems(reach, tp_size)
    scratch += [
        DMA((blocks * levels,)), DMA((blocks * levels,)), DMA((chips,)), DMA((chips,)), DMA((2,)),
    ]
    scratch += aside_scratch
    return pl.pallas_call(
        kernel,
        out_shape=(
            jax.ShapeDtypeStruct((reach * block_rows, width), BF16),
            *(jax.ShapeDtypeStruct(shape, F32) for shape in side_shapes),
            *aside_outs,
        ),
        in_specs=[VMEM_SPEC] * (1 + len(extras) + len(aside_inputs)),
        out_specs=(HBM_SPEC,) + (VMEM_SPEC,) * len(side_shapes)
        + (aside.out_specs if beside else ()),
        scratch_shapes=scratch,
        compiler_params=pltpu.CompilerParams(
            collective_id=identity, has_side_effects=True, vmem_limit_bytes=32 << 20
        ),
    )(term, *extras, *aside_inputs)


def unit_places(place):
    low = place % 2
    part = ((place + 1) // 2) % 2
    base = 2 + 3 * part
    return [base, base + 1, base + 2, low, 1 - low], part


def opening(cot_rows, groups, gains, hidden_weights, mesh_shape, identity):
    ctx_size, tp_size = mesh_shape
    block_rows, width = cot_rows.shape
    rows = block_rows // tp_size
    weights = [w for group in groups for w in group]
    depth = weights[0].shape[0]
    places = []
    for g, group in enumerate(groups):
        at = 0
        for w in group:
            places.append((g, at, w.shape[1]))
            at += w.shape[1]
    wholes = [
        jax.ShapeDtypeStruct((2 * depth, sum(w.shape[1] for w in group)), BF16) for group in groups
    ]

    unit = hidden_weights[0].shape[1] // 8
    kinds = len(hidden_weights)

    def kernel(cot_ref, *refs):
        weight_refs = refs[: len(weights)]
        gain_ref = refs[len(weights)]
        refs = refs[len(weights) + 1 :]
        hidden_refs = refs[:kinds]
        refs = refs[kinds:]
        all_ref, gain_far_ref = refs[:2]
        whole_refs = refs[2 : 2 + len(groups)]
        refs = refs[2 + len(groups) :]
        pack_refs = refs[:5]
        refs = refs[5:]
        sems = refs[:7]
        send, recv, pack_sems = refs[7:]
        units, _ = unit_places(lax.axis_index("ctx"))
        packs = [
            pltpu.make_async_copy(
                hidden_refs[k].at[:, pl.ds(pl.multiple_of(at * unit, unit), unit)],
                pack_refs[c].at[:, pl.ds(k * unit, unit)], pack_sems.at[c * kinds + k],
            )
            for c, at in enumerate(units) for k in range(kinds)
        ]
        enter(ctx_size, tp_size, along=True, side=True)
        far = {"fsdp": 1 - lax.axis_index("fsdp")}
        last = len(weights)
        swaps = [remote(gain_ref, gain_far_ref, send.at[last], recv.at[last], far)]
        for i, (g, at, wide) in enumerate(places):
            swaps.append(
                remote(
                    weight_refs[i], whole_refs[g].at[pl.ds(depth, depth), pl.ds(at, wide)],
                    send.at[i], recv.at[i], far,
                )
            )
        for swap in swaps:
            swap.start()
        for pack in packs:
            pack.start()
        for i, (g, at, wide) in enumerate(places):
            whole_refs[g][0:depth, at : at + wide] = weight_refs[i][...]
        mine = rows_at(cot_ref, lax.axis_index("tp") * rows, rows)
        gather_rows(mine, all_ref, ctx_size, tp_size, sems, block=cot_ref)
        for pack in packs:
            pack.wait()
        for swap in swaps:
            swap.wait()

    return pl.pallas_call(
        kernel,
        out_shape=(
            jax.ShapeDtypeStruct((ctx_size * block_rows, width), BF16),
            jax.ShapeDtypeStruct(gains.shape, F32),
            *wholes,
            *[jax.ShapeDtypeStruct((depth, kinds * unit), BF16)] * 5,
        ),
        in_specs=[VMEM_SPEC] * (2 + len(weights)) + [HBM_SPEC] * kinds,
        out_specs=(HBM_SPEC,) + (VMEM_SPEC,) * (6 + len(groups)),
        scratch_shapes=gather_sems(ctx_size, tp_size)
        + [DMA((len(weights) + 1,)), DMA((len(weights) + 1,)), DMA((5 * kinds,))],
        compiler_params=pltpu.CompilerParams(
            collective_id=identity, has_side_effects=True, vmem_limit_bytes=40 << 20
        ),
    )(cot_rows, *weights, gains, *hidden_weights)


def place_blocks(table, pieces, wide, blocks, base=None):
    count = len(pieces)
    depth = pieces[0][0].shape[0]
    tile = min(depth, 1024)

    def kernel(table_ref, *refs):
        out_ref = refs[-1]
        step = pl.program_id(1)
        for k in range(count):
            @pl.when(step == k)
            def _(k=k):
                out_ref[...] = refs[k][...].astype(F32)

    return pl.pallas_call(
        kernel,
        grid_spec=pltpu.PrefetchScalarGridSpec(
            num_scalar_prefetch=1,
            grid=(depth // tile, count),
            in_specs=[
                pl.BlockSpec((tile, wide), lambda i, step, table_ref, at=at: (i, at))
                for _, at in pieces
            ]
            + ([] if base is None else [HBM_SPEC]),
            out_specs=pl.BlockSpec((tile, wide), lambda i, step, table_ref: (i, table_ref[step])),
        ),
        out_shape=jax.ShapeDtypeStruct((depth, blocks * wide), F32),
        input_output_aliases={} if base is None else {1 + count: 0},
    )(table, *(array for array, _ in pieces), *(() if base is None else (base,)))


def transposed_grads(slices, first, widths):
    count, columns, depth = slices.shape
    tile = min(depth, 256)

    def kernel(in_ref, *out_refs):
        head = jnp.concatenate([in_ref[z, 0:first, :] for z in range(count)], axis=0)
        head = head.astype(F32).T
        at = 0
        for out_ref, wide in zip(out_refs[:-1], widths[:-1]):
            out_ref[...] = head[:, at : at + wide]
            at += wide
        last = jnp.concatenate([in_ref[z, first:columns, :] for z in range(count)], axis=0)
        out_refs[-1][...] = last.astype(F32).T

    return pl.pallas_call(
        kernel,
        grid=(depth // tile,),
        in_specs=[pl.BlockSpec((count, columns, tile), lambda i: (0, 0, i))],
        out_specs=tuple(pl.BlockSpec((tile, wide), lambda i: (i, 0)) for wide in widths),
        out_shape=tuple(jax.ShapeDtypeStruct((depth, wide), F32) for wide in widths),
    )(slices)


def mean_square(rows):
    return jnp.mean(rows * rows, axis=-1, keepdims=True)


def finish_middle(total, start, resid_ref, gain_ref, middle_ref):
    rows = total.shape[0]
    middle = resid_ref[pl.ds(start, rows), :].astype(F32) + total
    middle_ref[...] = middle
    return (middle * lax.rsqrt(mean_square(middle) + EPSILON) * gain_ref[...]).astype(BF16)


def norm_back(grad, base, values, gain):
    rms = lax.rsqrt(mean_square(values) + EPSILON)
    scaled = grad * gain
    gain_grad = jnp.sum(grad * values * rms, axis=0, keepdims=True)
    cube = rms * rms * rms
    full = base + rms * scaled - values * cube * jnp.mean(scaled * values, axis=-1, keepdims=True)
    return full, gain_grad


def finish_grad_middle(total, start, middle_ref, cot_ref, gain_ref, grad_ref, gain_grad_ref):
    base = cot_ref[pl.ds(start, total.shape[0]), :].astype(F32)
    full, gain_grad = norm_back(total, base, middle_ref[...], gain_ref[...])
    grad_ref[...] = full
    gain_grad_ref[...] = gain_grad
    return full.astype(BF16)


def finish_grad_input(total, start, grad_ref, resid_ref, gain_ref, gain_grad_ref):
    values = resid_ref[pl.ds(start, total.shape[0]), :].astype(F32)
    full, gain_grad = norm_back(total, grad_ref[...], values, gain_ref[...])
    gain_grad_ref[...] = gain_grad
    return full.astype(BF16)


def finish_output(total, start, middle_ref):
    return (middle_ref[...] + total).astype(BF16)


def make_local(ctx_size, tp_size):
    mesh_shape = (ctx_size, tp_size)
    swap_x = [(0, 1), (1, 0)]
    swap_z = [(i, i ^ 1) for i in range(ctx_size)]

    def swap_rows(array):
        return lax.ppermute(array, "fsdp", swap_x)

    def local(
        inputs, cotangent, prefix, attn_gain, w_query, key_projection, value_projection, w_out,
        ffn_gain, w_gate, w_up, w_down,
    ):
        side = lax.axis_index("fsdp")
        place = lax.axis_index("ctx")
        units, part = unit_places(place)
        row_count, model_width = inputs.shape[1:]
        half_width = model_width // 2
        query_width = w_query.shape[1]
        key_width = key_projection.shape[1]
        ffn_width = w_gate.shape[1]
        unit = ffn_width // 8
        query_heads = query_width // HEAD_SIZE
        kv_heads = key_width // HEAD_SIZE
        row_start = place * row_count
        pair_start = (place // 2) * 2 * row_count

        def own_first(rows):
            a = lax.dynamic_slice_in_dim(rows, side * half_width, half_width, 1)
            b = lax.dynamic_slice_in_dim(rows, (1 - side) * half_width, half_width, 1)
            return jnp.concatenate([a, b], axis=1)

        gains = jnp.stack([attn_gain, ffn_gain]).astype(F32)
        residual_low = own_first(inputs[0])
        cot_low = own_first(cotangent[0])
        rows_all, gains_far, qkv_weight, out_weight, *owns = opening(
            jnp.concatenate([cot_low, residual_low], axis=1),
            ((w_query, jnp.concatenate([key_projection, value_projection], axis=1)), (w_out,)),
            gains, (w_gate, w_up, w_down), mesh_shape, 0,
        )
        cot_all = rows_all[:, :model_width]
        gains = jnp.concatenate([gains, gains_far], axis=1)
        gain_first, gain_second = gains[0], gains[1]
        others = [swap_rows(owns[0]), swap_rows(owns[1]), None, None, None]

        cosine_lookup, sine_lookup = (table.T for table in rope_tables(row_start, row_count))
        residual = residual_low.astype(F32)
        rms_first = lax.rsqrt(jnp.mean(residual * residual, axis=-1, keepdims=True) + EPSILON)
        normalized_rows = (residual * rms_first * gain_first).astype(BF16)
        qkv = contract(qkv_weight, normalized_rows, 0, 1)
        queries = apply_rotary(
            qkv[:query_width].reshape(query_heads, HEAD_SIZE, row_count),
            cosine_lookup, sine_lookup, 1.0,
        ).astype(BF16)
        key_rot = apply_rotary(
            qkv[query_width : query_width + key_width].reshape(kv_heads, HEAD_SIZE, row_count),
            cosine_lookup, sine_lookup, 1.0,
        ).astype(BF16)
        value_rows = qkv[query_width + key_width :].astype(BF16)
        kv_own = jnp.concatenate([key_rot, value_rows.reshape(kv_heads, HEAD_SIZE, row_count)], axis=0)
        kv_whole = lax.all_gather(
            kv_own.reshape(2 * key_width, row_count).T, "ctx", axis=0, tiled=True
        )
        length_total = kv_whole.shape[0]
        by_place = kv_whole.reshape(length_total, 2 * kv_heads, HEAD_SIZE).transpose(1, 0, 2)
        by_feature = kv_whole.T.reshape(2 * kv_heads, HEAD_SIZE, length_total)
        bounds = jnp.stack([prefix[0], row_start.astype(jnp.int32)])
        attended, log_total = attend(
            bounds, queries, by_place[:kv_heads], by_feature[kv_heads:]
        )
        attended_flat = attended.reshape(query_width, row_count)
        attn_term = contract(attended_flat, out_weight, 0, 1).astype(BF16)
        attn_term, owns[2], others[0] = lax.optimization_barrier((attn_term, owns[2], others[0]))
        others[2] = swap_rows(owns[2])
        slice_shape = (row_count // tp_size, model_width)
        normed_all, middle = reduce_gather(
            attn_term, (residual_low, gain_second[None]), finish_middle,
            (slice_shape,), mesh_shape, 1, 1, True,
        )

        ffn_term = 0.0
        mid_term = 0.0
        sides = []
        fars = []
        received = []

        def pair(rows):
            return lax.dynamic_slice_in_dim(rows, pair_start, 2 * row_count, 0)

        def outer(sides_of, part_of):
            return [contract(part_of(rows), cols, 0, 0) for rows, cols in sides_of]

        def near_of(c):
            return jnp.concatenate(outer(sides[c], lambda rows: rows[:, :half_width]), axis=1)

        def summed(c, near=None):
            near = near_of(c) if near is None else near
            return (near + received[c].astype(F32)).astype(BF16)

        def forward(c):
            both_w = jnp.concatenate([owns[c], others[c]], axis=0)
            pair_w, down_w = both_w[:, : 2 * unit], both_w[:, 2 * unit :]
            both = jnp.dot(normed_all, pair_w, preferred_element_type=F32)
            gating, upward = both[:, :unit], both[:, unit:]
            grad_hidden = jnp.dot(cot_all, down_w, preferred_element_type=F32)
            sigmoid_gate = jax.nn.sigmoid(gating)
            hidden = (gating * sigmoid_gate * upward).astype(BF16)
            grad_gating = (
                grad_hidden * upward * sigmoid_gate * (1.0 + gating * (1.0 - sigmoid_gate))
            ).astype(BF16)
            grad_upward = (grad_hidden * gating * sigmoid_gate).astype(BF16)
            grad_both = jnp.concatenate([grad_gating, grad_upward], axis=1)
            sides.append(((normed_all, grad_both), (cot_all, hidden)))
            far = outer(sides[c], lambda rows: rows[:, half_width:])
            fars.append(jnp.concatenate([f.astype(BF16) for f in far], axis=1))
            return pair_w, down_w, grad_both, hidden

        for c in range(4):
            if c:
                others[c], fars[-1] = lax.optimization_barrier((others[c], fars[-1]))
            if c == 1:
                owns[3], others[1] = lax.optimization_barrier((owns[3], others[1]))
                others[3] = swap_rows(owns[3])
            pair_w, down_w, grad_both, hidden = forward(c)
            ffn_term += contract(pair(hidden), down_w, 1, 1)
            mid_term += contract(pair(grad_both), pair_w, 1, 1)

        def swap_ctx(total):
            return lax.ppermute(total, "ctx", swap_z)

        received = [swap_rows(fars[0]), swap_rows(fars[1])]
        mid_low, fars[2], fars[3], received[0] = lax.optimization_barrier(
            (mid_term.astype(BF16), fars[2], fars[3], received[0])
        )
        received.append(swap_rows(fars[2]))
        totals = [summed(0)]
        mid_low, totals[0] = lax.optimization_barrier((mid_low, totals[0]))
        swapped = [swap_ctx(totals[0])]
        branch_low, grad_middle, gain_grad_second = reduce_gather(
            mid_low, (middle, cot_low, gain_second[None]), finish_grad_middle,
            (slice_shape, (1, model_width)), mesh_shape, 2, 2, False,
        )
        branch_low, received[1], owns[4], swapped[0], rows_all = lax.optimization_barrier(
            (branch_low, received[1], owns[4], swapped[0], rows_all)
        )
        others[4] = swap_rows(owns[4])
        totals.append(summed(1))
        branch_low, totals[1] = lax.optimization_barrier((branch_low, totals[1]))
        swapped.append(swap_ctx(totals[1]))
        grad_out = jnp.dot(attended_flat, branch_low, preferred_element_type=F32)
        grad_out_half = grad_out[:, half_width:].astype(BF16)
        grad_attended = contract(out_weight, branch_low, 0, 1).astype(BF16)
        grad_query_rot, grad_kv = attend_back(
            bounds, queries, by_place[:kv_heads], by_feature[:kv_heads], by_place[kv_heads:],
            grad_attended.reshape(query_heads, HEAD_SIZE, row_count), log_total,
        )
        grad_kv = grad_kv.reshape(2 * key_width, length_total)
        far_base = 2 + 3 * (1 - part)
        table = jnp.stack(units + [far_base, far_base + 1, far_base + 2])
        grad_kv, received[2] = lax.optimization_barrier((grad_kv, received[2]))
        totals.append(summed(2))
        grad_kv, totals[2], others[4], fars[3], grad_out_half = lax.optimization_barrier(
            (grad_kv, totals[2], others[4], fars[3], grad_out_half)
        )
        swapped.append(swap_ctx(totals[2]))
        grad_out_far = swap_rows(grad_out_half)
        received.append(swap_rows(fars[3]))
        forward(4)
        near_four = near_of(4)
        early = totals + swapped[:1]
        placed = [
            place_blocks(
                jnp.stack([table[0], table[1], table[2], table[5]]),
                [(piece, block) for piece in early], unit, 8,
            )
            for block in range(3)
        ]
        near_three = near_of(3)
        residual_all = rows_all[:, model_width:].astype(F32)
        rms_all = lax.rsqrt(jnp.mean(residual_all * residual_all, axis=-1, keepdims=True) + EPSILON)
        norm_all = (residual_all * rms_all * gain_first).astype(BF16)
        grad_kv, placed, near_three, near_four, norm_all, fars[4], swapped[1] = (
            lax.optimization_barrier(
                (grad_kv, placed, near_three, near_four, norm_all, fars[4], swapped[1])
            )
        )
        received.append(swap_rows(fars[4]))
        output_rows, grad_kv = reduce_gather(
            ffn_term.astype(BF16), (middle,), finish_output, (), mesh_shape, 3, 2, False,
            KvSum(grad_kv, ctx_size),
        )
        output_rows, grad_kv, swapped[2] = lax.optimization_barrier(
            (output_rows, grad_kv, swapped[2])
        )
        grad_query_pre = apply_rotary(
            grad_query_rot, cosine_lookup, sine_lookup, -1.0
        ).astype(BF16).reshape(query_width, row_count)
        grad_key_pre = apply_rotary(
            grad_kv[:key_width].reshape(kv_heads, HEAD_SIZE, row_count),
            cosine_lookup, sine_lookup, -1.0,
        ).astype(BF16).reshape(key_width, row_count)
        grad_value_pre = grad_kv[key_width:].astype(BF16)
        grad_qkv_pre = jnp.concatenate([grad_query_pre, grad_key_pre, grad_value_pre], axis=0)
        attn_width = grad_qkv_pre.shape[0]
        pre_slabs = grad_qkv_pre.reshape(ctx_size, attn_width // ctx_size, row_count)
        normed_term = contract(grad_qkv_pre, qkv_weight, 0, 1).astype(BF16)
        grad_out_rows = (grad_out[:, :half_width] + grad_out_far.astype(F32)).astype(BF16)
        normed_term, received[3], grad_out_far = lax.optimization_barrier(
            (normed_term, received[3], grad_out_far)
        )
        totals.append(summed(3, near_three))
        normed_term, totals[3] = lax.optimization_barrier((normed_term, totals[3]))
        input_rows, _, grad_attn, gain_grads = reduce_gather(
            normed_term,
            (grad_middle, residual_low, gain_first[None]), finish_grad_input,
            ((1, model_width),), mesh_shape, 4, 1, False,
            AttnTail(pre_slabs, norm_all, gain_grad_second, grad_out_rows, mesh_shape),
        )
        grad_attn, received[4] = lax.optimization_barrier((grad_attn, received[4]))
        grad_query, grad_key, grad_value, grad_out = transposed_grads(
            grad_attn.reshape(ctx_size, -1, half_width), attn_width // ctx_size,
            (query_width, key_width, key_width, query_width),
        )
        totals.append(summed(4, near_four))

        def result(block):
            pieces = [(piece, block) for piece in totals[3:] + swapped[1:]]
            late = jnp.stack([table[3], table[4], table[6], table[7]])
            return place_blocks(late, pieces, unit, 8, placed[block])

        return (
            own_first(output_rows)[None],
            own_first(input_rows)[None],
            gain_grads[0],
            grad_query,
            grad_key,
            grad_value,
            grad_out,
            gain_grads[1],
            result(0),
            result(1),
            result(2),
        )

    return local


def solution(mesh):
    return jax.shard_map(
        make_local(mesh.shape["ctx"], mesh.shape["tp"]),
        mesh=mesh,
        in_specs=(
            P("fsdp", "ctx", None), P("fsdp", "ctx", None), P("fsdp"), P("fsdp"),
            P("fsdp", "tp"), P("fsdp", "tp"), P("fsdp", "tp"), P("fsdp", "tp"),
            P("fsdp"), P("fsdp", "tp"), P("fsdp", "tp"), P("fsdp", "tp"),
        ),
        out_specs=(
            P("fsdp", "ctx", None), P("fsdp", "ctx", None), P("fsdp"), P("fsdp", "tp"),
            P("fsdp", "tp"), P("fsdp", "tp"), P("fsdp", "tp"), P("fsdp"),
            P("fsdp", "tp"), P("fsdp", "tp"), P("fsdp", "tp"),
        ),
        check_vma=False,
    )
```

```python
import math

import jax
import jax.numpy as jnp
from jax import lax
from jax.experimental import pallas as pl
from jax.experimental.pallas import tpu as pltpu
from jax.sharding import PartitionSpec as P

HEAD_SIZE = 64
EPSILON = 1e-05
THETA = 500000.0
MASKED = -1e30
F32 = jnp.float32
BF16 = jnp.bfloat16


def contract(left, right, left_dim, right_dim):
    return lax.dot_general(
        left, right, (((left_dim,), (right_dim,)), ((), ())), preferred_element_type=F32
    )


def rope_tables(row_start, row_count):
    position = (row_start + jnp.arange(row_count, dtype=jnp.int32)).astype(F32)
    exponent = jnp.arange(HEAD_SIZE // 2, dtype=jnp.int32).astype(F32) * (2.0 / HEAD_SIZE)
    angles = position[:, None] * jnp.power(THETA, -exponent)[None, :]
    return (jnp.cos(angles), jnp.sin(angles))


def apply_rotary(values, cosine_lookup, sine_lookup, direction):
    half_width = values.shape[1] // 2
    leading = values[:, :half_width]
    trailing = values[:, half_width:]
    sin = direction * sine_lookup
    return jnp.concatenate(
        [leading * cosine_lookup - trailing * sin, trailing * cosine_lookup + leading * sin],
        axis=1,
    )


def allowed_pairs(bounds_ref, shape):
    key_place = lax.broadcasted_iota(jnp.int32, shape, 0)
    query_place = bounds_ref[1] + lax.broadcasted_iota(jnp.int32, shape, 1)
    return (key_place <= query_place) | (key_place < bounds_ref[0])


SCORE_SCALE = 1.0 / math.sqrt(HEAD_SIZE)
SMEM_SPEC = pl.BlockSpec(memory_space=pltpu.SMEM)


def attend(bounds, queries, keys, values_flat):
    heads, _, rows = queries.shape
    places = keys.shape[1]
    group = heads // keys.shape[0]

    def kernel(bounds_ref, query_ref, key_ref, value_ref, out_ref, log_ref):
        @pl.loop(0, heads)
        def _(h):
            k = h // group
            scores = jnp.dot(key_ref[k], query_ref[h], preferred_element_type=F32) * SCORE_SCALE
            scores = jnp.where(allowed_pairs(bounds_ref, (places, rows)), scores, MASKED)
            peak = jnp.max(scores, axis=0, keepdims=True)
            weights = jnp.exp(scores - peak)
            total = jnp.sum(weights, axis=0, keepdims=True)
            probabilities = (weights * (1.0 / total)).astype(BF16)
            out_ref[h] = jnp.dot(
                value_ref[k], probabilities, preferred_element_type=F32
            ).astype(BF16)
            log_ref[h] = peak + jnp.log(total)

    return pl.pallas_call(
        kernel,
        out_shape=(
            jax.ShapeDtypeStruct(queries.shape, BF16),
            jax.ShapeDtypeStruct((heads, 1, rows), F32),
        ),
        in_specs=[SMEM_SPEC] + [pl.BlockSpec(memory_space=pltpu.VMEM)] * 3,
        out_specs=(pl.BlockSpec(memory_space=pltpu.VMEM),) * 2,
        compiler_params=pltpu.CompilerParams(vmem_limit_bytes=24 << 20),
    )(bounds, queries, keys, values_flat)


def attend_back(bounds, queries, keys, keys_flat, values, grads, log_total):
    heads, size, rows = queries.shape
    key_heads, places, _ = keys.shape
    group = heads // key_heads

    def kernel(
        bounds_ref, query_ref, key_ref, key_flat_ref, value_ref, grad_ref, log_ref, query_grad_ref,
        both_grad_ref, totals,
    ):
        totals[...] = jnp.zeros_like(totals)

        @pl.loop(0, heads)
        def _(h):
            k = h // group
            scores = jnp.dot(key_ref[k], query_ref[h], preferred_element_type=F32) * SCORE_SCALE
            scores = jnp.where(allowed_pairs(bounds_ref, (places, rows)), scores, MASKED)
            probabilities = jnp.exp(scores - log_ref[h])
            grad_probs = jnp.dot(value_ref[k], grad_ref[h], preferred_element_type=F32)
            delta = jnp.sum(probabilities * grad_probs, axis=0, keepdims=True)
            grad_scores = (probabilities * (grad_probs - delta)).astype(BF16)
            query_grad_ref[h] = SCORE_SCALE * jnp.dot(
                key_flat_ref[k], grad_scores, preferred_element_type=F32
            )
            totals[k] += SCORE_SCALE * contract(query_ref[h], grad_scores, 1, 1)
            totals[key_heads + k] += contract(grad_ref[h], probabilities.astype(BF16), 1, 1)

        both_grad_ref[...] = totals[...].astype(BF16)

    return pl.pallas_call(
        kernel,
        out_shape=(
            jax.ShapeDtypeStruct(queries.shape, F32),
            jax.ShapeDtypeStruct((2 * key_heads, size, places), BF16),
        ),
        in_specs=[SMEM_SPEC] + [pl.BlockSpec(memory_space=pltpu.VMEM)] * 6,
        out_specs=(pl.BlockSpec(memory_space=pltpu.VMEM),) * 2,
        scratch_shapes=[pltpu.VMEM((2 * key_heads, size, places), F32)],
        compiler_params=pltpu.CompilerParams(vmem_limit_bytes=32 << 20),
    )(bounds, queries, keys, keys_flat, values, grads, log_total)


MESH = pl.DeviceIdType.MESH
HBM_SPEC = pl.BlockSpec(memory_space=pl.ANY)
VMEM_SPEC = pl.BlockSpec(memory_space=pltpu.VMEM)
DMA = pltpu.SemaphoreType.DMA


def remote(src, dst, send, recv, peer):
    return pltpu.make_async_remote_copy(
        src_ref=src, dst_ref=dst, send_sem=send, recv_sem=recv, device_id=peer, device_id_type=MESH
    )


def rows_at(ref, start, count):
    return ref.at[pl.ds(pl.multiple_of(start, count), count)]


def guarded(condition, body):
    if condition is None:
        body()
    else:
        pl.when(condition)(body)


def tp_peers(tp_size):
    me = lax.axis_index("tp")
    core = lax.rem(me, 2)
    level = me // 2
    levels = tp_size // 2
    partner = me + 1 - 2 * core
    others = [lax.rem(level + step, levels) * 2 + core for step in range(1, levels)]
    return me, core, level, partner, others


def enter(ctx_size, tp_size, along=False, pair=False, side=False, tensor=True, line=False):
    place = lax.axis_index("ctx")
    barrier = pltpu.get_barrier_semaphore()

    def greet(peer):
        pl.semaphore_signal(barrier, inc=1, device_id=peer, device_id_type=MESH)

    count = 0
    if tensor:
        _, _, _, partner, others = tp_peers(tp_size)
        for peer in [partner] + others:
            greet({"tp": peer})
        count = count + 1 + len(others)
    if side:
        greet({"fsdp": 1 - lax.axis_index("fsdp")})
        count = count + 1
    if along:
        up = place + 1 < ctx_size
        down = place > 0

        @pl.when(up)
        def _():
            greet({"ctx": place + 1})

        @pl.when(down)
        def _():
            greet({"ctx": place - 1})

        count = count + up.astype(jnp.int32) + down.astype(jnp.int32)
    if pair:
        greet({"ctx": place + 1 - 2 * lax.rem(place, 2)})
        count = count + 1
    if line:
        for step in range(1, ctx_size):
            greet({"ctx": lax.rem(place + step, ctx_size)})
        count = count + ctx_size - 1
    pl.semaphore_wait(barrier, count)


def gather_sems(ctx_size, tp_size):
    spread = 2 * ctx_size - 1
    levels = tp_size // 2
    chips = max(levels - 1, 1)
    return [
        DMA((spread + 1,)), DMA((spread,)), DMA((chips, spread)), DMA((chips, spread)),
        DMA((levels, spread)), DMA((levels, spread)), DMA((1,)),
    ]


def gather_rows(mine, all_ref, ctx_size, tp_size, sems, block=None):
    hop_send, hop_recv, chip_send, chip_recv, core_send, core_recv, own_sem = sems
    place = lax.axis_index("ctx") if ctx_size > 1 else 0
    me, core, level, partner, others = tp_peers(tp_size)
    levels = tp_size // 2
    rows = mine.shape[0]
    middle = ctx_size - 1
    offsets = [0]
    for step in range(1, ctx_size):
        offsets += [-step, step]

    def spot(offset, who):
        return rows_at(all_ref, ((place + offset) * tp_size + who) * rows, rows)

    def hop(offset, step, src):
        slot = 2 * middle + 1 if offset == 0 and step < 0 else middle + offset
        return remote(
            src, spot(offset, me), hop_send.at[slot], hop_recv.at[middle + offset - step],
            {"ctx": place + step},
        )

    def hop_arrival(offset):
        step = -1 if offset < 0 else 1
        return remote(
            spot(offset, me), spot(offset, me), hop_send.at[middle + offset],
            hop_recv.at[middle + offset], {"ctx": place + step},
        )

    def chip(offset, index, src):
        return remote(
            src, spot(offset, me), chip_send.at[index, middle + offset],
            chip_recv.at[levels - 2 - index, middle + offset], {"tp": others[index]},
        )

    def chip_arrival(offset, index):
        where = spot(offset, others[index])
        return remote(
            where, where, chip_send.at[index, middle + offset],
            chip_recv.at[index, middle + offset], {"tp": others[index]},
        )

    def to_core(offset, index, who, src):
        return remote(
            src, spot(offset, who), core_send.at[index, middle + offset],
            core_recv.at[index, middle + offset], {"tp": partner},
        )

    def valid(offset):
        if offset == 0:
            return None
        return place + offset >= 0 if offset < 0 else place + offset < ctx_size

    def onward(offset):
        if offset < 0:
            return 1, jnp.logical_and(place + offset >= 0, place + 1 < ctx_size)
        return -1, jnp.logical_and(place + offset < ctx_size, place > 0)

    def fan_out(offset, src):
        for index in range(levels - 1):
            chip(offset, index, src).start()
        to_core(offset, 0, me, src).start()

    if block is None:
        own = pltpu.make_async_copy(mine, spot(0, me), own_sem.at[0])
    else:
        own = pltpu.make_async_copy(
            block, rows_at(all_ref, place * block.shape[0], block.shape[0]), own_sem.at[0]
        )
    own.start()
    if ctx_size > 1:
        @pl.when(place + 1 < ctx_size)
        def _():
            hop(0, 1, mine).start()

        @pl.when(place > 0)
        def _():
            hop(0, -1, mine).start()

    if block is None:
        fan_out(0, mine)
    for offset in offsets[1:]:
        def arrived(offset=offset):
            hop_arrival(offset).wait_recv()
            fan_out(offset, spot(offset, me))

        guarded(valid(offset), arrived)
        step, more = onward(offset)

        @pl.when(more)
        def _(offset=offset, step=step):
            hop(offset, step, spot(offset, me)).start()

    shared = offsets if block is None else offsets[1:]
    for offset in shared:
        def relay(offset=offset):
            for index in range(levels - 1):
                chip_arrival(offset, index).wait_recv()
                to_core(offset, 1 + index, others[index], spot(offset, others[index])).start()

        guarded(valid(offset), relay)

    for offset in shared:
        def drain(offset=offset):
            for index in range(levels):
                to_core(offset, index, me, spot(offset, me)).wait()
            for index in range(levels - 1):
                chip(offset, index, spot(offset, me)).wait_send()

        guarded(valid(offset), drain)
    own.wait()
    if ctx_size > 1:
        @pl.when(place + 1 < ctx_size)
        def _():
            hop(0, 1, mine).wait_send()

        @pl.when(place > 0)
        def _():
            hop(0, -1, mine).wait_send()

        for offset in offsets[1:]:
            step, more = onward(offset)

            @pl.when(more)
            def _(offset=offset, step=step):
                hop(offset, step, spot(offset, me)).wait_send()


def line_sems(ctx_size):
    spread = 2 * ctx_size - 1
    return [DMA((spread + 1,)), DMA((spread,)), DMA((1,))]


def line_gather(mine, all_ref, ctx_size, sems):
    hop_send, hop_recv, own_sem = sems
    place = lax.axis_index("ctx")
    rows = mine.shape[0]
    middle = ctx_size - 1
    offsets = [o for step in range(1, ctx_size) for o in (-step, step)]

    def spot(offset):
        return rows_at(all_ref, (place + offset) * rows, rows)

    def hop(offset, step, src):
        slot = 2 * middle + 1 if offset == 0 and step < 0 else middle + offset
        return remote(
            src, spot(offset), hop_send.at[slot], hop_recv.at[middle + offset - step],
            {"ctx": place + step},
        )

    def arrival(offset):
        step = -1 if offset < 0 else 1
        return remote(
            spot(offset), spot(offset), hop_send.at[middle + offset],
            hop_recv.at[middle + offset], {"ctx": place + step},
        )

    def valid(offset):
        return place + offset >= 0 if offset < 0 else place + offset < ctx_size

    def onward(offset):
        if offset < 0:
            return 1, jnp.logical_and(place + offset >= 0, place + 1 < ctx_size)
        return -1, jnp.logical_and(place + offset < ctx_size, place > 0)

    own = pltpu.make_async_copy(mine, spot(0), own_sem.at[0])
    ends = ((1, place + 1 < ctx_size), (-1, place > 0))

    def begin():
        for step, there in ends:
            @pl.when(there)
            def _(step=step):
                hop(0, step, mine).start()

        own.start()

    def stage(step):
        for offset in (-step, step):
            @pl.when(valid(offset))
            def _(offset=offset):
                arrival(offset).wait_recv()

            way, more = onward(offset)

            @pl.when(more)
            def _(offset=offset, way=way):
                hop(offset, way, spot(offset)).start()

    def drain():
        own.wait()
        for step, there in ends:
            @pl.when(there)
            def _(step=step):
                hop(0, step, mine).wait_send()

        for offset in offsets:
            step, more = onward(offset)

            @pl.when(more)
            def _(offset=offset, step=step):
                hop(offset, step, spot(offset)).wait_send()

    return begin, stage, drain


class KvSum:
    side = False

    def __init__(self, grad_kv, ctx_size):
        self.ctx_size = ctx_size
        self.inputs = (grad_kv,)
        self.rows = grad_kv.shape[1] // ctx_size
        self.block = (grad_kv.shape[0], self.rows)
        self.outs = (jax.ShapeDtypeStruct(self.block, F32),)
        self.out_specs = (VMEM_SPEC,)
        self.scratch = [
            pltpu.VMEM((ctx_size, *self.block), BF16), DMA((ctx_size,)), DMA((ctx_size,)),
        ]

    def bind(self, in_refs, out_refs, side_refs, scratch):
        (grad_ref,) = in_refs
        (sum_ref,) = out_refs
        slots, send, recv = scratch
        ctx_size, rows = self.ctx_size, self.rows
        place = lax.axis_index("ctx")

        def to(step):
            peer = lax.rem(place + step, ctx_size)
            return remote(
                grad_ref.at[:, pl.ds(pl.multiple_of(peer * rows, rows), rows)], slots.at[place],
                send.at[step], recv.at[step], {"ctx": peer},
            )

        def arrival(step):
            src = lax.rem(place + ctx_size - step, ctx_size)
            return remote(slots.at[src], slots.at[src], send.at[step], recv.at[step], {"ctx": src})

        def begin():
            for step in range(1, ctx_size):
                to(step).start()
            slots[place] = grad_ref[:, pl.ds(pl.multiple_of(place * rows, rows), rows)]

        def middle():
            pass

        def end():
            for step in range(1, ctx_size):
                arrival(step).wait_recv()
            total = slots[0].astype(F32)
            for z in range(1, ctx_size):
                total += slots[z].astype(F32)
            sum_ref[...] = total
            for step in range(1, ctx_size):
                to(step).wait_send()

        return begin, middle, end


class AttnTail:
    side = True

    def __init__(self, pre_slabs, norm_all, gain_second, out_rows, mesh_shape):
        self.ctx_size, self.tp_size = mesh_shape
        self.inputs = (pre_slabs, norm_all, gain_second, out_rows)
        self.wide, self.rows = pre_slabs.shape[1:]
        self.out_wide = out_rows.shape[0] // self.ctx_size
        self.half = norm_all.shape[1] // 2
        levels = self.tp_size // 2
        self.levels = levels
        self.outs = (
            jax.ShapeDtypeStruct((self.ctx_size * self.wide, self.half), BF16),
            jax.ShapeDtypeStruct((self.ctx_size * self.out_wide, self.half), BF16),
            jax.ShapeDtypeStruct((2, self.half), F32),
        )
        self.out_specs = (HBM_SPEC, HBM_SPEC, VMEM_SPEC)
        chips = max(levels - 1, 1)
        self.scratch = [
            pltpu.VMEM(pre_slabs.shape, BF16),
            pltpu.VMEM((self.wide, self.half), F32),
            pltpu.VMEM((self.wide, self.half), BF16),
            pltpu.VMEM((self.wide, self.half), BF16),
            pltpu.VMEM((self.wide, self.half), BF16),
            pltpu.VMEM((4, 2, self.half), F32),
            pltpu.VMEM((levels, 2, self.half), F32),
            pltpu.VMEM((self.ctx_size, 2, self.half), F32),
            DMA((self.ctx_size,)), DMA((self.ctx_size,)),
            DMA((6,)),
            DMA((chips,)), DMA((chips,)),
            DMA((self.ctx_size,)), DMA((self.ctx_size,)),
        ] + line_sems(self.ctx_size) + [
            pltpu.VMEM((self.ctx_size, self.out_wide, self.half), BF16),
            DMA((self.ctx_size,)), DMA((self.ctx_size,)),
            pltpu.VMEM((self.out_wide, self.half), BF16),
        ] + line_sems(self.ctx_size)

    def bind(self, in_refs, out_refs, side_refs, scratch):
        pre_ref, norm_ref, gain_second_ref, out_ref = in_refs
        all_ref, out_all_ref, gains_ref = out_refs
        slabs, own_half, far_half, from_far, quarter, swaps, by_level, by_place = scratch[:8]
        all_send, all_recv, duo, lev_send, lev_recv, ctx_send, ctx_recv = scratch[8:15]
        ctx_size, levels, half, rows = self.ctx_size, self.levels, self.half, self.rows
        place = lax.axis_index("ctx")
        _, _, level, partner, others = tp_peers(self.tp_size)
        far = {"fsdp": 1 - lax.axis_index("fsdp")}
        tile = min(512, half)
        line_begin, line_stage, line_drain = line_gather(quarter, all_ref, ctx_size, scratch[15:18])
        out_slots, out_send, out_recv, out_quarter = scratch[18:22]
        out_wide = self.out_wide
        out_begin, out_stage, out_drain = line_gather(
            out_quarter, out_all_ref, ctx_size, scratch[22:25]
        )

        def out_slab(step):
            peer = lax.rem(place + step, ctx_size)
            return remote(
                rows_at(out_ref, peer * out_wide, out_wide), out_slots.at[place],
                out_send.at[step], out_recv.at[step], {"ctx": peer},
            )

        def out_arrival(step):
            src = lax.rem(place + ctx_size - step, ctx_size)
            where = out_slots.at[src]
            return remote(where, where, out_send.at[step], out_recv.at[step], {"ctx": src})

        def slab(step):
            peer = lax.rem(place + step, ctx_size)
            return remote(
                pre_ref.at[peer], slabs.at[place], all_send.at[step], all_recv.at[step], {"ctx": peer}
            )

        def slab_arrival(step):
            src = lax.rem(place + ctx_size - step, ctx_size)
            return remote(
                slabs.at[src], slabs.at[src], all_send.at[step], all_recv.at[step], {"ctx": src}
            )

        grads = remote(far_half, from_far, duo.at[0], duo.at[1], far)
        gain_x = remote(swaps.at[0], swaps.at[1], duo.at[2], duo.at[3], far)
        gain_core = remote(swaps.at[2], swaps.at[3], duo.at[4], duo.at[5], {"tp": partner})

        def gain_level(index):
            return remote(
                by_level.at[level], by_level.at[level], lev_send.at[index],
                lev_recv.at[levels - 2 - index], {"tp": others[index]},
            )

        def gain_level_arrival(index):
            where = by_level.at[lax.rem(level + 1 + index, levels)]
            return remote(where, where, lev_send.at[index], lev_recv.at[index], {"tp": others[index]})

        def gain_place(step):
            peer = lax.rem(place + step, ctx_size)
            return remote(
                by_place.at[place], by_place.at[place], ctx_send.at[step], ctx_recv.at[step],
                {"ctx": peer},
            )

        def gain_place_arrival(step):
            src = lax.rem(place + ctx_size - step, ctx_size)
            where = by_place.at[src]
            return remote(where, where, ctx_send.at[step], ctx_recv.at[step], {"ctx": src})

        def product(at):
            columns = pl.ds(pl.multiple_of(at, tile), tile)
            total = jnp.dot(
                slabs[0], norm_ref[0:rows, columns], preferred_element_type=F32
            )
            for z in range(1, ctx_size):
                total += jnp.dot(
                    slabs[z], norm_ref[z * rows : (z + 1) * rows, columns],
                    preferred_element_type=F32,
                )
            return total

        def begin():
            for step in range(1, ctx_size):
                slab(step).start()
            slabs[place] = pre_ref[place]
            out_slots[place] = out_ref[pl.ds(pl.multiple_of(place * out_wide, out_wide), out_wide), :]

        def middle():
            for step in range(1, ctx_size):
                slab_arrival(step).wait_recv()
            for step in range(1, ctx_size):
                out_slab(step).start()

            @pl.loop(0, half // tile)
            def _(i):
                far_half[:, pl.ds(pl.multiple_of(i * tile, tile), tile)] = product(
                    half + i * tile
                ).astype(BF16)

            grads.start()

            @pl.loop(0, half // tile)
            def _(i):
                own_half[:, pl.ds(pl.multiple_of(i * tile, tile), tile)] = product(i * tile)

        def end():
            gain_first = side_refs[0]
            swaps[0, 0:1, :] = gain_first[:, half:]
            swaps[0, 1:2, :] = gain_second_ref[:, half:]
            gain_x.start()
            grads.wait_recv()
            quarter[...] = (own_half[...] + from_far[...].astype(F32)).astype(BF16)
            line_begin()
            gain_x.wait_recv()
            swaps[2, 0:1, :] = gain_first[:, :half] + swaps[1, 0:1, :]
            swaps[2, 1:2, :] = gain_second_ref[:, :half] + swaps[1, 1:2, :]
            gain_core.start()
            for step in range(1, ctx_size):
                out_arrival(step).wait_recv()
            total = out_slots[0].astype(F32)
            for z in range(1, ctx_size):
                total += out_slots[z].astype(F32)
            out_quarter[...] = total.astype(BF16)
            out_begin()
            gain_core.wait_recv()
            by_level[level] = swaps[2] + swaps[3]
            for index in range(levels - 1):
                gain_level(index).start()
            line_stage(1)
            for index in range(levels - 1):
                gain_level_arrival(index).wait_recv()
            total = by_level[0]
            for lev in range(1, levels):
                total += by_level[lev]
            by_place[place] = total
            for step in range(1, ctx_size):
                gain_place(step).start()
            out_stage(1)
            for step in range(2, ctx_size):
                line_stage(step)
                out_stage(step)
            for step in range(1, ctx_size):
                gain_place_arrival(step).wait_recv()
            total = by_place[0]
            for z in range(1, ctx_size):
                total += by_place[z]
            gains_ref[...] = total
            line_drain()
            out_drain()
            for step in range(1, ctx_size):
                slab(step).wait_send()
                out_slab(step).wait_send()
                gain_place(step).wait_send()
            for index in range(levels - 1):
                gain_level(index).wait_send()
            grads.wait_send()
            gain_x.wait_send()
            gain_core.wait_send()

        return begin, middle, end


def reduce_gather(term, extras, finish, side_shapes, mesh_shape, identity, blocks, across, aside=None):
    ctx_size, tp_size = mesh_shape
    levels = tp_size // 2
    width = term.shape[1]
    block_rows = term.shape[0] // blocks
    rows = block_rows // tp_size
    reach = ctx_size if across else 1
    beside = aside is not None
    aside_inputs = aside.inputs if beside else ()
    aside_outs = aside.outs if beside else ()
    aside_scratch = aside.scratch if beside else []

    def kernel(term_ref, *refs):
        extra_refs = refs[: len(extras)]
        refs = refs[len(extras) :]
        aside_in = refs[: len(aside_inputs)]
        refs = refs[len(aside_inputs) :]
        all_ref = refs[0]
        side_refs = refs[1 : 1 + len(side_shapes)]
        refs = refs[1 + len(side_shapes) :]
        aside_out = refs[: len(aside_outs)]
        refs = refs[len(aside_outs) :]
        from_core, stage, from_chip, mine = refs[:4]
        refs = refs[4:]
        if blocks == 2:
            pair_stage, from_pair = refs[:2]
            refs = refs[2:]
        sems = refs[:7]
        core_send, core_recv, chip_send, chip_recv, pair_sems = refs[7:12]
        place = lax.axis_index("ctx")
        me, core, level, partner, others = tp_peers(tp_size)
        enter(
            ctx_size, tp_size, along=across, pair=blocks == 2 and not beside,
            side=beside and aside.side, line=beside,
        )
        if beside:
            aside_begin, aside_middle, aside_end = aside.bind(
                aside_in, aside_out, side_refs, refs[12:]
            )
            aside_begin()

        def to_core(block, lev):
            slot = block * levels + lev
            return remote(
                rows_at(term_ref, block * block_rows + (2 * lev + 1 - core) * rows, rows),
                from_core.at[slot], core_send.at[slot], core_recv.at[slot], {"tp": partner},
            )

        def to_chip(index):
            return remote(
                stage.at[index], from_chip.at[levels - 2 - index], chip_send.at[index],
                chip_recv.at[levels - 2 - index], {"tp": others[index]},
            )

        def chip_sum(block, lev):
            own = term_ref[
                pl.ds(pl.multiple_of(block * block_rows + (2 * lev + core) * rows, rows), rows), :
            ]
            return own.astype(F32) + from_core[block * levels + lev].astype(F32)

        for lev in range(levels):
            for block in range(blocks):
                to_core(block, lev).start()
        for lev in range(levels):
            for block in range(blocks):
                to_core(block, lev).wait_recv()
        for index in range(levels - 1):
            lev = lax.rem(level + 1 + index, levels)
            for block in range(blocks):
                stage[index, block * rows : (block + 1) * rows, :] = chip_sum(block, lev).astype(
                    BF16
                )
            to_chip(index).start()
        if beside:
            aside_middle()
        for index in range(levels - 1):
            to_chip(index).wait_recv()

        def tp_sum(block):
            total = chip_sum(block, level)
            for index in range(levels - 1):
                total += from_chip[
                    index, pl.ds(pl.multiple_of(block * rows, rows), rows), :
                ].astype(F32)
            return total

        if blocks == 2:
            low = lax.rem(place, 2)
            pair_stage[...] = tp_sum(1 - low).astype(BF16)
            swap = remote(
                pair_stage, from_pair, pair_sems.at[0], pair_sems.at[1], {"ctx": place + 1 - 2 * low}
            )
            swap.start()
            total = tp_sum(low)
            swap.wait_recv()
            total += from_pair[...].astype(F32)
        else:
            total = tp_sum(0)
        start = pl.multiple_of(me * rows, rows)
        mine[...] = finish(total, start, *extra_refs, *side_refs)
        gather_rows(mine, all_ref, reach, tp_size, sems)
        if beside:
            aside_end()
        for lev in range(levels):
            for block in range(blocks):
                to_core(block, lev).wait_send()
        for index in range(levels - 1):
            to_chip(index).wait_send()
        if blocks == 2:
            swap.wait_send()

    chips = max(levels - 1, 1)
    scratch = [
        pltpu.VMEM((blocks * levels, rows, width), BF16),
        pltpu.VMEM((chips, blocks * rows, width), BF16),
        pltpu.VMEM((chips, blocks * rows, width), BF16),
        pltpu.VMEM((rows, width), BF16),
    ]
    if blocks == 2:
        scratch += [pltpu.VMEM((rows, width), BF16)] * 2
    scratch += gather_sems(reach, tp_size)
    scratch += [
        DMA((blocks * levels,)), DMA((blocks * levels,)), DMA((chips,)), DMA((chips,)), DMA((2,)),
    ]
    scratch += aside_scratch
    return pl.pallas_call(
        kernel,
        out_shape=(
            jax.ShapeDtypeStruct((reach * block_rows, width), BF16),
            *(jax.ShapeDtypeStruct(shape, F32) for shape in side_shapes),
            *aside_outs,
        ),
        in_specs=[VMEM_SPEC] * (1 + len(extras) + len(aside_inputs)),
        out_specs=(HBM_SPEC,) + (VMEM_SPEC,) * len(side_shapes)
        + (aside.out_specs if beside else ()),
        scratch_shapes=scratch,
        compiler_params=pltpu.CompilerParams(
            collective_id=identity, has_side_effects=True, vmem_limit_bytes=32 << 20
        ),
    )(term, *extras, *aside_inputs)


def unit_places(place):
    low = place % 2
    part = ((place + 1) // 2) % 2
    base = 2 + 3 * part
    return [base, low, base + 1, base + 2, 1 - low], part


def opening(cot_rows, groups, gains, hidden_weights, mesh_shape, identity):
    ctx_size, tp_size = mesh_shape
    block_rows, width = cot_rows.shape
    rows = block_rows // tp_size
    weights = [w for group in groups for w in group]
    depth = weights[0].shape[0]
    places = []
    for g, group in enumerate(groups):
        at = 0
        for w in group:
            places.append((g, at, w.shape[1]))
            at += w.shape[1]
    wholes = [
        jax.ShapeDtypeStruct((2 * depth, sum(w.shape[1] for w in group)), BF16) for group in groups
    ]

    unit = hidden_weights[0].shape[1] // 8
    kinds = len(hidden_weights)

    def kernel(cot_ref, *refs):
        weight_refs = refs[: len(weights)]
        gain_ref = refs[len(weights)]
        refs = refs[len(weights) + 1 :]
        hidden_refs = refs[:kinds]
        refs = refs[kinds:]
        all_ref, gain_far_ref = refs[:2]
        whole_refs = refs[2 : 2 + len(groups)]
        refs = refs[2 + len(groups) :]
        pack_refs = refs[:5]
        refs = refs[5:]
        sems = refs[:7]
        send, recv, pack_sems = refs[7:]
        units, _ = unit_places(lax.axis_index("ctx"))
        packs = [
            pltpu.make_async_copy(
                hidden_refs[k].at[:, pl.ds(pl.multiple_of(at * unit, unit), unit)],
                pack_refs[c].at[:, pl.ds(k * unit, unit)], pack_sems.at[c * kinds + k],
            )
            for c, at in enumerate(units) for k in range(kinds)
        ]
        enter(ctx_size, tp_size, along=True, side=True)
        far = {"fsdp": 1 - lax.axis_index("fsdp")}
        last = len(weights)
        swaps = [remote(gain_ref, gain_far_ref, send.at[last], recv.at[last], far)]
        for i, (g, at, wide) in enumerate(places):
            swaps.append(
                remote(
                    weight_refs[i], whole_refs[g].at[pl.ds(depth, depth), pl.ds(at, wide)],
                    send.at[i], recv.at[i], far,
                )
            )
        for swap in swaps:
            swap.start()
        for pack in packs:
            pack.start()
        for i, (g, at, wide) in enumerate(places):
            whole_refs[g][0:depth, at : at + wide] = weight_refs[i][...]
        mine = rows_at(cot_ref, lax.axis_index("tp") * rows, rows)
        gather_rows(mine, all_ref, ctx_size, tp_size, sems, block=cot_ref)
        for pack in packs:
            pack.wait()
        for swap in swaps:
            swap.wait()

    return pl.pallas_call(
        kernel,
        out_shape=(
            jax.ShapeDtypeStruct((ctx_size * block_rows, width), BF16),
            jax.ShapeDtypeStruct(gains.shape, F32),
            *wholes,
            *[jax.ShapeDtypeStruct((depth, kinds * unit), BF16)] * 5,
        ),
        in_specs=[VMEM_SPEC] * (2 + len(weights)) + [HBM_SPEC] * kinds,
        out_specs=(HBM_SPEC,) + (VMEM_SPEC,) * (6 + len(groups)),
        scratch_shapes=gather_sems(ctx_size, tp_size)
        + [DMA((len(weights) + 1,)), DMA((len(weights) + 1,)), DMA((5 * kinds,))],
        compiler_params=pltpu.CompilerParams(
            collective_id=identity, has_side_effects=True, vmem_limit_bytes=40 << 20
        ),
    )(cot_rows, *weights, gains, *hidden_weights)


def place_blocks(table, pieces, wide, blocks, base=None):
    count = len(pieces)
    depth = pieces[0][0].shape[0]
    tile = min(depth, 1024)

    def kernel(table_ref, *refs):
        out_ref = refs[-1]
        step = pl.program_id(1)
        for k in range(count):
            @pl.when(step == k)
            def _(k=k):
                out_ref[...] = refs[k][...].astype(F32)

    return pl.pallas_call(
        kernel,
        grid_spec=pltpu.PrefetchScalarGridSpec(
            num_scalar_prefetch=1,
            grid=(depth // tile, count),
            in_specs=[
                pl.BlockSpec((tile, wide), lambda i, step, table_ref, at=at: (i, at))
                for _, at in pieces
            ]
            + ([] if base is None else [HBM_SPEC]),
            out_specs=pl.BlockSpec((tile, wide), lambda i, step, table_ref: (i, table_ref[step])),
        ),
        out_shape=jax.ShapeDtypeStruct((depth, blocks * wide), F32),
        input_output_aliases={} if base is None else {1 + count: 0},
    )(table, *(array for array, _ in pieces), *(() if base is None else (base,)))


def transposed_grads(columns, widths, last):
    depth = columns.shape[1]
    tile = min(depth, 256)
    widths = list(widths) + [last.shape[0]]

    def kernel(in_ref, last_ref, *out_refs):
        head = in_ref[...].astype(F32).T
        at = 0
        for out_ref, wide in zip(out_refs[:-1], widths[:-1]):
            out_ref[...] = head[:, at : at + wide]
            at += wide
        out_refs[-1][...] = last_ref[...].astype(F32).T

    return pl.pallas_call(
        kernel,
        grid=(depth // tile,),
        in_specs=[
            pl.BlockSpec((array.shape[0], tile), lambda i: (0, i)) for array in (columns, last)
        ],
        out_specs=tuple(pl.BlockSpec((tile, wide), lambda i: (i, 0)) for wide in widths),
        out_shape=tuple(jax.ShapeDtypeStruct((depth, wide), F32) for wide in widths),
    )(columns, last)


def mean_square(rows):
    return jnp.mean(rows * rows, axis=-1, keepdims=True)


def finish_middle(total, start, resid_ref, gain_ref, middle_ref):
    rows = total.shape[0]
    middle = resid_ref[pl.ds(start, rows), :].astype(F32) + total
    middle_ref[...] = middle
    return (middle * lax.rsqrt(mean_square(middle) + EPSILON) * gain_ref[...]).astype(BF16)


def norm_back(grad, base, values, gain):
    rms = lax.rsqrt(mean_square(values) + EPSILON)
    scaled = grad * gain
    gain_grad = jnp.sum(grad * values * rms, axis=0, keepdims=True)
    cube = rms * rms * rms
    full = base + rms * scaled - values * cube * jnp.mean(scaled * values, axis=-1, keepdims=True)
    return full, gain_grad


def finish_grad_middle(total, start, middle_ref, cot_ref, gain_ref, grad_ref, gain_grad_ref):
    base = cot_ref[pl.ds(start, total.shape[0]), :].astype(F32)
    full, gain_grad = norm_back(total, base, middle_ref[...], gain_ref[...])
    grad_ref[...] = full
    gain_grad_ref[...] = gain_grad
    return full.astype(BF16)


def finish_grad_input(total, start, grad_ref, resid_ref, gain_ref, gain_grad_ref):
    values = resid_ref[pl.ds(start, total.shape[0]), :].astype(F32)
    full, gain_grad = norm_back(total, grad_ref[...], values, gain_ref[...])
    gain_grad_ref[...] = gain_grad
    return full.astype(BF16)


def finish_output(total, start, middle_ref):
    return (middle_ref[...] + total).astype(BF16)


def make_local(ctx_size, tp_size):
    mesh_shape = (ctx_size, tp_size)
    swap_x = [(0, 1), (1, 0)]
    swap_z = [(i, i ^ 1) for i in range(ctx_size)]

    def swap_rows(array):
        return lax.ppermute(array, "fsdp", swap_x)

    def local(
        inputs, cotangent, prefix, attn_gain, w_query, key_projection, value_projection, w_out,
        ffn_gain, w_gate, w_up, w_down,
    ):
        side = lax.axis_index("fsdp")
        place = lax.axis_index("ctx")
        units, part = unit_places(place)
        row_count, model_width = inputs.shape[1:]
        half_width = model_width // 2
        query_width = w_query.shape[1]
        key_width = key_projection.shape[1]
        ffn_width = w_gate.shape[1]
        unit = ffn_width // 8
        query_heads = query_width // HEAD_SIZE
        kv_heads = key_width // HEAD_SIZE
        row_start = place * row_count
        pair_start = (place // 2) * 2 * row_count

        def own_first(rows):
            a = lax.dynamic_slice_in_dim(rows, side * half_width, half_width, 1)
            b = lax.dynamic_slice_in_dim(rows, (1 - side) * half_width, half_width, 1)
            return jnp.concatenate([a, b], axis=1)

        gains = jnp.stack([attn_gain, ffn_gain]).astype(F32)
        residual_low = own_first(inputs[0])
        cot_low = own_first(cotangent[0])
        rows_all, gains_far, qkv_weight, out_weight, *owns = opening(
            jnp.concatenate([cot_low, residual_low], axis=1),
            ((w_query, jnp.concatenate([key_projection, value_projection], axis=1)), (w_out,)),
            gains, (w_gate, w_up, w_down), mesh_shape, 0,
        )
        cot_all = rows_all[:, :model_width]
        gains = jnp.concatenate([gains, gains_far], axis=1)
        gain_first, gain_second = gains[0], gains[1]
        others = [swap_rows(owns[0]), swap_rows(owns[1]), None, None, None]

        cosine_lookup, sine_lookup = (table.T for table in rope_tables(row_start, row_count))
        residual = residual_low.astype(F32)
        rms_first = lax.rsqrt(jnp.mean(residual * residual, axis=-1, keepdims=True) + EPSILON)
        normalized_rows = (residual * rms_first * gain_first).astype(BF16)
        qkv = contract(qkv_weight, normalized_rows, 0, 1)
        queries = apply_rotary(
            qkv[:query_width].reshape(query_heads, HEAD_SIZE, row_count),
            cosine_lookup, sine_lookup, 1.0,
        ).astype(BF16)
        key_rot = apply_rotary(
            qkv[query_width : query_width + key_width].reshape(kv_heads, HEAD_SIZE, row_count),
            cosine_lookup, sine_lookup, 1.0,
        ).astype(BF16)
        value_rows = qkv[query_width + key_width :].astype(BF16)
        kv_own = jnp.concatenate([key_rot, value_rows.reshape(kv_heads, HEAD_SIZE, row_count)], axis=0)
        kv_whole = lax.all_gather(
            kv_own.reshape(2 * key_width, row_count).T, "ctx", axis=0, tiled=True
        )
        length_total = kv_whole.shape[0]
        by_place = kv_whole.reshape(length_total, 2 * kv_heads, HEAD_SIZE).transpose(1, 0, 2)
        by_feature = kv_whole.T.reshape(2 * kv_heads, HEAD_SIZE, length_total)
        bounds = jnp.stack([prefix[0], row_start.astype(jnp.int32)])
        attended, log_total = attend(
            bounds, queries, by_place[:kv_heads], by_feature[kv_heads:]
        )
        attended_flat = attended.reshape(query_width, row_count)
        attn_term = contract(attended_flat, out_weight, 0, 1).astype(BF16)
        attn_term, owns[2], others[0] = lax.optimization_barrier((attn_term, owns[2], others[0]))
        others[2] = swap_rows(owns[2])
        slice_shape = (row_count // tp_size, model_width)
        normed_all, middle = reduce_gather(
            attn_term, (residual_low, gain_second[None]), finish_middle,
            (slice_shape,), mesh_shape, 1, 1, True,
        )

        ffn_term = 0.0
        mid_term = 0.0
        sides = []
        fars = []
        received = []

        def pair(rows):
            return lax.dynamic_slice_in_dim(rows, pair_start, 2 * row_count, 0)

        def outer(sides_of, part_of):
            return [contract(part_of(rows), cols, 0, 0) for rows, cols in sides_of]

        def near_of(c):
            return jnp.concatenate(outer(sides[c], lambda rows: rows[:, :half_width]), axis=1)

        def summed(c, near=None):
            near = near_of(c) if near is None else near
            return (near + received[c].astype(F32)).astype(BF16)

        def forward(c):
            both_w = jnp.concatenate([owns[c], others[c]], axis=0)
            pair_w, down_w = both_w[:, : 2 * unit], both_w[:, 2 * unit :]
            both = jnp.dot(normed_all, pair_w, preferred_element_type=F32)
            gating, upward = both[:, :unit], both[:, unit:]
            grad_hidden = jnp.dot(cot_all, down_w, preferred_element_type=F32)
            sigmoid_gate = jax.nn.sigmoid(gating)
            hidden = (gating * sigmoid_gate * upward).astype(BF16)
            grad_gating = (
                grad_hidden * upward * sigmoid_gate * (1.0 + gating * (1.0 - sigmoid_gate))
            ).astype(BF16)
            grad_upward = (grad_hidden * gating * sigmoid_gate).astype(BF16)
            grad_both = jnp.concatenate([grad_gating, grad_upward], axis=1)
            sides.append(((normed_all, grad_both), (cot_all, hidden)))
            far = outer(sides[c], lambda rows: rows[:, half_width:])
            fars.append(jnp.concatenate([f.astype(BF16) for f in far], axis=1))
            return pair_w, down_w, grad_both, hidden

        for c in range(4):
            if c:
                others[c], fars[-1] = lax.optimization_barrier((others[c], fars[-1]))
            if c == 1:
                owns[3], others[1] = lax.optimization_barrier((owns[3], others[1]))
                others[3] = swap_rows(owns[3])
                others[4] = lax.ppermute(others[1], "ctx", swap_z)
            if c == 3:
                others[3], others[4] = lax.optimization_barrier((others[3], others[4]))
            pair_w, down_w, grad_both, hidden = forward(c)
            ffn_term += contract(pair(hidden), down_w, 1, 1)
            mid_term += contract(pair(grad_both), pair_w, 1, 1)

        def swap_ctx(total):
            return lax.ppermute(total, "ctx", swap_z)

        received = {0: swap_rows(fars[0]), 2: swap_rows(fars[2])}
        totals, swapped = {}, {}
        mid_low, fars[1], fars[3], received[0] = lax.optimization_barrier(
            (mid_term.astype(BF16), fars[1], fars[3], received[0])
        )
        received[3] = swap_rows(fars[3])
        totals[0] = summed(0)
        mid_low, totals[0] = lax.optimization_barrier((mid_low, totals[0]))
        swapped[0] = swap_ctx(totals[0])
        branch_low, grad_middle, gain_grad_second = reduce_gather(
            mid_low, (middle, cot_low, gain_second[None]), finish_grad_middle,
            (slice_shape, (1, model_width)), mesh_shape, 2, 2, False,
        )
        branch_low, received[2], fars[1], swapped[0], rows_all = lax.optimization_barrier(
            (branch_low, received[2], fars[1], swapped[0], rows_all)
        )
        received[1] = swap_rows(fars[1])
        totals[2] = summed(2)
        near_one = near_of(1)
        residual_all = rows_all[:, model_width:].astype(F32)
        rms_all = lax.rsqrt(jnp.mean(residual_all * residual_all, axis=-1, keepdims=True) + EPSILON)
        norm_all = (residual_all * rms_all * gain_first).astype(BF16)
        branch_low, totals[2], near_one, norm_all = lax.optimization_barrier(
            (branch_low, totals[2], near_one, norm_all)
        )
        swapped[2] = swap_ctx(totals[2])
        grad_out = jnp.dot(attended_flat, branch_low, preferred_element_type=F32)
        grad_out_half = grad_out[:, half_width:].astype(BF16)
        grad_attended = contract(out_weight, branch_low, 0, 1).astype(BF16)
        grad_query_rot, grad_kv = attend_back(
            bounds, queries, by_place[:kv_heads], by_feature[:kv_heads], by_place[kv_heads:],
            grad_attended.reshape(query_heads, HEAD_SIZE, row_count), log_total,
        )
        grad_kv = grad_kv.reshape(2 * key_width, length_total)
        far_base = 2 + 3 * (1 - part)
        table = jnp.stack(units + [far_base, far_base + 1, far_base + 2])
        grad_kv, received[3] = lax.optimization_barrier((grad_kv, received[3]))
        totals[3] = summed(3)
        grad_kv, totals[3] = lax.optimization_barrier((grad_kv, totals[3]))
        swapped[3] = swap_ctx(totals[3])
        early = [totals[0], totals[2], totals[3], swapped[0]]
        placed = [
            place_blocks(
                jnp.stack([table[0], table[2], table[3], table[5]]),
                [(piece, block) for piece in early], unit, 8,
            )
            for block in range(3)
        ]
        others[4], placed, swapped[2], received[1], grad_out_half = lax.optimization_barrier(
            (others[4], placed, swapped[2], received[1], grad_out_half)
        )
        grad_out_far = swap_rows(grad_out_half)
        forward(4)
        near_four = near_of(4)
        totals[1] = summed(1, near_one)
        grad_kv, near_four, fars[4], totals[1] = lax.optimization_barrier(
            (grad_kv, near_four, fars[4], totals[1])
        )
        received[4] = swap_rows(fars[4])
        output_rows, grad_kv = reduce_gather(
            ffn_term.astype(BF16), (middle,), finish_output, (), mesh_shape, 3, 2, False,
            KvSum(grad_kv, ctx_size),
        )
        output_rows, grad_kv, swapped[3], grad_out_far = lax.optimization_barrier(
            (output_rows, grad_kv, swapped[3], grad_out_far)
        )
        grad_query_pre = apply_rotary(
            grad_query_rot, cosine_lookup, sine_lookup, -1.0
        ).astype(BF16).reshape(query_width, row_count)
        grad_key_pre = apply_rotary(
            grad_kv[:key_width].reshape(kv_heads, HEAD_SIZE, row_count),
            cosine_lookup, sine_lookup, -1.0,
        ).astype(BF16).reshape(key_width, row_count)
        grad_value_pre = grad_kv[key_width:].astype(BF16)
        grad_qkv_pre = jnp.concatenate([grad_query_pre, grad_key_pre, grad_value_pre], axis=0)
        attn_width = grad_qkv_pre.shape[0]
        pre_slabs = grad_qkv_pre.reshape(ctx_size, attn_width // ctx_size, row_count)
        normed_term = contract(grad_qkv_pre, qkv_weight, 0, 1).astype(BF16)
        grad_out_rows = (grad_out[:, :half_width] + grad_out_far.astype(F32)).astype(BF16)
        input_rows, _, grad_attn, grad_out, gain_grads = reduce_gather(
            normed_term,
            (grad_middle, residual_low, gain_first[None]), finish_grad_input,
            ((1, model_width),), mesh_shape, 4, 1, False,
            AttnTail(pre_slabs, norm_all, gain_grad_second, grad_out_rows, mesh_shape),
        )
        grad_attn, received[4] = lax.optimization_barrier((grad_attn, received[4]))
        grad_query, grad_key, grad_value, grad_out = transposed_grads(
            grad_attn, (query_width, key_width, key_width), grad_out
        )
        totals[4] = summed(4, near_four)

        def result(block):
            pieces = [(piece, block) for piece in (totals[1], totals[4], swapped[2], swapped[3])]
            late = jnp.stack([table[1], table[4], table[6], table[7]])
            return place_blocks(late, pieces, unit, 8, placed[block])

        return (
            own_first(output_rows)[None],
            own_first(input_rows)[None],
            gain_grads[0],
            grad_query,
            grad_key,
            grad_value,
            grad_out,
            gain_grads[1],
            result(0),
            result(1),
            result(2),
        )

    return local


def solution(mesh):
    return jax.shard_map(
        make_local(mesh.shape["ctx"], mesh.shape["tp"]),
        mesh=mesh,
        in_specs=(
            P("fsdp", "ctx", None), P("fsdp", "ctx", None), P("fsdp"), P("fsdp"),
            P("fsdp", "tp"), P("fsdp", "tp"), P("fsdp", "tp"), P("fsdp", "tp"),
            P("fsdp"), P("fsdp", "tp"), P("fsdp", "tp"), P("fsdp", "tp"),
        ),
        out_specs=(
            P("fsdp", "ctx", None), P("fsdp", "ctx", None), P("fsdp"), P("fsdp", "tp"),
            P("fsdp", "tp"), P("fsdp", "tp"), P("fsdp", "tp"), P("fsdp"),
            P("fsdp", "tp"), P("fsdp", "tp"), P("fsdp", "tp"),
        ),
        check_vma=False,
    )
```

```python
import math

import jax
import jax.numpy as jnp
from jax import lax
from jax.experimental import pallas as pl
from jax.experimental.pallas import tpu as pltpu
from jax.sharding import PartitionSpec as P

HEAD_SIZE = 64
EPSILON = 1e-05
THETA = 500000.0
MASKED = -1e30
F32 = jnp.float32
BF16 = jnp.bfloat16


def contract(left, right, left_dim, right_dim):
    return lax.dot_general(
        left, right, (((left_dim,), (right_dim,)), ((), ())), preferred_element_type=F32
    )


def rope_tables(row_start, row_count):
    position = (row_start + jnp.arange(row_count, dtype=jnp.int32)).astype(F32)
    exponent = jnp.arange(HEAD_SIZE // 2, dtype=jnp.int32).astype(F32) * (2.0 / HEAD_SIZE)
    angles = position[:, None] * jnp.power(THETA, -exponent)[None, :]
    return (jnp.cos(angles), jnp.sin(angles))


def apply_rotary(values, cosine_lookup, sine_lookup, direction):
    half_width = values.shape[1] // 2
    leading = values[:, :half_width]
    trailing = values[:, half_width:]
    sin = direction * sine_lookup
    return jnp.concatenate(
        [leading * cosine_lookup - trailing * sin, trailing * cosine_lookup + leading * sin],
        axis=1,
    )


def allowed_pairs(bounds_ref, shape):
    key_place = lax.broadcasted_iota(jnp.int32, shape, 0)
    query_place = bounds_ref[1] + lax.broadcasted_iota(jnp.int32, shape, 1)
    return (key_place <= query_place) | (key_place < bounds_ref[0])


SCORE_SCALE = 1.0 / math.sqrt(HEAD_SIZE)
SMEM_SPEC = pl.BlockSpec(memory_space=pltpu.SMEM)


def attend(bounds, queries, keys, values_flat):
    heads, _, rows = queries.shape
    places = keys.shape[1]
    group = heads // keys.shape[0]

    def kernel(bounds_ref, query_ref, key_ref, value_ref, out_ref, log_ref):
        @pl.loop(0, heads)
        def _(h):
            k = h // group
            scores = jnp.dot(key_ref[k], query_ref[h], preferred_element_type=F32) * SCORE_SCALE
            scores = jnp.where(allowed_pairs(bounds_ref, (places, rows)), scores, MASKED)
            peak = jnp.max(scores, axis=0, keepdims=True)
            weights = jnp.exp(scores - peak)
            total = jnp.sum(weights, axis=0, keepdims=True)
            probabilities = (weights * (1.0 / total)).astype(BF16)
            out_ref[h] = jnp.dot(
                value_ref[k], probabilities, preferred_element_type=F32
            ).astype(BF16)
            log_ref[h] = peak + jnp.log(total)

    return pl.pallas_call(
        kernel,
        out_shape=(
            jax.ShapeDtypeStruct(queries.shape, BF16),
            jax.ShapeDtypeStruct((heads, 1, rows), F32),
        ),
        in_specs=[SMEM_SPEC] + [pl.BlockSpec(memory_space=pltpu.VMEM)] * 3,
        out_specs=(pl.BlockSpec(memory_space=pltpu.VMEM),) * 2,
        compiler_params=pltpu.CompilerParams(vmem_limit_bytes=24 << 20),
    )(bounds, queries, keys, values_flat)


def attend_back(bounds, queries, keys, keys_flat, values, grads, log_total):
    heads, size, rows = queries.shape
    key_heads, places, _ = keys.shape
    group = heads // key_heads

    def kernel(
        bounds_ref, query_ref, key_ref, key_flat_ref, value_ref, grad_ref, log_ref, query_grad_ref,
        both_grad_ref, totals,
    ):
        totals[...] = jnp.zeros_like(totals)

        @pl.loop(0, heads)
        def _(h):
            k = h // group
            scores = jnp.dot(key_ref[k], query_ref[h], preferred_element_type=F32) * SCORE_SCALE
            scores = jnp.where(allowed_pairs(bounds_ref, (places, rows)), scores, MASKED)
            probabilities = jnp.exp(scores - log_ref[h])
            grad_probs = jnp.dot(value_ref[k], grad_ref[h], preferred_element_type=F32)
            delta = jnp.sum(probabilities * grad_probs, axis=0, keepdims=True)
            grad_scores = (probabilities * (grad_probs - delta)).astype(BF16)
            query_grad_ref[h] = SCORE_SCALE * jnp.dot(
                key_flat_ref[k], grad_scores, preferred_element_type=F32
            )
            totals[k] += SCORE_SCALE * contract(query_ref[h], grad_scores, 1, 1)
            totals[key_heads + k] += contract(grad_ref[h], probabilities.astype(BF16), 1, 1)

        both_grad_ref[...] = totals[...].astype(BF16)

    return pl.pallas_call(
        kernel,
        out_shape=(
            jax.ShapeDtypeStruct(queries.shape, F32),
            jax.ShapeDtypeStruct((2 * key_heads, size, places), BF16),
        ),
        in_specs=[SMEM_SPEC] + [pl.BlockSpec(memory_space=pltpu.VMEM)] * 6,
        out_specs=(pl.BlockSpec(memory_space=pltpu.VMEM),) * 2,
        scratch_shapes=[pltpu.VMEM((2 * key_heads, size, places), F32)],
        compiler_params=pltpu.CompilerParams(vmem_limit_bytes=32 << 20),
    )(bounds, queries, keys, keys_flat, values, grads, log_total)


MESH = pl.DeviceIdType.MESH
HBM_SPEC = pl.BlockSpec(memory_space=pl.ANY)
VMEM_SPEC = pl.BlockSpec(memory_space=pltpu.VMEM)
DMA = pltpu.SemaphoreType.DMA


def remote(src, dst, send, recv, peer):
    return pltpu.make_async_remote_copy(
        src_ref=src, dst_ref=dst, send_sem=send, recv_sem=recv, device_id=peer, device_id_type=MESH
    )


def rows_at(ref, start, count):
    return ref.at[pl.ds(pl.multiple_of(start, count), count)]


def guarded(condition, body):
    if condition is None:
        body()
    else:
        pl.when(condition)(body)


def tp_peers(tp_size):
    me = lax.axis_index("tp")
    core = lax.rem(me, 2)
    level = me // 2
    levels = tp_size // 2
    partner = me + 1 - 2 * core
    others = [lax.rem(level + step, levels) * 2 + core for step in range(1, levels)]
    return me, core, level, partner, others


def enter(ctx_size, tp_size, along=False, pair=False, side=False, tensor=True, line=False):
    place = lax.axis_index("ctx")
    barrier = pltpu.get_barrier_semaphore()

    def greet(peer):
        pl.semaphore_signal(barrier, inc=1, device_id=peer, device_id_type=MESH)

    count = 0
    if tensor:
        _, _, _, partner, others = tp_peers(tp_size)
        for peer in [partner] + others:
            greet({"tp": peer})
        count = count + 1 + len(others)
    if side:
        greet({"fsdp": 1 - lax.axis_index("fsdp")})
        count = count + 1
    if along:
        up = place + 1 < ctx_size
        down = place > 0

        @pl.when(up)
        def _():
            greet({"ctx": place + 1})

        @pl.when(down)
        def _():
            greet({"ctx": place - 1})

        count = count + up.astype(jnp.int32) + down.astype(jnp.int32)
    if pair:
        greet({"ctx": place + 1 - 2 * lax.rem(place, 2)})
        count = count + 1
    if line:
        for step in range(1, ctx_size):
            greet({"ctx": lax.rem(place + step, ctx_size)})
        count = count + ctx_size - 1
    pl.semaphore_wait(barrier, count)


def gather_sems(ctx_size, tp_size):
    spread = 2 * ctx_size - 1
    levels = tp_size // 2
    chips = max(levels - 1, 1)
    return [
        DMA((spread + 1,)), DMA((spread,)), DMA((chips, spread)), DMA((chips, spread)),
        DMA((levels, spread)), DMA((levels, spread)), DMA((1,)),
    ]


def gather_rows(mine, all_ref, ctx_size, tp_size, sems, block=None):
    hop_send, hop_recv, chip_send, chip_recv, core_send, core_recv, own_sem = sems
    place = lax.axis_index("ctx") if ctx_size > 1 else 0
    me, core, level, partner, others = tp_peers(tp_size)
    levels = tp_size // 2
    rows = mine.shape[0]
    middle = ctx_size - 1
    offsets = [0]
    for step in range(1, ctx_size):
        offsets += [-step, step]

    def spot(offset, who):
        return rows_at(all_ref, ((place + offset) * tp_size + who) * rows, rows)

    def hop(offset, step, src):
        slot = 2 * middle + 1 if offset == 0 and step < 0 else middle + offset
        return remote(
            src, spot(offset, me), hop_send.at[slot], hop_recv.at[middle + offset - step],
            {"ctx": place + step},
        )

    def hop_arrival(offset):
        step = -1 if offset < 0 else 1
        return remote(
            spot(offset, me), spot(offset, me), hop_send.at[middle + offset],
            hop_recv.at[middle + offset], {"ctx": place + step},
        )

    def chip(offset, index, src):
        return remote(
            src, spot(offset, me), chip_send.at[index, middle + offset],
            chip_recv.at[levels - 2 - index, middle + offset], {"tp": others[index]},
        )

    def chip_arrival(offset, index):
        where = spot(offset, others[index])
        return remote(
            where, where, chip_send.at[index, middle + offset],
            chip_recv.at[index, middle + offset], {"tp": others[index]},
        )

    def to_core(offset, index, who, src):
        return remote(
            src, spot(offset, who), core_send.at[index, middle + offset],
            core_recv.at[index, middle + offset], {"tp": partner},
        )

    def valid(offset):
        if offset == 0:
            return None
        return place + offset >= 0 if offset < 0 else place + offset < ctx_size

    def onward(offset):
        if offset < 0:
            return 1, jnp.logical_and(place + offset >= 0, place + 1 < ctx_size)
        return -1, jnp.logical_and(place + offset < ctx_size, place > 0)

    def fan_out(offset, src):
        for index in range(levels - 1):
            chip(offset, index, src).start()
        to_core(offset, 0, me, src).start()

    if block is None:
        own = pltpu.make_async_copy(mine, spot(0, me), own_sem.at[0])
    else:
        own = pltpu.make_async_copy(
            block, rows_at(all_ref, place * block.shape[0], block.shape[0]), own_sem.at[0]
        )
    own.start()
    if ctx_size > 1:
        @pl.when(place + 1 < ctx_size)
        def _():
            hop(0, 1, mine).start()

        @pl.when(place > 0)
        def _():
            hop(0, -1, mine).start()

    if block is None:
        fan_out(0, mine)
    for offset in offsets[1:]:
        def arrived(offset=offset):
            hop_arrival(offset).wait_recv()
            fan_out(offset, spot(offset, me))

        guarded(valid(offset), arrived)
        step, more = onward(offset)

        @pl.when(more)
        def _(offset=offset, step=step):
            hop(offset, step, spot(offset, me)).start()

    shared = offsets if block is None else offsets[1:]
    for offset in shared:
        def relay(offset=offset):
            for index in range(levels - 1):
                chip_arrival(offset, index).wait_recv()
                to_core(offset, 1 + index, others[index], spot(offset, others[index])).start()

        guarded(valid(offset), relay)

    for offset in shared:
        def drain(offset=offset):
            for index in range(levels):
                to_core(offset, index, me, spot(offset, me)).wait()
            for index in range(levels - 1):
                chip(offset, index, spot(offset, me)).wait_send()

        guarded(valid(offset), drain)
    own.wait()
    if ctx_size > 1:
        @pl.when(place + 1 < ctx_size)
        def _():
            hop(0, 1, mine).wait_send()

        @pl.when(place > 0)
        def _():
            hop(0, -1, mine).wait_send()

        for offset in offsets[1:]:
            step, more = onward(offset)

            @pl.when(more)
            def _(offset=offset, step=step):
                hop(offset, step, spot(offset, me)).wait_send()


def line_sems(ctx_size):
    spread = 2 * ctx_size - 1
    return [DMA((spread + 1,)), DMA((spread,)), DMA((1,))]


def line_gather(mine, all_ref, ctx_size, sems):
    hop_send, hop_recv, own_sem = sems
    place = lax.axis_index("ctx")
    rows = mine.shape[0]
    middle = ctx_size - 1
    offsets = [o for step in range(1, ctx_size) for o in (-step, step)]

    def spot(offset):
        return rows_at(all_ref, (place + offset) * rows, rows)

    def hop(offset, step, src):
        slot = 2 * middle + 1 if offset == 0 and step < 0 else middle + offset
        return remote(
            src, spot(offset), hop_send.at[slot], hop_recv.at[middle + offset - step],
            {"ctx": place + step},
        )

    def arrival(offset):
        step = -1 if offset < 0 else 1
        return remote(
            spot(offset), spot(offset), hop_send.at[middle + offset],
            hop_recv.at[middle + offset], {"ctx": place + step},
        )

    def valid(offset):
        return place + offset >= 0 if offset < 0 else place + offset < ctx_size

    def onward(offset):
        if offset < 0:
            return 1, jnp.logical_and(place + offset >= 0, place + 1 < ctx_size)
        return -1, jnp.logical_and(place + offset < ctx_size, place > 0)

    own = pltpu.make_async_copy(mine, spot(0), own_sem.at[0])
    ends = ((1, place + 1 < ctx_size), (-1, place > 0))

    def begin():
        for step, there in ends:
            @pl.when(there)
            def _(step=step):
                hop(0, step, mine).start()

        own.start()

    def stage(step):
        for offset in (-step, step):
            @pl.when(valid(offset))
            def _(offset=offset):
                arrival(offset).wait_recv()

            way, more = onward(offset)

            @pl.when(more)
            def _(offset=offset, way=way):
                hop(offset, way, spot(offset)).start()

    def drain():
        own.wait()
        for step, there in ends:
            @pl.when(there)
            def _(step=step):
                hop(0, step, mine).wait_send()

        for offset in offsets:
            step, more = onward(offset)

            @pl.when(more)
            def _(offset=offset, step=step):
                hop(offset, step, spot(offset)).wait_send()

    return begin, stage, drain


class KvSum:
    side = False

    def __init__(self, grad_kv, ctx_size):
        self.ctx_size = ctx_size
        self.inputs = (grad_kv,)
        self.rows = grad_kv.shape[1] // ctx_size
        self.block = (grad_kv.shape[0], self.rows)
        self.outs = (jax.ShapeDtypeStruct(self.block, F32),)
        self.out_specs = (VMEM_SPEC,)
        self.scratch = [
            pltpu.VMEM((ctx_size, *self.block), BF16), DMA((ctx_size,)), DMA((ctx_size,)),
        ]

    def bind(self, in_refs, out_refs, side_refs, scratch):
        (grad_ref,) = in_refs
        (sum_ref,) = out_refs
        slots, send, recv = scratch
        ctx_size, rows = self.ctx_size, self.rows
        place = lax.axis_index("ctx")

        def to(step):
            peer = lax.rem(place + step, ctx_size)
            return remote(
                grad_ref.at[:, pl.ds(pl.multiple_of(peer * rows, rows), rows)], slots.at[place],
                send.at[step], recv.at[step], {"ctx": peer},
            )

        def arrival(step):
            src = lax.rem(place + ctx_size - step, ctx_size)
            return remote(slots.at[src], slots.at[src], send.at[step], recv.at[step], {"ctx": src})

        def begin():
            for step in range(1, ctx_size):
                to(step).start()
            slots[place] = grad_ref[:, pl.ds(pl.multiple_of(place * rows, rows), rows)]

        def middle():
            pass

        def end():
            for step in range(1, ctx_size):
                arrival(step).wait_recv()
            total = slots[0].astype(F32)
            for z in range(1, ctx_size):
                total += slots[z].astype(F32)
            sum_ref[...] = total
            for step in range(1, ctx_size):
                to(step).wait_send()

        return begin, middle, end


class AttnTail:
    side = True

    def __init__(self, pre_slabs, norm_all, gain_second, out_rows, mesh_shape):
        self.ctx_size, self.tp_size = mesh_shape
        self.inputs = (pre_slabs, norm_all, gain_second, out_rows)
        self.wide, self.rows = pre_slabs.shape[1:]
        self.out_wide = out_rows.shape[0] // self.ctx_size
        self.half = norm_all.shape[1] // 2
        levels = self.tp_size // 2
        self.levels = levels
        self.outs = (
            jax.ShapeDtypeStruct((self.ctx_size * self.wide, self.half), BF16),
            jax.ShapeDtypeStruct((self.ctx_size * self.out_wide, self.half), BF16),
            jax.ShapeDtypeStruct((2, self.half), F32),
        )
        self.out_specs = (HBM_SPEC, HBM_SPEC, VMEM_SPEC)
        chips = max(levels - 1, 1)
        self.scratch = [
            pltpu.VMEM(pre_slabs.shape, BF16),
            pltpu.VMEM((self.wide, self.half), F32),
            pltpu.VMEM((self.wide, self.half), BF16),
            pltpu.VMEM((self.wide, self.half), BF16),
            pltpu.VMEM((self.wide, self.half), BF16),
            pltpu.VMEM((4, 2, self.half), F32),
            pltpu.VMEM((levels, 2, self.half), F32),
            pltpu.VMEM((self.ctx_size, 2, self.half), F32),
            DMA((self.ctx_size,)), DMA((self.ctx_size,)),
            DMA((6,)),
            DMA((chips,)), DMA((chips,)),
            DMA((self.ctx_size,)), DMA((self.ctx_size,)),
        ] + line_sems(self.ctx_size) + [
            pltpu.VMEM((self.ctx_size, self.out_wide, self.half), BF16),
            DMA((self.ctx_size,)), DMA((self.ctx_size,)),
            pltpu.VMEM((self.out_wide, self.half), BF16),
        ] + line_sems(self.ctx_size)

    def bind(self, in_refs, out_refs, side_refs, scratch):
        pre_ref, norm_ref, gain_second_ref, out_ref = in_refs
        all_ref, out_all_ref, gains_ref = out_refs
        slabs, own_half, far_half, from_far, quarter, swaps, by_level, by_place = scratch[:8]
        all_send, all_recv, duo, lev_send, lev_recv, ctx_send, ctx_recv = scratch[8:15]
        ctx_size, levels, half, rows = self.ctx_size, self.levels, self.half, self.rows
        place = lax.axis_index("ctx")
        _, _, level, partner, others = tp_peers(self.tp_size)
        far = {"fsdp": 1 - lax.axis_index("fsdp")}
        tile = min(512, half)
        line_begin, line_stage, line_drain = line_gather(quarter, all_ref, ctx_size, scratch[15:18])
        out_slots, out_send, out_recv, out_quarter = scratch[18:22]
        out_wide = self.out_wide
        out_begin, out_stage, out_drain = line_gather(
            out_quarter, out_all_ref, ctx_size, scratch[22:25]
        )

        def out_slab(step):
            peer = lax.rem(place + step, ctx_size)
            return remote(
                rows_at(out_ref, peer * out_wide, out_wide), out_slots.at[place],
                out_send.at[step], out_recv.at[step], {"ctx": peer},
            )

        def out_arrival(step):
            src = lax.rem(place + ctx_size - step, ctx_size)
            where = out_slots.at[src]
            return remote(where, where, out_send.at[step], out_recv.at[step], {"ctx": src})

        def slab(step):
            peer = lax.rem(place + step, ctx_size)
            return remote(
                pre_ref.at[peer], slabs.at[place], all_send.at[step], all_recv.at[step], {"ctx": peer}
            )

        def slab_arrival(step):
            src = lax.rem(place + ctx_size - step, ctx_size)
            return remote(
                slabs.at[src], slabs.at[src], all_send.at[step], all_recv.at[step], {"ctx": src}
            )

        grads = remote(far_half, from_far, duo.at[0], duo.at[1], far)
        gain_x = remote(swaps.at[0], swaps.at[1], duo.at[2], duo.at[3], far)
        gain_core = remote(swaps.at[2], swaps.at[3], duo.at[4], duo.at[5], {"tp": partner})

        def gain_level(index):
            return remote(
                by_level.at[level], by_level.at[level], lev_send.at[index],
                lev_recv.at[levels - 2 - index], {"tp": others[index]},
            )

        def gain_level_arrival(index):
            where = by_level.at[lax.rem(level + 1 + index, levels)]
            return remote(where, where, lev_send.at[index], lev_recv.at[index], {"tp": others[index]})

        def gain_place(step):
            peer = lax.rem(place + step, ctx_size)
            return remote(
                by_place.at[place], by_place.at[place], ctx_send.at[step], ctx_recv.at[step],
                {"ctx": peer},
            )

        def gain_place_arrival(step):
            src = lax.rem(place + ctx_size - step, ctx_size)
            where = by_place.at[src]
            return remote(where, where, ctx_send.at[step], ctx_recv.at[step], {"ctx": src})

        def product(at):
            columns = pl.ds(pl.multiple_of(at, tile), tile)
            total = jnp.dot(
                slabs[0], norm_ref[0:rows, columns], preferred_element_type=F32
            )
            for z in range(1, ctx_size):
                total += jnp.dot(
                    slabs[z], norm_ref[z * rows : (z + 1) * rows, columns],
                    preferred_element_type=F32,
                )
            return total

        def begin():
            for step in range(1, ctx_size):
                slab(step).start()
            slabs[place] = pre_ref[place]
            out_slots[place] = out_ref[pl.ds(pl.multiple_of(place * out_wide, out_wide), out_wide), :]

        def middle():
            for step in range(1, ctx_size):
                slab_arrival(step).wait_recv()
            for step in range(1, ctx_size):
                out_slab(step).start()

            @pl.loop(0, half // tile)
            def _(i):
                far_half[:, pl.ds(pl.multiple_of(i * tile, tile), tile)] = product(
                    half + i * tile
                ).astype(BF16)

            grads.start()

            @pl.loop(0, half // tile)
            def _(i):
                own_half[:, pl.ds(pl.multiple_of(i * tile, tile), tile)] = product(i * tile)

        def end():
            gain_first = side_refs[0]
            swaps[0, 0:1, :] = gain_first[:, half:]
            swaps[0, 1:2, :] = gain_second_ref[:, half:]
            gain_x.start()
            grads.wait_recv()
            quarter[...] = (own_half[...] + from_far[...].astype(F32)).astype(BF16)
            line_begin()
            gain_x.wait_recv()
            swaps[2, 0:1, :] = gain_first[:, :half] + swaps[1, 0:1, :]
            swaps[2, 1:2, :] = gain_second_ref[:, :half] + swaps[1, 1:2, :]
            gain_core.start()
            for step in range(1, ctx_size):
                out_arrival(step).wait_recv()
            total = out_slots[0].astype(F32)
            for z in range(1, ctx_size):
                total += out_slots[z].astype(F32)
            out_quarter[...] = total.astype(BF16)
            out_begin()
            gain_core.wait_recv()
            by_level[level] = swaps[2] + swaps[3]
            for index in range(levels - 1):
                gain_level(index).start()
            line_stage(1)
            for index in range(levels - 1):
                gain_level_arrival(index).wait_recv()
            total = by_level[0]
            for lev in range(1, levels):
                total += by_level[lev]
            by_place[place] = total
            for step in range(1, ctx_size):
                gain_place(step).start()
            out_stage(1)
            for step in range(2, ctx_size):
                line_stage(step)
                out_stage(step)
            for step in range(1, ctx_size):
                gain_place_arrival(step).wait_recv()
            total = by_place[0]
            for z in range(1, ctx_size):
                total += by_place[z]
            gains_ref[...] = total
            line_drain()
            out_drain()
            for step in range(1, ctx_size):
                slab(step).wait_send()
                out_slab(step).wait_send()
                gain_place(step).wait_send()
            for index in range(levels - 1):
                gain_level(index).wait_send()
            grads.wait_send()
            gain_x.wait_send()
            gain_core.wait_send()

        return begin, middle, end


def reduce_gather(term, extras, finish, side_shapes, mesh_shape, identity, blocks, across, aside=None):
    ctx_size, tp_size = mesh_shape
    levels = tp_size // 2
    width = term.shape[1]
    block_rows = term.shape[0] // blocks
    rows = block_rows // tp_size
    reach = ctx_size if across else 1
    beside = aside is not None
    aside_inputs = aside.inputs if beside else ()
    aside_outs = aside.outs if beside else ()
    aside_scratch = aside.scratch if beside else []

    def kernel(term_ref, *refs):
        extra_refs = refs[: len(extras)]
        refs = refs[len(extras) :]
        aside_in = refs[: len(aside_inputs)]
        refs = refs[len(aside_inputs) :]
        all_ref = refs[0]
        side_refs = refs[1 : 1 + len(side_shapes)]
        refs = refs[1 + len(side_shapes) :]
        aside_out = refs[: len(aside_outs)]
        refs = refs[len(aside_outs) :]
        from_core, stage, from_chip, mine = refs[:4]
        refs = refs[4:]
        if blocks == 2:
            pair_stage, from_pair = refs[:2]
            refs = refs[2:]
        sems = refs[:7]
        core_send, core_recv, chip_send, chip_recv, pair_sems = refs[7:12]
        place = lax.axis_index("ctx")
        me, core, level, partner, others = tp_peers(tp_size)
        enter(
            ctx_size, tp_size, along=across, pair=blocks == 2 and not beside,
            side=beside and aside.side, line=beside,
        )
        if beside:
            aside_begin, aside_middle, aside_end = aside.bind(
                aside_in, aside_out, side_refs, refs[12:]
            )
            aside_begin()

        def to_core(block, lev):
            slot = block * levels + lev
            return remote(
                rows_at(term_ref, block * block_rows + (2 * lev + 1 - core) * rows, rows),
                from_core.at[slot], core_send.at[slot], core_recv.at[slot], {"tp": partner},
            )

        def to_chip(index):
            return remote(
                stage.at[index], from_chip.at[levels - 2 - index], chip_send.at[index],
                chip_recv.at[levels - 2 - index], {"tp": others[index]},
            )

        def chip_sum(block, lev):
            own = term_ref[
                pl.ds(pl.multiple_of(block * block_rows + (2 * lev + core) * rows, rows), rows), :
            ]
            return own.astype(F32) + from_core[block * levels + lev].astype(F32)

        for lev in range(levels):
            for block in range(blocks):
                to_core(block, lev).start()
        for lev in range(levels):
            for block in range(blocks):
                to_core(block, lev).wait_recv()
        for index in range(levels - 1):
            lev = lax.rem(level + 1 + index, levels)
            for block in range(blocks):
                stage[index, block * rows : (block + 1) * rows, :] = chip_sum(block, lev).astype(
                    BF16
                )
            to_chip(index).start()
        if beside:
            aside_middle()
        for index in range(levels - 1):
            to_chip(index).wait_recv()

        def tp_sum(block):
            total = chip_sum(block, level)
            for index in range(levels - 1):
                total += from_chip[
                    index, pl.ds(pl.multiple_of(block * rows, rows), rows), :
                ].astype(F32)
            return total

        if blocks == 2:
            low = lax.rem(place, 2)
            pair_stage[...] = tp_sum(1 - low).astype(BF16)
            swap = remote(
                pair_stage, from_pair, pair_sems.at[0], pair_sems.at[1], {"ctx": place + 1 - 2 * low}
            )
            swap.start()
            total = tp_sum(low)
            swap.wait_recv()
            total += from_pair[...].astype(F32)
        else:
            total = tp_sum(0)
        start = pl.multiple_of(me * rows, rows)
        mine[...] = finish(total, start, *extra_refs, *side_refs)
        gather_rows(mine, all_ref, reach, tp_size, sems)
        if beside:
            aside_end()
        for lev in range(levels):
            for block in range(blocks):
                to_core(block, lev).wait_send()
        for index in range(levels - 1):
            to_chip(index).wait_send()
        if blocks == 2:
            swap.wait_send()

    chips = max(levels - 1, 1)
    scratch = [
        pltpu.VMEM((blocks * levels, rows, width), BF16),
        pltpu.VMEM((chips, blocks * rows, width), BF16),
        pltpu.VMEM((chips, blocks * rows, width), BF16),
        pltpu.VMEM((rows, width), BF16),
    ]
    if blocks == 2:
        scratch += [pltpu.VMEM((rows, width), BF16)] * 2
    scratch += gather_sems(reach, tp_size)
    scratch += [
        DMA((blocks * levels,)), DMA((blocks * levels,)), DMA((chips,)), DMA((chips,)), DMA((2,)),
    ]
    scratch += aside_scratch
    return pl.pallas_call(
        kernel,
        out_shape=(
            jax.ShapeDtypeStruct((reach * block_rows, width), BF16),
            *(jax.ShapeDtypeStruct(shape, F32) for shape in side_shapes),
            *aside_outs,
        ),
        in_specs=[VMEM_SPEC] * (1 + len(extras) + len(aside_inputs)),
        out_specs=(HBM_SPEC,) + (VMEM_SPEC,) * len(side_shapes)
        + (aside.out_specs if beside else ()),
        scratch_shapes=scratch,
        compiler_params=pltpu.CompilerParams(
            collective_id=identity, has_side_effects=True, vmem_limit_bytes=32 << 20
        ),
    )(term, *extras, *aside_inputs)


def unit_places(place):
    low = place % 2
    part = ((place + 1) // 2) % 2
    base = 2 + 3 * part
    return [base, low, base + 1, base + 2, 1 - low], part


def opening(cot_rows, groups, gains, hidden_weights, mesh_shape, identity):
    ctx_size, tp_size = mesh_shape
    block_rows, width = cot_rows.shape
    rows = block_rows // tp_size
    weights = [w for group in groups for w in group]
    depth = weights[0].shape[0]
    places = []
    for g, group in enumerate(groups):
        at = 0
        for w in group:
            places.append((g, at, w.shape[1]))
            at += w.shape[1]
    wholes = [
        jax.ShapeDtypeStruct((2 * depth, sum(w.shape[1] for w in group)), BF16) for group in groups
    ]

    unit = hidden_weights[0].shape[1] // 8
    kinds = len(hidden_weights)

    def kernel(cot_ref, *refs):
        weight_refs = refs[: len(weights)]
        gain_ref = refs[len(weights)]
        refs = refs[len(weights) + 1 :]
        hidden_refs = refs[:kinds]
        refs = refs[kinds:]
        all_ref, gain_far_ref = refs[:2]
        whole_refs = refs[2 : 2 + len(groups)]
        refs = refs[2 + len(groups) :]
        pack_refs = refs[:5]
        refs = refs[5:]
        sems = refs[:7]
        send, recv, pack_sems = refs[7:]
        units, _ = unit_places(lax.axis_index("ctx"))
        packs = [
            pltpu.make_async_copy(
                hidden_refs[k].at[:, pl.ds(pl.multiple_of(at * unit, unit), unit)],
                pack_refs[c].at[:, pl.ds(k * unit, unit)], pack_sems.at[c * kinds + k],
            )
            for c, at in enumerate(units) for k in range(kinds)
        ]
        enter(ctx_size, tp_size, along=True, side=True)
        far = {"fsdp": 1 - lax.axis_index("fsdp")}
        last = len(weights)
        swaps = [remote(gain_ref, gain_far_ref, send.at[last], recv.at[last], far)]
        for i, (g, at, wide) in enumerate(places):
            swaps.append(
                remote(
                    weight_refs[i], whole_refs[g].at[pl.ds(depth, depth), pl.ds(at, wide)],
                    send.at[i], recv.at[i], far,
                )
            )
        for swap in swaps:
            swap.start()
        for pack in packs:
            pack.start()
        for i, (g, at, wide) in enumerate(places):
            whole_refs[g][0:depth, at : at + wide] = weight_refs[i][...]
        mine = rows_at(cot_ref, lax.axis_index("tp") * rows, rows)
        gather_rows(mine, all_ref, ctx_size, tp_size, sems, block=cot_ref)
        for pack in packs:
            pack.wait()
        for swap in swaps:
            swap.wait()

    return pl.pallas_call(
        kernel,
        out_shape=(
            jax.ShapeDtypeStruct((ctx_size * block_rows, width), BF16),
            jax.ShapeDtypeStruct(gains.shape, F32),
            *wholes,
            *[jax.ShapeDtypeStruct((depth, kinds * unit), BF16)] * 5,
        ),
        in_specs=[VMEM_SPEC] * (2 + len(weights)) + [HBM_SPEC] * kinds,
        out_specs=(HBM_SPEC,) + (VMEM_SPEC,) * (6 + len(groups)),
        scratch_shapes=gather_sems(ctx_size, tp_size)
        + [DMA((len(weights) + 1,)), DMA((len(weights) + 1,)), DMA((5 * kinds,))],
        compiler_params=pltpu.CompilerParams(
            collective_id=identity, has_side_effects=True, vmem_limit_bytes=40 << 20
        ),
    )(cot_rows, *weights, gains, *hidden_weights)


def place_blocks(table, pieces, wide, blocks, bases=None):
    count = len(pieces)
    depth, width = pieces[0].shape
    outs = width // wide

    def kernel(table_ref, *refs):
        which, step = pl.program_id(0), pl.program_id(1)
        for o in range(outs):
            for k in range(count):
                @pl.when(jnp.logical_and(which == o, step == k))
                def _(o=o, k=k):
                    refs[len(refs) - outs + o][...] = refs[k][...].astype(F32)

    def target(o):
        def index(which, step, table_ref):
            now = jnp.where(which < o, 0, jnp.where(which > o, count - 1, step))
            return 0, table_ref[now]

        return index

    shape = jax.ShapeDtypeStruct((depth, blocks * wide), F32)
    return pl.pallas_call(
        kernel,
        grid_spec=pltpu.PrefetchScalarGridSpec(
            num_scalar_prefetch=1,
            grid=(outs, count),
            in_specs=[
                pl.BlockSpec((depth, wide), lambda which, step, table_ref: (0, which))
            ] * count
            + [HBM_SPEC] * (0 if bases is None else outs),
            out_specs=tuple(pl.BlockSpec((depth, wide), target(o)) for o in range(outs)),
        ),
        out_shape=(shape,) * outs,
        input_output_aliases={} if bases is None else {1 + count + o: o for o in range(outs)},
        compiler_params=pltpu.CompilerParams(vmem_limit_bytes=32 << 20),
    )(table, *pieces, *(() if bases is None else bases))


def transposed_grads(columns, widths, last):
    depth = columns.shape[1]
    tile = min(depth, 256)
    widths = list(widths) + [last.shape[0]]

    def kernel(in_ref, last_ref, *out_refs):
        head = in_ref[...].astype(F32).T
        at = 0
        for out_ref, wide in zip(out_refs[:-1], widths[:-1]):
            out_ref[...] = head[:, at : at + wide]
            at += wide
        out_refs[-1][...] = last_ref[...].astype(F32).T

    return pl.pallas_call(
        kernel,
        grid=(depth // tile,),
        in_specs=[
            pl.BlockSpec((array.shape[0], tile), lambda i: (0, i)) for array in (columns, last)
        ],
        out_specs=tuple(pl.BlockSpec((tile, wide), lambda i: (i, 0)) for wide in widths),
        out_shape=tuple(jax.ShapeDtypeStruct((depth, wide), F32) for wide in widths),
    )(columns, last)


def mean_square(rows):
    return jnp.mean(rows * rows, axis=-1, keepdims=True)


def finish_middle(total, start, resid_ref, gain_ref, middle_ref):
    rows = total.shape[0]
    middle = resid_ref[pl.ds(start, rows), :].astype(F32) + total
    middle_ref[...] = middle
    return (middle * lax.rsqrt(mean_square(middle) + EPSILON) * gain_ref[...]).astype(BF16)


def norm_back(grad, base, values, gain):
    rms = lax.rsqrt(mean_square(values) + EPSILON)
    scaled = grad * gain
    gain_grad = jnp.sum(grad * values * rms, axis=0, keepdims=True)
    cube = rms * rms * rms
    full = base + rms * scaled - values * cube * jnp.mean(scaled * values, axis=-1, keepdims=True)
    return full, gain_grad


def finish_grad_middle(total, start, middle_ref, cot_ref, gain_ref, grad_ref, gain_grad_ref):
    base = cot_ref[pl.ds(start, total.shape[0]), :].astype(F32)
    full, gain_grad = norm_back(total, base, middle_ref[...], gain_ref[...])
    grad_ref[...] = full
    gain_grad_ref[...] = gain_grad
    return full.astype(BF16)


def finish_grad_input(total, start, grad_ref, resid_ref, gain_ref, gain_grad_ref):
    values = resid_ref[pl.ds(start, total.shape[0]), :].astype(F32)
    full, gain_grad = norm_back(total, grad_ref[...], values, gain_ref[...])
    gain_grad_ref[...] = gain_grad
    return full.astype(BF16)


def finish_output(total, start, middle_ref):
    return (middle_ref[...] + total).astype(BF16)


def make_local(ctx_size, tp_size):
    mesh_shape = (ctx_size, tp_size)
    swap_x = [(0, 1), (1, 0)]
    swap_z = [(i, i ^ 1) for i in range(ctx_size)]

    def swap_rows(array):
        return lax.ppermute(array, "fsdp", swap_x)

    def local(
        inputs, cotangent, prefix, attn_gain, w_query, key_projection, value_projection, w_out,
        ffn_gain, w_gate, w_up, w_down,
    ):
        side = lax.axis_index("fsdp")
        place = lax.axis_index("ctx")
        units, part = unit_places(place)
        row_count, model_width = inputs.shape[1:]
        half_width = model_width // 2
        query_width = w_query.shape[1]
        key_width = key_projection.shape[1]
        ffn_width = w_gate.shape[1]
        unit = ffn_width // 8
        query_heads = query_width // HEAD_SIZE
        kv_heads = key_width // HEAD_SIZE
        row_start = place * row_count
        pair_start = (place // 2) * 2 * row_count

        def own_first(rows):
            a = lax.dynamic_slice_in_dim(rows, side * half_width, half_width, 1)
            b = lax.dynamic_slice_in_dim(rows, (1 - side) * half_width, half_width, 1)
            return jnp.concatenate([a, b], axis=1)

        gains = jnp.stack([attn_gain, ffn_gain]).astype(F32)
        residual_low = own_first(inputs[0])
        cot_low = own_first(cotangent[0])
        rows_all, gains_far, qkv_weight, out_weight, *owns = opening(
            jnp.concatenate([cot_low, residual_low], axis=1),
            ((w_query, jnp.concatenate([key_projection, value_projection], axis=1)), (w_out,)),
            gains, (w_gate, w_up, w_down), mesh_shape, 0,
        )
        cot_all = rows_all[:, :model_width]
        gains = jnp.concatenate([gains, gains_far], axis=1)
        gain_first, gain_second = gains[0], gains[1]
        others = [swap_rows(owns[0]), swap_rows(owns[1]), None, None, None]

        cosine_lookup, sine_lookup = (table.T for table in rope_tables(row_start, row_count))
        residual = residual_low.astype(F32)
        rms_first = lax.rsqrt(jnp.mean(residual * residual, axis=-1, keepdims=True) + EPSILON)
        normalized_rows = (residual * rms_first * gain_first).astype(BF16)
        qkv = contract(qkv_weight, normalized_rows, 0, 1)
        queries = apply_rotary(
            qkv[:query_width].reshape(query_heads, HEAD_SIZE, row_count),
            cosine_lookup, sine_lookup, 1.0,
        ).astype(BF16)
        key_rot = apply_rotary(
            qkv[query_width : query_width + key_width].reshape(kv_heads, HEAD_SIZE, row_count),
            cosine_lookup, sine_lookup, 1.0,
        ).astype(BF16)
        value_rows = qkv[query_width + key_width :].astype(BF16)
        kv_own = jnp.concatenate([key_rot, value_rows.reshape(kv_heads, HEAD_SIZE, row_count)], axis=0)
        kv_whole = lax.all_gather(
            kv_own.reshape(2 * key_width, row_count).T, "ctx", axis=0, tiled=True
        )
        length_total = kv_whole.shape[0]
        by_place = kv_whole.reshape(length_total, 2 * kv_heads, HEAD_SIZE).transpose(1, 0, 2)
        by_feature = kv_whole.T.reshape(2 * kv_heads, HEAD_SIZE, length_total)
        bounds = jnp.stack([prefix[0], row_start.astype(jnp.int32)])
        attended, log_total = attend(
            bounds, queries, by_place[:kv_heads], by_feature[kv_heads:]
        )
        attended_flat = attended.reshape(query_width, row_count)
        attn_term = contract(attended_flat, out_weight, 0, 1).astype(BF16)
        attn_term, owns[2], others[0] = lax.optimization_barrier((attn_term, owns[2], others[0]))
        others[2] = swap_rows(owns[2])
        slice_shape = (row_count // tp_size, model_width)
        normed_all, middle = reduce_gather(
            attn_term, (residual_low, gain_second[None]), finish_middle,
            (slice_shape,), mesh_shape, 1, 1, True,
        )

        ffn_term = 0.0
        mid_term = 0.0
        sides = []
        fars = []
        received = []

        def pair(rows):
            return lax.dynamic_slice_in_dim(rows, pair_start, 2 * row_count, 0)

        def outer(sides_of, part_of):
            return [contract(part_of(rows), cols, 0, 0) for rows, cols in sides_of]

        def near_of(c):
            return jnp.concatenate(outer(sides[c], lambda rows: rows[:, :half_width]), axis=1)

        def summed(c, near=None):
            near = near_of(c) if near is None else near
            return (near + received[c].astype(F32)).astype(BF16)

        def forward(c):
            both_w = jnp.concatenate([owns[c], others[c]], axis=0)
            pair_w, down_w = both_w[:, : 2 * unit], both_w[:, 2 * unit :]
            both = jnp.dot(normed_all, pair_w, preferred_element_type=F32)
            gating, upward = both[:, :unit], both[:, unit:]
            grad_hidden = jnp.dot(cot_all, down_w, preferred_element_type=F32)
            sigmoid_gate = jax.nn.sigmoid(gating)
            hidden = (gating * sigmoid_gate * upward).astype(BF16)
            grad_gating = (
                grad_hidden * upward * sigmoid_gate * (1.0 + gating * (1.0 - sigmoid_gate))
            ).astype(BF16)
            grad_upward = (grad_hidden * gating * sigmoid_gate).astype(BF16)
            grad_both = jnp.concatenate([grad_gating, grad_upward], axis=1)
            sides.append(((normed_all, grad_both), (cot_all, hidden)))
            far = outer(sides[c], lambda rows: rows[:, half_width:])
            fars.append(jnp.concatenate([f.astype(BF16) for f in far], axis=1))
            return pair_w, down_w, grad_both, hidden

        for c in range(4):
            if c:
                others[c], fars[-1] = lax.optimization_barrier((others[c], fars[-1]))
            if c == 1:
                owns[3], others[1] = lax.optimization_barrier((owns[3], others[1]))
                others[3] = swap_rows(owns[3])
                others[4] = lax.ppermute(others[1], "ctx", swap_z)
            if c == 3:
                others[3], others[4] = lax.optimization_barrier((others[3], others[4]))
            pair_w, down_w, grad_both, hidden = forward(c)
            ffn_term += contract(pair(hidden), down_w, 1, 1)
            mid_term += contract(pair(grad_both), pair_w, 1, 1)

        def swap_ctx(total):
            return lax.ppermute(total, "ctx", swap_z)

        received = {0: swap_rows(fars[0]), 2: swap_rows(fars[2])}
        totals, swapped = {}, {}
        mid_low, fars[1], fars[3], received[0] = lax.optimization_barrier(
            (mid_term.astype(BF16), fars[1], fars[3], received[0])
        )
        received[3] = swap_rows(fars[3])
        totals[0] = summed(0)
        mid_low, totals[0] = lax.optimization_barrier((mid_low, totals[0]))
        swapped[0] = swap_ctx(totals[0])
        branch_low, grad_middle, gain_grad_second = reduce_gather(
            mid_low, (middle, cot_low, gain_second[None]), finish_grad_middle,
            (slice_shape, (1, model_width)), mesh_shape, 2, 2, False,
        )
        branch_low, received[2], fars[1], swapped[0], rows_all = lax.optimization_barrier(
            (branch_low, received[2], fars[1], swapped[0], rows_all)
        )
        received[1] = swap_rows(fars[1])
        totals[2] = summed(2)
        near_one = near_of(1)
        residual_all = rows_all[:, model_width:].astype(F32)
        rms_all = lax.rsqrt(jnp.mean(residual_all * residual_all, axis=-1, keepdims=True) + EPSILON)
        norm_all = (residual_all * rms_all * gain_first).astype(BF16)
        branch_low, totals[2], near_one, norm_all = lax.optimization_barrier(
            (branch_low, totals[2], near_one, norm_all)
        )
        swapped[2] = swap_ctx(totals[2])
        grad_out = jnp.dot(attended_flat, branch_low, preferred_element_type=F32)
        grad_out_half = grad_out[:, half_width:].astype(BF16)
        grad_attended = contract(out_weight, branch_low, 0, 1).astype(BF16)
        grad_query_rot, grad_kv = attend_back(
            bounds, queries, by_place[:kv_heads], by_feature[:kv_heads], by_place[kv_heads:],
            grad_attended.reshape(query_heads, HEAD_SIZE, row_count), log_total,
        )
        grad_kv = grad_kv.reshape(2 * key_width, length_total)
        far_base = 2 + 3 * (1 - part)
        table = jnp.stack(units + [far_base, far_base + 1, far_base + 2])
        grad_kv, received[3] = lax.optimization_barrier((grad_kv, received[3]))
        totals[3] = summed(3)
        grad_kv, totals[3] = lax.optimization_barrier((grad_kv, totals[3]))
        swapped[3] = swap_ctx(totals[3])
        early = [totals[0], totals[2], totals[3], swapped[0]]
        placed = place_blocks(
            jnp.stack([table[0], table[2], table[3], table[5]]), early, unit, 8
        )
        others[4], placed, swapped[2], received[1], grad_out_half = lax.optimization_barrier(
            (others[4], placed, swapped[2], received[1], grad_out_half)
        )
        grad_out_far = swap_rows(grad_out_half)
        forward(4)
        near_four = near_of(4)
        totals[1] = summed(1, near_one)
        grad_kv, near_four, fars[4], totals[1] = lax.optimization_barrier(
            (grad_kv, near_four, fars[4], totals[1])
        )
        received[4] = swap_rows(fars[4])
        output_rows, grad_kv = reduce_gather(
            ffn_term.astype(BF16), (middle,), finish_output, (), mesh_shape, 3, 2, False,
            KvSum(grad_kv, ctx_size),
        )
        output_rows, grad_kv, swapped[3], grad_out_far = lax.optimization_barrier(
            (output_rows, grad_kv, swapped[3], grad_out_far)
        )
        grad_query_pre = apply_rotary(
            grad_query_rot, cosine_lookup, sine_lookup, -1.0
        ).astype(BF16).reshape(query_width, row_count)
        grad_key_pre = apply_rotary(
            grad_kv[:key_width].reshape(kv_heads, HEAD_SIZE, row_count),
            cosine_lookup, sine_lookup, -1.0,
        ).astype(BF16).reshape(key_width, row_count)
        grad_value_pre = grad_kv[key_width:].astype(BF16)
        grad_qkv_pre = jnp.concatenate([grad_query_pre, grad_key_pre, grad_value_pre], axis=0)
        attn_width = grad_qkv_pre.shape[0]
        pre_slabs = grad_qkv_pre.reshape(ctx_size, attn_width // ctx_size, row_count)
        normed_term = contract(grad_qkv_pre, qkv_weight, 0, 1).astype(BF16)
        grad_out_rows = (grad_out[:, :half_width] + grad_out_far.astype(F32)).astype(BF16)
        input_rows, _, grad_attn, grad_out, gain_grads = reduce_gather(
            normed_term,
            (grad_middle, residual_low, gain_first[None]), finish_grad_input,
            ((1, model_width),), mesh_shape, 4, 1, False,
            AttnTail(pre_slabs, norm_all, gain_grad_second, grad_out_rows, mesh_shape),
        )
        grad_attn, received[4] = lax.optimization_barrier((grad_attn, received[4]))
        grad_query, grad_key, grad_value, grad_out = transposed_grads(
            grad_attn, (query_width, key_width, key_width), grad_out
        )
        totals[4] = summed(4, near_four)

        late = jnp.stack([table[1], table[4], table[6], table[7]])
        result = place_blocks(
            late, [totals[1], totals[4], swapped[2], swapped[3]], unit, 8, placed
        )

        return (
            own_first(output_rows)[None],
            own_first(input_rows)[None],
            gain_grads[0],
            grad_query,
            grad_key,
            grad_value,
            grad_out,
            gain_grads[1],
            result[0],
            result[1],
            result[2],
        )

    return local


def solution(mesh):
    return jax.shard_map(
        make_local(mesh.shape["ctx"], mesh.shape["tp"]),
        mesh=mesh,
        in_specs=(
            P("fsdp", "ctx", None), P("fsdp", "ctx", None), P("fsdp"), P("fsdp"),
            P("fsdp", "tp"), P("fsdp", "tp"), P("fsdp", "tp"), P("fsdp", "tp"),
            P("fsdp"), P("fsdp", "tp"), P("fsdp", "tp"), P("fsdp", "tp"),
        ),
        out_specs=(
            P("fsdp", "ctx", None), P("fsdp", "ctx", None), P("fsdp"), P("fsdp", "tp"),
            P("fsdp", "tp"), P("fsdp", "tp"), P("fsdp", "tp"), P("fsdp"),
            P("fsdp", "tp"), P("fsdp", "tp"), P("fsdp", "tp"),
        ),
        check_vma=False,
    )
```

```python
import math

import jax
import jax.numpy as jnp
from jax import lax
from jax.experimental import pallas as pl
from jax.experimental.pallas import tpu as pltpu
from jax.sharding import PartitionSpec as P

HEAD_SIZE = 64
EPSILON = 1e-05
THETA = 500000.0
MASKED = -1e30
F32 = jnp.float32
BF16 = jnp.bfloat16


def contract(left, right, left_dim, right_dim):
    return lax.dot_general(
        left, right, (((left_dim,), (right_dim,)), ((), ())), preferred_element_type=F32
    )


def rope_tables(row_start, row_count):
    position = (row_start + jnp.arange(row_count, dtype=jnp.int32)).astype(F32)
    exponent = jnp.arange(HEAD_SIZE // 2, dtype=jnp.int32).astype(F32) * (2.0 / HEAD_SIZE)
    angles = position[:, None] * jnp.power(THETA, -exponent)[None, :]
    return (jnp.cos(angles), jnp.sin(angles))


def apply_rotary(values, cosine_lookup, sine_lookup, direction):
    half_width = values.shape[1] // 2
    leading = values[:, :half_width]
    trailing = values[:, half_width:]
    sin = direction * sine_lookup
    return jnp.concatenate(
        [leading * cosine_lookup - trailing * sin, trailing * cosine_lookup + leading * sin],
        axis=1,
    )


def allowed_pairs(bounds_ref, shape):
    key_place = lax.broadcasted_iota(jnp.int32, shape, 0)
    query_place = bounds_ref[1] + lax.broadcasted_iota(jnp.int32, shape, 1)
    return (key_place <= query_place) | (key_place < bounds_ref[0])


SCORE_SCALE = 1.0 / math.sqrt(HEAD_SIZE)
SMEM_SPEC = pl.BlockSpec(memory_space=pltpu.SMEM)


def attend(bounds, queries, keys, values_flat):
    heads, _, rows = queries.shape
    places = keys.shape[1]
    group = heads // keys.shape[0]

    def kernel(bounds_ref, query_ref, key_ref, value_ref, out_ref, log_ref):
        @pl.loop(0, heads)
        def _(h):
            k = h // group
            scores = jnp.dot(key_ref[k], query_ref[h], preferred_element_type=F32) * SCORE_SCALE
            scores = jnp.where(allowed_pairs(bounds_ref, (places, rows)), scores, MASKED)
            peak = jnp.max(scores, axis=0, keepdims=True)
            weights = jnp.exp(scores - peak)
            total = jnp.sum(weights, axis=0, keepdims=True)
            probabilities = (weights * (1.0 / total)).astype(BF16)
            out_ref[h] = jnp.dot(
                value_ref[k], probabilities, preferred_element_type=F32
            ).astype(BF16)
            log_ref[h] = peak + jnp.log(total)

    return pl.pallas_call(
        kernel,
        out_shape=(
            jax.ShapeDtypeStruct(queries.shape, BF16),
            jax.ShapeDtypeStruct((heads, 1, rows), F32),
        ),
        in_specs=[SMEM_SPEC] + [pl.BlockSpec(memory_space=pltpu.VMEM)] * 3,
        out_specs=(pl.BlockSpec(memory_space=pltpu.VMEM),) * 2,
        compiler_params=pltpu.CompilerParams(vmem_limit_bytes=24 << 20),
    )(bounds, queries, keys, values_flat)


def attend_back(bounds, queries, keys, keys_flat, values, grads, log_total):
    heads, size, rows = queries.shape
    key_heads, places, _ = keys.shape
    group = heads // key_heads

    def kernel(
        bounds_ref, query_ref, key_ref, key_flat_ref, value_ref, grad_ref, log_ref, query_grad_ref,
        both_grad_ref, totals,
    ):
        totals[...] = jnp.zeros_like(totals)

        @pl.loop(0, heads)
        def _(h):
            k = h // group
            scores = jnp.dot(key_ref[k], query_ref[h], preferred_element_type=F32) * SCORE_SCALE
            scores = jnp.where(allowed_pairs(bounds_ref, (places, rows)), scores, MASKED)
            probabilities = jnp.exp(scores - log_ref[h])
            grad_probs = jnp.dot(value_ref[k], grad_ref[h], preferred_element_type=F32)
            delta = jnp.sum(probabilities * grad_probs, axis=0, keepdims=True)
            grad_scores = (probabilities * (grad_probs - delta)).astype(BF16)
            query_grad_ref[h] = SCORE_SCALE * jnp.dot(
                key_flat_ref[k], grad_scores, preferred_element_type=F32
            )
            totals[k] += SCORE_SCALE * contract(query_ref[h], grad_scores, 1, 1)
            totals[key_heads + k] += contract(grad_ref[h], probabilities.astype(BF16), 1, 1)

        both_grad_ref[...] = totals[...].astype(BF16)

    return pl.pallas_call(
        kernel,
        out_shape=(
            jax.ShapeDtypeStruct(queries.shape, F32),
            jax.ShapeDtypeStruct((2 * key_heads, size, places), BF16),
        ),
        in_specs=[SMEM_SPEC] + [pl.BlockSpec(memory_space=pltpu.VMEM)] * 6,
        out_specs=(pl.BlockSpec(memory_space=pltpu.VMEM),) * 2,
        scratch_shapes=[pltpu.VMEM((2 * key_heads, size, places), F32)],
        compiler_params=pltpu.CompilerParams(vmem_limit_bytes=32 << 20),
    )(bounds, queries, keys, keys_flat, values, grads, log_total)


MESH = pl.DeviceIdType.MESH
HBM_SPEC = pl.BlockSpec(memory_space=pl.ANY)
VMEM_SPEC = pl.BlockSpec(memory_space=pltpu.VMEM)
DMA = pltpu.SemaphoreType.DMA


def remote(src, dst, send, recv, peer):
    return pltpu.make_async_remote_copy(
        src_ref=src, dst_ref=dst, send_sem=send, recv_sem=recv, device_id=peer, device_id_type=MESH
    )


def rows_at(ref, start, count):
    return ref.at[pl.ds(pl.multiple_of(start, count), count)]


def guarded(condition, body):
    if condition is None:
        body()
    else:
        pl.when(condition)(body)


def tp_peers(tp_size):
    me = lax.axis_index("tp")
    core = lax.rem(me, 2)
    level = me // 2
    levels = tp_size // 2
    partner = me + 1 - 2 * core
    others = [lax.rem(level + step, levels) * 2 + core for step in range(1, levels)]
    return me, core, level, partner, others


def enter(ctx_size, tp_size, along=False, pair=False, side=False, tensor=True, line=False):
    place = lax.axis_index("ctx")
    barrier = pltpu.get_barrier_semaphore()

    def greet(peer):
        pl.semaphore_signal(barrier, inc=1, device_id=peer, device_id_type=MESH)

    count = 0
    if tensor:
        _, _, _, partner, others = tp_peers(tp_size)
        for peer in [partner] + others:
            greet({"tp": peer})
        count = count + 1 + len(others)
    if side:
        greet({"fsdp": 1 - lax.axis_index("fsdp")})
        count = count + 1
    if along:
        up = place + 1 < ctx_size
        down = place > 0

        @pl.when(up)
        def _():
            greet({"ctx": place + 1})

        @pl.when(down)
        def _():
            greet({"ctx": place - 1})

        count = count + up.astype(jnp.int32) + down.astype(jnp.int32)
    if pair:
        greet({"ctx": place + 1 - 2 * lax.rem(place, 2)})
        count = count + 1
    if line:
        for step in range(1, ctx_size):
            greet({"ctx": lax.rem(place + step, ctx_size)})
        count = count + ctx_size - 1
    pl.semaphore_wait(barrier, count)


def gather_sems(ctx_size, tp_size):
    spread = 2 * ctx_size - 1
    levels = tp_size // 2
    chips = max(levels - 1, 1)
    return [
        DMA((spread + 1,)), DMA((spread,)), DMA((chips, spread)), DMA((chips, spread)),
        DMA((levels, spread)), DMA((levels, spread)), DMA((1,)),
    ]


def gather_rows(mine, all_ref, ctx_size, tp_size, sems, block=None):
    hop_send, hop_recv, chip_send, chip_recv, core_send, core_recv, own_sem = sems
    place = lax.axis_index("ctx") if ctx_size > 1 else 0
    me, core, level, partner, others = tp_peers(tp_size)
    levels = tp_size // 2
    rows = mine.shape[0]
    middle = ctx_size - 1
    offsets = [0]
    for step in range(1, ctx_size):
        offsets += [-step, step]

    def spot(offset, who):
        return rows_at(all_ref, ((place + offset) * tp_size + who) * rows, rows)

    def hop(offset, step, src):
        slot = 2 * middle + 1 if offset == 0 and step < 0 else middle + offset
        return remote(
            src, spot(offset, me), hop_send.at[slot], hop_recv.at[middle + offset - step],
            {"ctx": place + step},
        )

    def hop_arrival(offset):
        step = -1 if offset < 0 else 1
        return remote(
            spot(offset, me), spot(offset, me), hop_send.at[middle + offset],
            hop_recv.at[middle + offset], {"ctx": place + step},
        )

    def chip(offset, index, src):
        return remote(
            src, spot(offset, me), chip_send.at[index, middle + offset],
            chip_recv.at[levels - 2 - index, middle + offset], {"tp": others[index]},
        )

    def chip_arrival(offset, index):
        where = spot(offset, others[index])
        return remote(
            where, where, chip_send.at[index, middle + offset],
            chip_recv.at[index, middle + offset], {"tp": others[index]},
        )

    def to_core(offset, index, who, src):
        return remote(
            src, spot(offset, who), core_send.at[index, middle + offset],
            core_recv.at[index, middle + offset], {"tp": partner},
        )

    def valid(offset):
        if offset == 0:
            return None
        return place + offset >= 0 if offset < 0 else place + offset < ctx_size

    def onward(offset):
        if offset < 0:
            return 1, jnp.logical_and(place + offset >= 0, place + 1 < ctx_size)
        return -1, jnp.logical_and(place + offset < ctx_size, place > 0)

    def fan_out(offset, src):
        for index in range(levels - 1):
            chip(offset, index, src).start()
        to_core(offset, 0, me, src).start()

    if block is None:
        own = pltpu.make_async_copy(mine, spot(0, me), own_sem.at[0])
    else:
        own = pltpu.make_async_copy(
            block, rows_at(all_ref, place * block.shape[0], block.shape[0]), own_sem.at[0]
        )
    own.start()
    if ctx_size > 1:
        @pl.when(place + 1 < ctx_size)
        def _():
            hop(0, 1, mine).start()

        @pl.when(place > 0)
        def _():
            hop(0, -1, mine).start()

    if block is None:
        fan_out(0, mine)
    for offset in offsets[1:]:
        def arrived(offset=offset):
            hop_arrival(offset).wait_recv()
            fan_out(offset, spot(offset, me))

        guarded(valid(offset), arrived)
        step, more = onward(offset)

        @pl.when(more)
        def _(offset=offset, step=step):
            hop(offset, step, spot(offset, me)).start()

    shared = offsets if block is None else offsets[1:]
    for offset in shared:
        def relay(offset=offset):
            for index in range(levels - 1):
                chip_arrival(offset, index).wait_recv()
                to_core(offset, 1 + index, others[index], spot(offset, others[index])).start()

        guarded(valid(offset), relay)

    for offset in shared:
        def drain(offset=offset):
            for index in range(levels):
                to_core(offset, index, me, spot(offset, me)).wait()
            for index in range(levels - 1):
                chip(offset, index, spot(offset, me)).wait_send()

        guarded(valid(offset), drain)
    own.wait()
    if ctx_size > 1:
        @pl.when(place + 1 < ctx_size)
        def _():
            hop(0, 1, mine).wait_send()

        @pl.when(place > 0)
        def _():
            hop(0, -1, mine).wait_send()

        for offset in offsets[1:]:
            step, more = onward(offset)

            @pl.when(more)
            def _(offset=offset, step=step):
                hop(offset, step, spot(offset, me)).wait_send()


def line_sems(ctx_size):
    spread = 2 * ctx_size - 1
    return [DMA((spread + 1,)), DMA((spread,)), DMA((1,))]


def line_gather(mine, all_ref, ctx_size, sems):
    hop_send, hop_recv, own_sem = sems
    place = lax.axis_index("ctx")
    rows = mine.shape[0]
    middle = ctx_size - 1
    offsets = [o for step in range(1, ctx_size) for o in (-step, step)]

    def spot(offset):
        return rows_at(all_ref, (place + offset) * rows, rows)

    def hop(offset, step, src):
        slot = 2 * middle + 1 if offset == 0 and step < 0 else middle + offset
        return remote(
            src, spot(offset), hop_send.at[slot], hop_recv.at[middle + offset - step],
            {"ctx": place + step},
        )

    def arrival(offset):
        step = -1 if offset < 0 else 1
        return remote(
            spot(offset), spot(offset), hop_send.at[middle + offset],
            hop_recv.at[middle + offset], {"ctx": place + step},
        )

    def valid(offset):
        return place + offset >= 0 if offset < 0 else place + offset < ctx_size

    def onward(offset):
        if offset < 0:
            return 1, jnp.logical_and(place + offset >= 0, place + 1 < ctx_size)
        return -1, jnp.logical_and(place + offset < ctx_size, place > 0)

    own = pltpu.make_async_copy(mine, spot(0), own_sem.at[0])
    ends = ((1, place + 1 < ctx_size), (-1, place > 0))

    def begin():
        for step, there in ends:
            @pl.when(there)
            def _(step=step):
                hop(0, step, mine).start()

        own.start()

    def stage(step):
        for offset in (-step, step):
            @pl.when(valid(offset))
            def _(offset=offset):
                arrival(offset).wait_recv()

            way, more = onward(offset)

            @pl.when(more)
            def _(offset=offset, way=way):
                hop(offset, way, spot(offset)).start()

    def drain():
        own.wait()
        for step, there in ends:
            @pl.when(there)
            def _(step=step):
                hop(0, step, mine).wait_send()

        for offset in offsets:
            step, more = onward(offset)

            @pl.when(more)
            def _(offset=offset, step=step):
                hop(offset, step, spot(offset)).wait_send()

    return begin, stage, drain


class KvSum:
    side = False

    def __init__(self, grad_kv, ctx_size):
        self.ctx_size = ctx_size
        self.inputs = (grad_kv,)
        self.rows = grad_kv.shape[1] // ctx_size
        self.block = (grad_kv.shape[0], self.rows)
        self.outs = (jax.ShapeDtypeStruct(self.block, F32),)
        self.out_specs = (VMEM_SPEC,)
        self.scratch = [
            pltpu.VMEM((ctx_size, *self.block), BF16), DMA((ctx_size,)), DMA((ctx_size,)),
        ]

    def bind(self, in_refs, out_refs, side_refs, scratch):
        (grad_ref,) = in_refs
        (sum_ref,) = out_refs
        slots, send, recv = scratch
        ctx_size, rows = self.ctx_size, self.rows
        place = lax.axis_index("ctx")

        def to(step):
            peer = lax.rem(place + step, ctx_size)
            return remote(
                grad_ref.at[:, pl.ds(pl.multiple_of(peer * rows, rows), rows)], slots.at[place],
                send.at[step], recv.at[step], {"ctx": peer},
            )

        def arrival(step):
            src = lax.rem(place + ctx_size - step, ctx_size)
            return remote(slots.at[src], slots.at[src], send.at[step], recv.at[step], {"ctx": src})

        def begin():
            for step in range(1, ctx_size):
                to(step).start()
            slots[place] = grad_ref[:, pl.ds(pl.multiple_of(place * rows, rows), rows)]

        def middle():
            pass

        def end():
            for step in range(1, ctx_size):
                arrival(step).wait_recv()
            total = slots[0].astype(F32)
            for z in range(1, ctx_size):
                total += slots[z].astype(F32)
            sum_ref[...] = total
            for step in range(1, ctx_size):
                to(step).wait_send()

        return begin, middle, end


class AttnTail:
    side = True

    def __init__(self, pre_slabs, norm_all, gain_second, out_rows, mesh_shape):
        self.ctx_size, self.tp_size = mesh_shape
        self.inputs = (pre_slabs, norm_all, gain_second, out_rows)
        self.wide, self.rows = pre_slabs.shape[1:]
        self.out_wide = out_rows.shape[0] // self.ctx_size
        self.half = norm_all.shape[1] // 2
        levels = self.tp_size // 2
        self.levels = levels
        self.outs = (
            jax.ShapeDtypeStruct((self.ctx_size * self.wide, self.half), BF16),
            jax.ShapeDtypeStruct((self.ctx_size * self.out_wide, self.half), BF16),
            jax.ShapeDtypeStruct((2, self.half), F32),
        )
        self.out_specs = (HBM_SPEC, HBM_SPEC, VMEM_SPEC)
        chips = max(levels - 1, 1)
        self.scratch = [
            pltpu.VMEM(pre_slabs.shape, BF16),
            pltpu.VMEM((self.wide, self.half), F32),
            pltpu.VMEM((self.wide, self.half), BF16),
            pltpu.VMEM((self.wide, self.half), BF16),
            pltpu.VMEM((self.wide, self.half), BF16),
            pltpu.VMEM((4, 2, self.half), F32),
            pltpu.VMEM((levels, 2, self.half), F32),
            pltpu.VMEM((self.ctx_size, 2, self.half), F32),
            DMA((self.ctx_size,)), DMA((self.ctx_size,)),
            DMA((6,)),
            DMA((chips,)), DMA((chips,)),
            DMA((self.ctx_size,)), DMA((self.ctx_size,)),
        ] + line_sems(self.ctx_size) + [
            pltpu.VMEM((self.ctx_size, self.out_wide, self.half), BF16),
            DMA((self.ctx_size,)), DMA((self.ctx_size,)),
            pltpu.VMEM((self.out_wide, self.half), BF16),
        ] + line_sems(self.ctx_size)

    def bind(self, in_refs, out_refs, side_refs, scratch):
        pre_ref, norm_ref, gain_second_ref, out_ref = in_refs
        all_ref, out_all_ref, gains_ref = out_refs
        slabs, own_half, far_half, from_far, quarter, swaps, by_level, by_place = scratch[:8]
        all_send, all_recv, duo, lev_send, lev_recv, ctx_send, ctx_recv = scratch[8:15]
        ctx_size, levels, half, rows = self.ctx_size, self.levels, self.half, self.rows
        place = lax.axis_index("ctx")
        _, _, level, partner, others = tp_peers(self.tp_size)
        far = {"fsdp": 1 - lax.axis_index("fsdp")}
        tile = min(512, half)
        line_begin, line_stage, line_drain = line_gather(quarter, all_ref, ctx_size, scratch[15:18])
        out_slots, out_send, out_recv, out_quarter = scratch[18:22]
        out_wide = self.out_wide
        out_begin, out_stage, out_drain = line_gather(
            out_quarter, out_all_ref, ctx_size, scratch[22:25]
        )

        def out_slab(step):
            peer = lax.rem(place + step, ctx_size)
            return remote(
                rows_at(out_ref, peer * out_wide, out_wide), out_slots.at[place],
                out_send.at[step], out_recv.at[step], {"ctx": peer},
            )

        def out_arrival(step):
            src = lax.rem(place + ctx_size - step, ctx_size)
            where = out_slots.at[src]
            return remote(where, where, out_send.at[step], out_recv.at[step], {"ctx": src})

        def slab(step):
            peer = lax.rem(place + step, ctx_size)
            return remote(
                pre_ref.at[peer], slabs.at[place], all_send.at[step], all_recv.at[step], {"ctx": peer}
            )

        def slab_arrival(step):
            src = lax.rem(place + ctx_size - step, ctx_size)
            return remote(
                slabs.at[src], slabs.at[src], all_send.at[step], all_recv.at[step], {"ctx": src}
            )

        grads = remote(far_half, from_far, duo.at[0], duo.at[1], far)
        gain_x = remote(swaps.at[0], swaps.at[1], duo.at[2], duo.at[3], far)
        gain_core = remote(swaps.at[2], swaps.at[3], duo.at[4], duo.at[5], {"tp": partner})

        def gain_level(index):
            return remote(
                by_level.at[level], by_level.at[level], lev_send.at[index],
                lev_recv.at[levels - 2 - index], {"tp": others[index]},
            )

        def gain_level_arrival(index):
            where = by_level.at[lax.rem(level + 1 + index, levels)]
            return remote(where, where, lev_send.at[index], lev_recv.at[index], {"tp": others[index]})

        def gain_place(step):
            peer = lax.rem(place + step, ctx_size)
            return remote(
                by_place.at[place], by_place.at[place], ctx_send.at[step], ctx_recv.at[step],
                {"ctx": peer},
            )

        def gain_place_arrival(step):
            src = lax.rem(place + ctx_size - step, ctx_size)
            where = by_place.at[src]
            return remote(where, where, ctx_send.at[step], ctx_recv.at[step], {"ctx": src})

        def product(at):
            columns = pl.ds(pl.multiple_of(at, tile), tile)
            total = jnp.dot(
                slabs[0], norm_ref[0:rows, columns], preferred_element_type=F32
            )
            for z in range(1, ctx_size):
                total += jnp.dot(
                    slabs[z], norm_ref[z * rows : (z + 1) * rows, columns],
                    preferred_element_type=F32,
                )
            return total

        def begin():
            for step in range(1, ctx_size):
                slab(step).start()
            slabs[place] = pre_ref[place]
            out_slots[place] = out_ref[pl.ds(pl.multiple_of(place * out_wide, out_wide), out_wide), :]

        def middle():
            for step in range(1, ctx_size):
                slab_arrival(step).wait_recv()
            for step in range(1, ctx_size):
                out_slab(step).start()

            @pl.loop(0, half // tile)
            def _(i):
                far_half[:, pl.ds(pl.multiple_of(i * tile, tile), tile)] = product(
                    half + i * tile
                ).astype(BF16)

            grads.start()

            @pl.loop(0, half // tile)
            def _(i):
                own_half[:, pl.ds(pl.multiple_of(i * tile, tile), tile)] = product(i * tile)

        def end():
            gain_first = side_refs[0]
            swaps[0, 0:1, :] = gain_first[:, half:]
            swaps[0, 1:2, :] = gain_second_ref[:, half:]
            gain_x.start()
            grads.wait_recv()
            quarter[...] = (own_half[...] + from_far[...].astype(F32)).astype(BF16)
            line_begin()
            gain_x.wait_recv()
            swaps[2, 0:1, :] = gain_first[:, :half] + swaps[1, 0:1, :]
            swaps[2, 1:2, :] = gain_second_ref[:, :half] + swaps[1, 1:2, :]
            gain_core.start()
            for step in range(1, ctx_size):
                out_arrival(step).wait_recv()
            total = out_slots[0].astype(F32)
            for z in range(1, ctx_size):
                total += out_slots[z].astype(F32)
            out_quarter[...] = total.astype(BF16)
            out_begin()
            gain_core.wait_recv()
            by_level[level] = swaps[2] + swaps[3]
            for index in range(levels - 1):
                gain_level(index).start()
            line_stage(1)
            for index in range(levels - 1):
                gain_level_arrival(index).wait_recv()
            total = by_level[0]
            for lev in range(1, levels):
                total += by_level[lev]
            by_place[place] = total
            for step in range(1, ctx_size):
                gain_place(step).start()
            out_stage(1)
            for step in range(2, ctx_size):
                line_stage(step)
                out_stage(step)
            for step in range(1, ctx_size):
                gain_place_arrival(step).wait_recv()
            total = by_place[0]
            for z in range(1, ctx_size):
                total += by_place[z]
            gains_ref[...] = total
            line_drain()
            out_drain()
            for step in range(1, ctx_size):
                slab(step).wait_send()
                out_slab(step).wait_send()
                gain_place(step).wait_send()
            for index in range(levels - 1):
                gain_level(index).wait_send()
            grads.wait_send()
            gain_x.wait_send()
            gain_core.wait_send()

        return begin, middle, end


def reduce_gather(term, extras, finish, side_shapes, mesh_shape, identity, blocks, across, aside=None):
    ctx_size, tp_size = mesh_shape
    levels = tp_size // 2
    width = term.shape[1]
    block_rows = term.shape[0] // blocks
    rows = block_rows // tp_size
    reach = ctx_size if across else 1
    beside = aside is not None
    aside_inputs = aside.inputs if beside else ()
    aside_outs = aside.outs if beside else ()
    aside_scratch = aside.scratch if beside else []

    def kernel(term_ref, *refs):
        extra_refs = refs[: len(extras)]
        refs = refs[len(extras) :]
        aside_in = refs[: len(aside_inputs)]
        refs = refs[len(aside_inputs) :]
        all_ref = refs[0]
        side_refs = refs[1 : 1 + len(side_shapes)]
        refs = refs[1 + len(side_shapes) :]
        aside_out = refs[: len(aside_outs)]
        refs = refs[len(aside_outs) :]
        from_core, stage, from_chip, mine = refs[:4]
        refs = refs[4:]
        if blocks == 2:
            pair_stage, from_pair = refs[:2]
            refs = refs[2:]
        sems = refs[:7]
        core_send, core_recv, chip_send, chip_recv, pair_sems = refs[7:12]
        place = lax.axis_index("ctx")
        me, core, level, partner, others = tp_peers(tp_size)
        enter(
            ctx_size, tp_size, along=across, pair=blocks == 2 and not beside,
            side=beside and aside.side, line=beside,
        )
        if beside:
            aside_begin, aside_middle, aside_end = aside.bind(
                aside_in, aside_out, side_refs, refs[12:]
            )
            aside_begin()

        def to_core(block, lev):
            slot = block * levels + lev
            return remote(
                rows_at(term_ref, block * block_rows + (2 * lev + 1 - core) * rows, rows),
                from_core.at[slot], core_send.at[slot], core_recv.at[slot], {"tp": partner},
            )

        def to_chip(index):
            return remote(
                stage.at[index], from_chip.at[levels - 2 - index], chip_send.at[index],
                chip_recv.at[levels - 2 - index], {"tp": others[index]},
            )

        def chip_sum(block, lev):
            own = term_ref[
                pl.ds(pl.multiple_of(block * block_rows + (2 * lev + core) * rows, rows), rows), :
            ]
            return own.astype(F32) + from_core[block * levels + lev].astype(F32)

        for lev in range(levels):
            for block in range(blocks):
                to_core(block, lev).start()
        for lev in range(levels):
            for block in range(blocks):
                to_core(block, lev).wait_recv()
        for index in range(levels - 1):
            lev = lax.rem(level + 1 + index, levels)
            for block in range(blocks):
                stage[index, block * rows : (block + 1) * rows, :] = chip_sum(block, lev).astype(
                    BF16
                )
            to_chip(index).start()
        if beside:
            aside_middle()
        for index in range(levels - 1):
            to_chip(index).wait_recv()

        def tp_sum(block):
            total = chip_sum(block, level)
            for index in range(levels - 1):
                total += from_chip[
                    index, pl.ds(pl.multiple_of(block * rows, rows), rows), :
                ].astype(F32)
            return total

        if blocks == 2:
            low = lax.rem(place, 2)
            pair_stage[...] = tp_sum(1 - low).astype(BF16)
            swap = remote(
                pair_stage, from_pair, pair_sems.at[0], pair_sems.at[1], {"ctx": place + 1 - 2 * low}
            )
            swap.start()
            total = tp_sum(low)
            swap.wait_recv()
            total += from_pair[...].astype(F32)
        else:
            total = tp_sum(0)
        start = pl.multiple_of(me * rows, rows)
        mine[...] = finish(total, start, *extra_refs, *side_refs)
        gather_rows(mine, all_ref, reach, tp_size, sems)
        if beside:
            aside_end()
        for lev in range(levels):
            for block in range(blocks):
                to_core(block, lev).wait_send()
        for index in range(levels - 1):
            to_chip(index).wait_send()
        if blocks == 2:
            swap.wait_send()

    chips = max(levels - 1, 1)
    scratch = [
        pltpu.VMEM((blocks * levels, rows, width), BF16),
        pltpu.VMEM((chips, blocks * rows, width), BF16),
        pltpu.VMEM((chips, blocks * rows, width), BF16),
        pltpu.VMEM((rows, width), BF16),
    ]
    if blocks == 2:
        scratch += [pltpu.VMEM((rows, width), BF16)] * 2
    scratch += gather_sems(reach, tp_size)
    scratch += [
        DMA((blocks * levels,)), DMA((blocks * levels,)), DMA((chips,)), DMA((chips,)), DMA((2,)),
    ]
    scratch += aside_scratch
    return pl.pallas_call(
        kernel,
        out_shape=(
            jax.ShapeDtypeStruct((reach * block_rows, width), BF16),
            *(jax.ShapeDtypeStruct(shape, F32) for shape in side_shapes),
            *aside_outs,
        ),
        in_specs=[VMEM_SPEC] * (1 + len(extras) + len(aside_inputs)),
        out_specs=(HBM_SPEC,) + (VMEM_SPEC,) * len(side_shapes)
        + (aside.out_specs if beside else ()),
        scratch_shapes=scratch,
        compiler_params=pltpu.CompilerParams(
            collective_id=identity, has_side_effects=True, vmem_limit_bytes=32 << 20
        ),
    )(term, *extras, *aside_inputs)


def unit_places(place):
    low = place % 2
    part = ((place + 1) // 2) % 2
    base = 2 + 3 * part
    return [base, low, base + 1, base + 2, 1 - low], part


def opening(cot_rows, groups, gains, hidden_weights, mesh_shape, identity):
    ctx_size, tp_size = mesh_shape
    block_rows, width = cot_rows.shape
    rows = block_rows // tp_size
    weights = [w for group in groups for w in group]
    depth = weights[0].shape[0]
    places = []
    for g, group in enumerate(groups):
        at = 0
        for w in group:
            places.append((g, at, w.shape[1]))
            at += w.shape[1]
    wholes = [
        jax.ShapeDtypeStruct((2 * depth, sum(w.shape[1] for w in group)), BF16) for group in groups
    ]

    unit = hidden_weights[0].shape[1] // 8
    kinds = len(hidden_weights)

    def kernel(cot_ref, *refs):
        weight_refs = refs[: len(weights)]
        gain_ref = refs[len(weights)]
        refs = refs[len(weights) + 1 :]
        hidden_refs = refs[:kinds]
        refs = refs[kinds:]
        all_ref, gain_far_ref = refs[:2]
        whole_refs = refs[2 : 2 + len(groups)]
        refs = refs[2 + len(groups) :]
        pack_refs = refs[:5]
        refs = refs[5:]
        sems = refs[:7]
        send, recv, pack_sems = refs[7:]
        units, _ = unit_places(lax.axis_index("ctx"))
        packs = [
            pltpu.make_async_copy(
                hidden_refs[k].at[:, pl.ds(pl.multiple_of(at * unit, unit), unit)],
                pack_refs[c].at[:, pl.ds(k * unit, unit)], pack_sems.at[c * kinds + k],
            )
            for c, at in enumerate(units) for k in range(kinds)
        ]
        enter(ctx_size, tp_size, along=True, side=True)
        far = {"fsdp": 1 - lax.axis_index("fsdp")}
        last = len(weights)
        swaps = [remote(gain_ref, gain_far_ref, send.at[last], recv.at[last], far)]
        for i, (g, at, wide) in enumerate(places):
            swaps.append(
                remote(
                    weight_refs[i], whole_refs[g].at[pl.ds(depth, depth), pl.ds(at, wide)],
                    send.at[i], recv.at[i], far,
                )
            )
        for swap in swaps:
            swap.start()
        for pack in packs:
            pack.start()
        for i, (g, at, wide) in enumerate(places):
            whole_refs[g][0:depth, at : at + wide] = weight_refs[i][...]
        mine = rows_at(cot_ref, lax.axis_index("tp") * rows, rows)
        gather_rows(mine, all_ref, ctx_size, tp_size, sems, block=cot_ref)
        for pack in packs:
            pack.wait()
        for swap in swaps:
            swap.wait()

    return pl.pallas_call(
        kernel,
        out_shape=(
            jax.ShapeDtypeStruct((ctx_size * block_rows, width), BF16),
            jax.ShapeDtypeStruct(gains.shape, F32),
            *wholes,
            *[jax.ShapeDtypeStruct((depth, kinds * unit), BF16)] * 5,
        ),
        in_specs=[VMEM_SPEC] * (2 + len(weights)) + [HBM_SPEC] * kinds,
        out_specs=(HBM_SPEC,) + (VMEM_SPEC,) * (6 + len(groups)),
        scratch_shapes=gather_sems(ctx_size, tp_size)
        + [DMA((len(weights) + 1,)), DMA((len(weights) + 1,)), DMA((5 * kinds,))],
        compiler_params=pltpu.CompilerParams(
            collective_id=identity, has_side_effects=True, vmem_limit_bytes=40 << 20
        ),
    )(cot_rows, *weights, gains, *hidden_weights)


def place_blocks(table, pieces, wide, blocks, bases=None):
    count = len(pieces)
    depth, width = pieces[0].shape
    outs = width // wide

    def kernel(table_ref, *refs):
        which, step = pl.program_id(0), pl.program_id(1)
        for o in range(outs):
            for k in range(count):
                @pl.when(jnp.logical_and(which == o, step == k))
                def _(o=o, k=k):
                    refs[len(refs) - outs + o][...] = refs[k][...].astype(F32)

    def target(o):
        def index(which, step, table_ref):
            now = jnp.where(which < o, 0, jnp.where(which > o, count - 1, step))
            return 0, table_ref[now]

        return index

    shape = jax.ShapeDtypeStruct((depth, blocks * wide), F32)
    return pl.pallas_call(
        kernel,
        grid_spec=pltpu.PrefetchScalarGridSpec(
            num_scalar_prefetch=1,
            grid=(outs, count),
            in_specs=[
                pl.BlockSpec((depth, wide), lambda which, step, table_ref: (0, which))
            ] * count
            + [HBM_SPEC] * (0 if bases is None else outs),
            out_specs=tuple(pl.BlockSpec((depth, wide), target(o)) for o in range(outs)),
        ),
        out_shape=(shape,) * outs,
        input_output_aliases={} if bases is None else {1 + count + o: o for o in range(outs)},
        compiler_params=pltpu.CompilerParams(vmem_limit_bytes=32 << 20),
    )(table, *pieces, *(() if bases is None else bases))


def transposed_grads(columns, widths, last):
    depth = columns.shape[1]
    tile = min(depth, 256)
    widths = list(widths) + [last.shape[0]]

    def kernel(in_ref, last_ref, *out_refs):
        head = in_ref[...].astype(F32).T
        at = 0
        for out_ref, wide in zip(out_refs[:-1], widths[:-1]):
            out_ref[...] = head[:, at : at + wide]
            at += wide
        out_refs[-1][...] = last_ref[...].astype(F32).T

    return pl.pallas_call(
        kernel,
        grid=(depth // tile,),
        in_specs=[
            pl.BlockSpec((array.shape[0], tile), lambda i: (0, i)) for array in (columns, last)
        ],
        out_specs=tuple(pl.BlockSpec((tile, wide), lambda i: (i, 0)) for wide in widths),
        out_shape=tuple(jax.ShapeDtypeStruct((depth, wide), F32) for wide in widths),
    )(columns, last)


def mean_square(rows):
    return jnp.mean(rows * rows, axis=-1, keepdims=True)


def normalize_rows(rows, gain):
    count, width = rows.shape[0], rows.shape[1] // 2
    tile = min(count, 256)

    def kernel(row_ref, gain_ref, out_ref):
        values = row_ref[...].astype(F32)
        out_ref[...] = (
            values * lax.rsqrt(mean_square(values) + EPSILON) * gain_ref[...]
        ).astype(BF16)

    return pl.pallas_call(
        kernel,
        grid=(count // tile,),
        in_specs=[
            pl.BlockSpec((tile, width), lambda i: (i, 1)),
            pl.BlockSpec((1, width), lambda i: (0, 0)),
        ],
        out_specs=pl.BlockSpec((tile, width), lambda i: (i, 0)),
        out_shape=jax.ShapeDtypeStruct((count, width), BF16),
    )(rows, gain)


def finish_middle(total, start, resid_ref, gain_ref, middle_ref):
    rows = total.shape[0]
    middle = resid_ref[pl.ds(start, rows), :].astype(F32) + total
    middle_ref[...] = middle
    return (middle * lax.rsqrt(mean_square(middle) + EPSILON) * gain_ref[...]).astype(BF16)


def norm_back(grad, base, values, gain):
    rms = lax.rsqrt(mean_square(values) + EPSILON)
    scaled = grad * gain
    gain_grad = jnp.sum(grad * values * rms, axis=0, keepdims=True)
    cube = rms * rms * rms
    full = base + rms * scaled - values * cube * jnp.mean(scaled * values, axis=-1, keepdims=True)
    return full, gain_grad


def finish_grad_middle(total, start, middle_ref, cot_ref, gain_ref, grad_ref, gain_grad_ref):
    base = cot_ref[pl.ds(start, total.shape[0]), :].astype(F32)
    full, gain_grad = norm_back(total, base, middle_ref[...], gain_ref[...])
    grad_ref[...] = full
    gain_grad_ref[...] = gain_grad
    return full.astype(BF16)


def finish_grad_input(total, start, grad_ref, resid_ref, gain_ref, gain_grad_ref):
    values = resid_ref[pl.ds(start, total.shape[0]), :].astype(F32)
    full, gain_grad = norm_back(total, grad_ref[...], values, gain_ref[...])
    gain_grad_ref[...] = gain_grad
    return full.astype(BF16)


def finish_output(total, start, middle_ref):
    return (middle_ref[...] + total).astype(BF16)


def make_local(ctx_size, tp_size):
    mesh_shape = (ctx_size, tp_size)
    swap_x = [(0, 1), (1, 0)]
    swap_z = [(i, i ^ 1) for i in range(ctx_size)]

    def swap_rows(array):
        return lax.ppermute(array, "fsdp", swap_x)

    def local(
        inputs, cotangent, prefix, attn_gain, w_query, key_projection, value_projection, w_out,
        ffn_gain, w_gate, w_up, w_down,
    ):
        side = lax.axis_index("fsdp")
        place = lax.axis_index("ctx")
        units, part = unit_places(place)
        row_count, model_width = inputs.shape[1:]
        half_width = model_width // 2
        query_width = w_query.shape[1]
        key_width = key_projection.shape[1]
        ffn_width = w_gate.shape[1]
        unit = ffn_width // 8
        query_heads = query_width // HEAD_SIZE
        kv_heads = key_width // HEAD_SIZE
        row_start = place * row_count
        pair_start = (place // 2) * 2 * row_count

        def own_first(rows):
            a = lax.dynamic_slice_in_dim(rows, side * half_width, half_width, 1)
            b = lax.dynamic_slice_in_dim(rows, (1 - side) * half_width, half_width, 1)
            return jnp.concatenate([a, b], axis=1)

        gains = jnp.stack([attn_gain, ffn_gain]).astype(F32)
        residual_low = own_first(inputs[0])
        cot_low = own_first(cotangent[0])
        rows_all, gains_far, qkv_weight, out_weight, *owns = opening(
            jnp.concatenate([cot_low, residual_low], axis=1),
            ((w_query, jnp.concatenate([key_projection, value_projection], axis=1)), (w_out,)),
            gains, (w_gate, w_up, w_down), mesh_shape, 0,
        )
        cot_all = rows_all[:, :model_width]
        gains = jnp.concatenate([gains, gains_far], axis=1)
        gain_first, gain_second = gains[0], gains[1]
        others = [swap_rows(owns[0]), swap_rows(owns[1]), None, None, None]

        cosine_lookup, sine_lookup = (table.T for table in rope_tables(row_start, row_count))
        residual = residual_low.astype(F32)
        rms_first = lax.rsqrt(jnp.mean(residual * residual, axis=-1, keepdims=True) + EPSILON)
        normalized_rows = (residual * rms_first * gain_first).astype(BF16)
        qkv = contract(qkv_weight, normalized_rows, 0, 1)
        queries = apply_rotary(
            qkv[:query_width].reshape(query_heads, HEAD_SIZE, row_count),
            cosine_lookup, sine_lookup, 1.0,
        ).astype(BF16)
        key_rot = apply_rotary(
            qkv[query_width : query_width + key_width].reshape(kv_heads, HEAD_SIZE, row_count),
            cosine_lookup, sine_lookup, 1.0,
        ).astype(BF16)
        value_rows = qkv[query_width + key_width :].astype(BF16)
        kv_own = jnp.concatenate([key_rot, value_rows.reshape(kv_heads, HEAD_SIZE, row_count)], axis=0)
        kv_whole = lax.all_gather(
            kv_own.reshape(2 * key_width, row_count).T, "ctx", axis=0, tiled=True
        )
        length_total = kv_whole.shape[0]
        by_place = kv_whole.reshape(length_total, 2 * kv_heads, HEAD_SIZE).transpose(1, 0, 2)
        by_feature = kv_whole.T.reshape(2 * kv_heads, HEAD_SIZE, length_total)
        bounds = jnp.stack([prefix[0], row_start.astype(jnp.int32)])
        attended, log_total = attend(
            bounds, queries, by_place[:kv_heads], by_feature[kv_heads:]
        )
        attended_flat = attended.reshape(query_width, row_count)
        attn_term = contract(attended_flat, out_weight, 0, 1).astype(BF16)
        attn_term, owns[2], others[0] = lax.optimization_barrier((attn_term, owns[2], others[0]))
        others[2] = swap_rows(owns[2])
        slice_shape = (row_count // tp_size, model_width)
        normed_all, middle = reduce_gather(
            attn_term, (residual_low, gain_second[None]), finish_middle,
            (slice_shape,), mesh_shape, 1, 1, True,
        )

        ffn_term = 0.0
        mid_term = 0.0
        sides = []
        fars = []
        received = []

        def pair(rows):
            return lax.dynamic_slice_in_dim(rows, pair_start, 2 * row_count, 0)

        def outer(sides_of, part_of):
            return [contract(part_of(rows), cols, 0, 0) for rows, cols in sides_of]

        def near_of(c):
            return jnp.concatenate(outer(sides[c], lambda rows: rows[:, :half_width]), axis=1)

        def summed(c, near=None):
            near = near_of(c) if near is None else near
            return (near + received[c].astype(F32)).astype(BF16)

        def forward(c):
            both_w = jnp.concatenate([owns[c], others[c]], axis=0)
            pair_w, down_w = both_w[:, : 2 * unit], both_w[:, 2 * unit :]
            both = jnp.dot(normed_all, pair_w, preferred_element_type=F32)
            gating, upward = both[:, :unit], both[:, unit:]
            grad_hidden = jnp.dot(cot_all, down_w, preferred_element_type=F32)
            sigmoid_gate = jax.nn.sigmoid(gating)
            hidden = (gating * sigmoid_gate * upward).astype(BF16)
            grad_gating = (
                grad_hidden * upward * sigmoid_gate * (1.0 + gating * (1.0 - sigmoid_gate))
            ).astype(BF16)
            grad_upward = (grad_hidden * gating * sigmoid_gate).astype(BF16)
            grad_both = jnp.concatenate([grad_gating, grad_upward], axis=1)
            sides.append(((normed_all, grad_both), (cot_all, hidden)))
            far = outer(sides[c], lambda rows: rows[:, half_width:])
            fars.append(jnp.concatenate([f.astype(BF16) for f in far], axis=1))
            return pair_w, down_w, grad_both, hidden

        for c in range(4):
            if c:
                others[c], fars[-1] = lax.optimization_barrier((others[c], fars[-1]))
            if c == 1:
                owns[3], others[1] = lax.optimization_barrier((owns[3], others[1]))
                others[3] = swap_rows(owns[3])
                others[4] = lax.ppermute(others[1], "ctx", swap_z)
            if c == 3:
                others[3], others[4] = lax.optimization_barrier((others[3], others[4]))
            pair_w, down_w, grad_both, hidden = forward(c)
            ffn_term += contract(pair(hidden), down_w, 1, 1)
            mid_term += contract(pair(grad_both), pair_w, 1, 1)

        def swap_ctx(total):
            return lax.ppermute(total, "ctx", swap_z)

        received = {0: swap_rows(fars[0]), 2: swap_rows(fars[2])}
        totals, swapped = {}, {}
        mid_low, fars[1], fars[3], received[0] = lax.optimization_barrier(
            (mid_term.astype(BF16), fars[1], fars[3], received[0])
        )
        received[3] = swap_rows(fars[3])
        totals[0] = summed(0)
        mid_low, totals[0] = lax.optimization_barrier((mid_low, totals[0]))
        swapped[0] = swap_ctx(totals[0])
        branch_low, grad_middle, gain_grad_second = reduce_gather(
            mid_low, (middle, cot_low, gain_second[None]), finish_grad_middle,
            (slice_shape, (1, model_width)), mesh_shape, 2, 2, False,
        )
        branch_low, received[2], fars[1], swapped[0], rows_all = lax.optimization_barrier(
            (branch_low, received[2], fars[1], swapped[0], rows_all)
        )
        received[1] = swap_rows(fars[1])
        totals[2] = summed(2)
        near_one = near_of(1)
        branch_low, totals[2], near_one = lax.optimization_barrier(
            (branch_low, totals[2], near_one)
        )
        swapped[2] = swap_ctx(totals[2])
        grad_out = jnp.dot(attended_flat, branch_low, preferred_element_type=F32)
        grad_out_half = grad_out[:, half_width:].astype(BF16)
        grad_attended = contract(out_weight, branch_low, 0, 1).astype(BF16)
        grad_query_rot, grad_kv = attend_back(
            bounds, queries, by_place[:kv_heads], by_feature[:kv_heads], by_place[kv_heads:],
            grad_attended.reshape(query_heads, HEAD_SIZE, row_count), log_total,
        )
        grad_kv = grad_kv.reshape(2 * key_width, length_total)
        far_base = 2 + 3 * (1 - part)
        table = jnp.stack(units + [far_base, far_base + 1, far_base + 2])
        grad_kv, received[3] = lax.optimization_barrier((grad_kv, received[3]))
        totals[3] = summed(3)
        grad_kv, totals[3] = lax.optimization_barrier((grad_kv, totals[3]))
        swapped[3] = swap_ctx(totals[3])
        early = [totals[0], totals[2], totals[3], swapped[0]]
        placed = place_blocks(
            jnp.stack([table[0], table[2], table[3], table[5]]), early, unit, 8
        )
        grad_kv, rows_all = lax.optimization_barrier((grad_kv, rows_all))
        norm_all = normalize_rows(rows_all, gain_first[None])
        placed, norm_all = lax.optimization_barrier((placed, norm_all))
        others[4], placed, swapped[2], received[1], grad_out_half = lax.optimization_barrier(
            (others[4], placed, swapped[2], received[1], grad_out_half)
        )
        grad_out_far = swap_rows(grad_out_half)
        forward(4)
        near_four = near_of(4)
        totals[1] = summed(1, near_one)
        grad_kv, near_four, fars[4], totals[1] = lax.optimization_barrier(
            (grad_kv, near_four, fars[4], totals[1])
        )
        received[4] = swap_rows(fars[4])
        output_rows, grad_kv = reduce_gather(
            ffn_term.astype(BF16), (middle,), finish_output, (), mesh_shape, 3, 2, False,
            KvSum(grad_kv, ctx_size),
        )
        output_rows, grad_kv, swapped[3], grad_out_far = lax.optimization_barrier(
            (output_rows, grad_kv, swapped[3], grad_out_far)
        )
        grad_query_pre = apply_rotary(
            grad_query_rot, cosine_lookup, sine_lookup, -1.0
        ).astype(BF16).reshape(query_width, row_count)
        grad_key_pre = apply_rotary(
            grad_kv[:key_width].reshape(kv_heads, HEAD_SIZE, row_count),
            cosine_lookup, sine_lookup, -1.0,
        ).astype(BF16).reshape(key_width, row_count)
        grad_value_pre = grad_kv[key_width:].astype(BF16)
        grad_qkv_pre = jnp.concatenate([grad_query_pre, grad_key_pre, grad_value_pre], axis=0)
        attn_width = grad_qkv_pre.shape[0]
        pre_slabs = grad_qkv_pre.reshape(ctx_size, attn_width // ctx_size, row_count)
        normed_term = contract(grad_qkv_pre, qkv_weight, 0, 1).astype(BF16)
        grad_out_rows = (grad_out[:, :half_width] + grad_out_far.astype(F32)).astype(BF16)
        input_rows, _, grad_attn, grad_out, gain_grads = reduce_gather(
            normed_term,
            (grad_middle, residual_low, gain_first[None]), finish_grad_input,
            ((1, model_width),), mesh_shape, 4, 1, False,
            AttnTail(pre_slabs, norm_all, gain_grad_second, grad_out_rows, mesh_shape),
        )
        grad_attn, received[4] = lax.optimization_barrier((grad_attn, received[4]))
        grad_query, grad_key, grad_value, grad_out = transposed_grads(
            grad_attn, (query_width, key_width, key_width), grad_out
        )
        totals[4] = summed(4, near_four)

        late = jnp.stack([table[1], table[4], table[6], table[7]])
        result = place_blocks(
            late, [totals[1], totals[4], swapped[2], swapped[3]], unit, 8, placed
        )

        return (
            own_first(output_rows)[None],
            own_first(input_rows)[None],
            gain_grads[0],
            grad_query,
            grad_key,
            grad_value,
            grad_out,
            gain_grads[1],
            result[0],
            result[1],
            result[2],
        )

    return local


def solution(mesh):
    return jax.shard_map(
        make_local(mesh.shape["ctx"], mesh.shape["tp"]),
        mesh=mesh,
        in_specs=(
            P("fsdp", "ctx", None), P("fsdp", "ctx", None), P("fsdp"), P("fsdp"),
            P("fsdp", "tp"), P("fsdp", "tp"), P("fsdp", "tp"), P("fsdp", "tp"),
            P("fsdp"), P("fsdp", "tp"), P("fsdp", "tp"), P("fsdp", "tp"),
        ),
        out_specs=(
            P("fsdp", "ctx", None), P("fsdp", "ctx", None), P("fsdp"), P("fsdp", "tp"),
            P("fsdp", "tp"), P("fsdp", "tp"), P("fsdp", "tp"), P("fsdp"),
            P("fsdp", "tp"), P("fsdp", "tp"), P("fsdp", "tp"),
        ),
        check_vma=False,
    )
```

```python
import math

import jax
import jax.numpy as jnp
from jax import lax
from jax.experimental import pallas as pl
from jax.experimental.pallas import tpu as pltpu
from jax.sharding import PartitionSpec as P

HEAD_SIZE = 64
EPSILON = 1e-05
THETA = 500000.0
MASKED = -1e30
F32 = jnp.float32
BF16 = jnp.bfloat16


def contract(left, right, left_dim, right_dim):
    return lax.dot_general(
        left, right, (((left_dim,), (right_dim,)), ((), ())), preferred_element_type=F32
    )


def rope_tables(row_start, row_count):
    position = (row_start + jnp.arange(row_count, dtype=jnp.int32)).astype(F32)
    exponent = jnp.arange(HEAD_SIZE // 2, dtype=jnp.int32).astype(F32) * (2.0 / HEAD_SIZE)
    angles = position[:, None] * jnp.power(THETA, -exponent)[None, :]
    return (jnp.cos(angles), jnp.sin(angles))


def apply_rotary(values, cosine_lookup, sine_lookup, direction):
    half_width = values.shape[1] // 2
    leading = values[:, :half_width]
    trailing = values[:, half_width:]
    sin = direction * sine_lookup
    return jnp.concatenate(
        [leading * cosine_lookup - trailing * sin, trailing * cosine_lookup + leading * sin],
        axis=1,
    )


def allowed_pairs(bounds_ref, shape):
    key_place = lax.broadcasted_iota(jnp.int32, shape, 0)
    query_place = bounds_ref[1] + lax.broadcasted_iota(jnp.int32, shape, 1)
    return (key_place <= query_place) | (key_place < bounds_ref[0])


SCORE_SCALE = 1.0 / math.sqrt(HEAD_SIZE)
SMEM_SPEC = pl.BlockSpec(memory_space=pltpu.SMEM)


def attend(bounds, queries, keys, values_flat):
    heads, _, rows = queries.shape
    places = keys.shape[1]
    group = heads // keys.shape[0]

    def kernel(bounds_ref, query_ref, key_ref, value_ref, out_ref, log_ref):
        @pl.loop(0, heads)
        def _(h):
            k = h // group
            scores = jnp.dot(key_ref[k], query_ref[h], preferred_element_type=F32) * SCORE_SCALE
            scores = jnp.where(allowed_pairs(bounds_ref, (places, rows)), scores, MASKED)
            peak = jnp.max(scores, axis=0, keepdims=True)
            weights = jnp.exp(scores - peak)
            total = jnp.sum(weights, axis=0, keepdims=True)
            probabilities = (weights * (1.0 / total)).astype(BF16)
            out_ref[h] = jnp.dot(
                value_ref[k], probabilities, preferred_element_type=F32
            ).astype(BF16)
            log_ref[h] = peak + jnp.log(total)

    return pl.pallas_call(
        kernel,
        out_shape=(
            jax.ShapeDtypeStruct(queries.shape, BF16),
            jax.ShapeDtypeStruct((heads, 1, rows), F32),
        ),
        in_specs=[SMEM_SPEC] + [pl.BlockSpec(memory_space=pltpu.VMEM)] * 3,
        out_specs=(pl.BlockSpec(memory_space=pltpu.VMEM),) * 2,
        compiler_params=pltpu.CompilerParams(vmem_limit_bytes=24 << 20),
    )(bounds, queries, keys, values_flat)


def attend_back(bounds, queries, keys, keys_flat, values, grads, log_total):
    heads, size, rows = queries.shape
    key_heads, places, _ = keys.shape
    group = heads // key_heads

    def kernel(
        bounds_ref, query_ref, key_ref, key_flat_ref, value_ref, grad_ref, log_ref, query_grad_ref,
        both_grad_ref, totals,
    ):
        totals[...] = jnp.zeros_like(totals)

        @pl.loop(0, heads)
        def _(h):
            k = h // group
            scores = jnp.dot(key_ref[k], query_ref[h], preferred_element_type=F32) * SCORE_SCALE
            scores = jnp.where(allowed_pairs(bounds_ref, (places, rows)), scores, MASKED)
            probabilities = jnp.exp(scores - log_ref[h])
            grad_probs = jnp.dot(value_ref[k], grad_ref[h], preferred_element_type=F32)
            delta = jnp.sum(probabilities * grad_probs, axis=0, keepdims=True)
            grad_scores = (probabilities * (grad_probs - delta)).astype(BF16)
            query_grad_ref[h] = SCORE_SCALE * jnp.dot(
                key_flat_ref[k], grad_scores, preferred_element_type=F32
            )
            totals[k] += SCORE_SCALE * contract(query_ref[h], grad_scores, 1, 1)
            totals[key_heads + k] += contract(grad_ref[h], probabilities.astype(BF16), 1, 1)

        both_grad_ref[...] = totals[...].astype(BF16)

    return pl.pallas_call(
        kernel,
        out_shape=(
            jax.ShapeDtypeStruct(queries.shape, F32),
            jax.ShapeDtypeStruct((2 * key_heads, size, places), BF16),
        ),
        in_specs=[SMEM_SPEC] + [pl.BlockSpec(memory_space=pltpu.VMEM)] * 6,
        out_specs=(pl.BlockSpec(memory_space=pltpu.VMEM),) * 2,
        scratch_shapes=[pltpu.VMEM((2 * key_heads, size, places), F32)],
        compiler_params=pltpu.CompilerParams(vmem_limit_bytes=32 << 20),
    )(bounds, queries, keys, keys_flat, values, grads, log_total)


MESH = pl.DeviceIdType.MESH
HBM_SPEC = pl.BlockSpec(memory_space=pl.ANY)
VMEM_SPEC = pl.BlockSpec(memory_space=pltpu.VMEM)
DMA = pltpu.SemaphoreType.DMA


def remote(src, dst, send, recv, peer):
    return pltpu.make_async_remote_copy(
        src_ref=src, dst_ref=dst, send_sem=send, recv_sem=recv, device_id=peer, device_id_type=MESH
    )


def rows_at(ref, start, count):
    return ref.at[pl.ds(pl.multiple_of(start, count), count)]


def guarded(condition, body):
    if condition is None:
        body()
    else:
        pl.when(condition)(body)


def tp_peers(tp_size):
    me = lax.axis_index("tp")
    core = lax.rem(me, 2)
    level = me // 2
    levels = tp_size // 2
    partner = me + 1 - 2 * core
    others = [lax.rem(level + step, levels) * 2 + core for step in range(1, levels)]
    return me, core, level, partner, others


def enter(ctx_size, tp_size, along=False, pair=False, side=False, tensor=True, line=False):
    place = lax.axis_index("ctx")
    barrier = pltpu.get_barrier_semaphore()

    def greet(peer):
        pl.semaphore_signal(barrier, inc=1, device_id=peer, device_id_type=MESH)

    count = 0
    if tensor:
        _, _, _, partner, others = tp_peers(tp_size)
        for peer in [partner] + others:
            greet({"tp": peer})
        count = count + 1 + len(others)
    if side:
        greet({"fsdp": 1 - lax.axis_index("fsdp")})
        count = count + 1
    if along:
        up = place + 1 < ctx_size
        down = place > 0

        @pl.when(up)
        def _():
            greet({"ctx": place + 1})

        @pl.when(down)
        def _():
            greet({"ctx": place - 1})

        count = count + up.astype(jnp.int32) + down.astype(jnp.int32)
    if pair:
        greet({"ctx": place + 1 - 2 * lax.rem(place, 2)})
        count = count + 1
    if line:
        for step in range(1, ctx_size):
            greet({"ctx": lax.rem(place + step, ctx_size)})
        count = count + ctx_size - 1
    pl.semaphore_wait(barrier, count)


def gather_sems(ctx_size, tp_size):
    spread = 2 * ctx_size - 1
    levels = tp_size // 2
    chips = max(levels - 1, 1)
    return [
        DMA((spread + 1,)), DMA((spread,)), DMA((chips, spread)), DMA((chips, spread)),
        DMA((levels, spread)), DMA((levels, spread)), DMA((1,)),
    ]


def gather_rows(mine, all_ref, ctx_size, tp_size, sems, block=None):
    hop_send, hop_recv, chip_send, chip_recv, core_send, core_recv, own_sem = sems
    place = lax.axis_index("ctx") if ctx_size > 1 else 0
    me, core, level, partner, others = tp_peers(tp_size)
    levels = tp_size // 2
    rows = mine.shape[0]
    middle = ctx_size - 1
    offsets = [0]
    for step in range(1, ctx_size):
        offsets += [-step, step]

    def spot(offset, who):
        return rows_at(all_ref, ((place + offset) * tp_size + who) * rows, rows)

    def hop(offset, step, src):
        slot = 2 * middle + 1 if offset == 0 and step < 0 else middle + offset
        return remote(
            src, spot(offset, me), hop_send.at[slot], hop_recv.at[middle + offset - step],
            {"ctx": place + step},
        )

    def hop_arrival(offset):
        step = -1 if offset < 0 else 1
        return remote(
            spot(offset, me), spot(offset, me), hop_send.at[middle + offset],
            hop_recv.at[middle + offset], {"ctx": place + step},
        )

    def chip(offset, index, src):
        return remote(
            src, spot(offset, me), chip_send.at[index, middle + offset],
            chip_recv.at[levels - 2 - index, middle + offset], {"tp": others[index]},
        )

    def chip_arrival(offset, index):
        where = spot(offset, others[index])
        return remote(
            where, where, chip_send.at[index, middle + offset],
            chip_recv.at[index, middle + offset], {"tp": others[index]},
        )

    def to_core(offset, index, who, src):
        return remote(
            src, spot(offset, who), core_send.at[index, middle + offset],
            core_recv.at[index, middle + offset], {"tp": partner},
        )

    def valid(offset):
        if offset == 0:
            return None
        return place + offset >= 0 if offset < 0 else place + offset < ctx_size

    def onward(offset):
        if offset < 0:
            return 1, jnp.logical_and(place + offset >= 0, place + 1 < ctx_size)
        return -1, jnp.logical_and(place + offset < ctx_size, place > 0)

    def fan_out(offset, src):
        for index in range(levels - 1):
            chip(offset, index, src).start()
        to_core(offset, 0, me, src).start()

    if block is None:
        own = pltpu.make_async_copy(mine, spot(0, me), own_sem.at[0])
    else:
        own = pltpu.make_async_copy(
            block, rows_at(all_ref, place * block.shape[0], block.shape[0]), own_sem.at[0]
        )
    own.start()
    if ctx_size > 1:
        @pl.when(place + 1 < ctx_size)
        def _():
            hop(0, 1, mine).start()

        @pl.when(place > 0)
        def _():
            hop(0, -1, mine).start()

    if block is None:
        fan_out(0, mine)
    for offset in offsets[1:]:
        def arrived(offset=offset):
            hop_arrival(offset).wait_recv()
            fan_out(offset, spot(offset, me))

        guarded(valid(offset), arrived)
        step, more = onward(offset)

        @pl.when(more)
        def _(offset=offset, step=step):
            hop(offset, step, spot(offset, me)).start()

    shared = offsets if block is None else offsets[1:]
    for offset in shared:
        def relay(offset=offset):
            for index in range(levels - 1):
                chip_arrival(offset, index).wait_recv()
                to_core(offset, 1 + index, others[index], spot(offset, others[index])).start()

        guarded(valid(offset), relay)

    for offset in shared:
        def drain(offset=offset):
            for index in range(levels):
                to_core(offset, index, me, spot(offset, me)).wait()
            for index in range(levels - 1):
                chip(offset, index, spot(offset, me)).wait_send()

        guarded(valid(offset), drain)
    own.wait()
    if ctx_size > 1:
        @pl.when(place + 1 < ctx_size)
        def _():
            hop(0, 1, mine).wait_send()

        @pl.when(place > 0)
        def _():
            hop(0, -1, mine).wait_send()

        for offset in offsets[1:]:
            step, more = onward(offset)

            @pl.when(more)
            def _(offset=offset, step=step):
                hop(offset, step, spot(offset, me)).wait_send()


def line_sems(ctx_size):
    spread = 2 * ctx_size - 1
    return [DMA((spread + 1,)), DMA((spread,)), DMA((1,))]


def line_gather(mine, all_ref, ctx_size, sems):
    hop_send, hop_recv, own_sem = sems
    place = lax.axis_index("ctx")
    rows = mine.shape[0]
    middle = ctx_size - 1
    offsets = [o for step in range(1, ctx_size) for o in (-step, step)]

    def spot(offset):
        return rows_at(all_ref, (place + offset) * rows, rows)

    def hop(offset, step, src):
        slot = 2 * middle + 1 if offset == 0 and step < 0 else middle + offset
        return remote(
            src, spot(offset), hop_send.at[slot], hop_recv.at[middle + offset - step],
            {"ctx": place + step},
        )

    def arrival(offset):
        step = -1 if offset < 0 else 1
        return remote(
            spot(offset), spot(offset), hop_send.at[middle + offset],
            hop_recv.at[middle + offset], {"ctx": place + step},
        )

    def valid(offset):
        return place + offset >= 0 if offset < 0 else place + offset < ctx_size

    def onward(offset):
        if offset < 0:
            return 1, jnp.logical_and(place + offset >= 0, place + 1 < ctx_size)
        return -1, jnp.logical_and(place + offset < ctx_size, place > 0)

    own = pltpu.make_async_copy(mine, spot(0), own_sem.at[0])
    ends = ((1, place + 1 < ctx_size), (-1, place > 0))

    def begin():
        for step, there in ends:
            @pl.when(there)
            def _(step=step):
                hop(0, step, mine).start()

        own.start()

    def stage(step):
        for offset in (-step, step):
            @pl.when(valid(offset))
            def _(offset=offset):
                arrival(offset).wait_recv()

            way, more = onward(offset)

            @pl.when(more)
            def _(offset=offset, way=way):
                hop(offset, way, spot(offset)).start()

    def drain():
        own.wait()
        for step, there in ends:
            @pl.when(there)
            def _(step=step):
                hop(0, step, mine).wait_send()

        for offset in offsets:
            step, more = onward(offset)

            @pl.when(more)
            def _(offset=offset, step=step):
                hop(offset, step, spot(offset)).wait_send()

    return begin, stage, drain


class KvSum:
    side = False

    def __init__(self, grad_kv, ctx_size):
        self.ctx_size = ctx_size
        self.inputs = (grad_kv,)
        self.rows = grad_kv.shape[1] // ctx_size
        self.block = (grad_kv.shape[0], self.rows)
        self.outs = (jax.ShapeDtypeStruct(self.block, F32),)
        self.out_specs = (VMEM_SPEC,)
        self.scratch = [
            pltpu.VMEM((ctx_size, *self.block), BF16), DMA((ctx_size,)), DMA((ctx_size,)),
        ]

    def bind(self, in_refs, out_refs, side_refs, scratch):
        (grad_ref,) = in_refs
        (sum_ref,) = out_refs
        slots, send, recv = scratch
        ctx_size, rows = self.ctx_size, self.rows
        place = lax.axis_index("ctx")

        def to(step):
            peer = lax.rem(place + step, ctx_size)
            return remote(
                grad_ref.at[:, pl.ds(pl.multiple_of(peer * rows, rows), rows)], slots.at[place],
                send.at[step], recv.at[step], {"ctx": peer},
            )

        def arrival(step):
            src = lax.rem(place + ctx_size - step, ctx_size)
            return remote(slots.at[src], slots.at[src], send.at[step], recv.at[step], {"ctx": src})

        def begin():
            for step in range(1, ctx_size):
                to(step).start()
            slots[place] = grad_ref[:, pl.ds(pl.multiple_of(place * rows, rows), rows)]

        def middle():
            pass

        def end():
            for step in range(1, ctx_size):
                arrival(step).wait_recv()
            total = slots[0].astype(F32)
            for z in range(1, ctx_size):
                total += slots[z].astype(F32)
            sum_ref[...] = total
            for step in range(1, ctx_size):
                to(step).wait_send()

        return begin, middle, end


class AttnTail:
    side = True

    def __init__(self, pre_slabs, norm_all, gain_second, out_rows, mesh_shape):
        self.ctx_size, self.tp_size = mesh_shape
        self.inputs = (pre_slabs, norm_all, gain_second, out_rows)
        self.wide, self.rows = pre_slabs.shape[1:]
        self.out_wide = out_rows.shape[0] // self.ctx_size
        self.half = norm_all.shape[1] // 2
        levels = self.tp_size // 2
        self.levels = levels
        self.outs = (
            jax.ShapeDtypeStruct((self.ctx_size * self.wide, self.half), BF16),
            jax.ShapeDtypeStruct((self.ctx_size * self.out_wide, self.half), BF16),
            jax.ShapeDtypeStruct((2, self.half), F32),
        )
        self.out_specs = (HBM_SPEC, HBM_SPEC, VMEM_SPEC)
        chips = max(levels - 1, 1)
        self.scratch = [
            pltpu.VMEM(pre_slabs.shape, BF16),
            pltpu.VMEM((self.wide, self.half), F32),
            pltpu.VMEM((self.wide, self.half), BF16),
            pltpu.VMEM((self.wide, self.half), BF16),
            pltpu.VMEM((self.wide, self.half), BF16),
            pltpu.VMEM((4, 2, self.half), F32),
            pltpu.VMEM((levels, 2, self.half), F32),
            pltpu.VMEM((self.ctx_size, 2, self.half), F32),
            DMA((self.ctx_size,)), DMA((self.ctx_size,)),
            DMA((6,)),
            DMA((chips,)), DMA((chips,)),
            DMA((self.ctx_size,)), DMA((self.ctx_size,)),
        ] + line_sems(self.ctx_size) + [
            pltpu.VMEM((self.ctx_size, self.out_wide, self.half), BF16),
            DMA((self.ctx_size,)), DMA((self.ctx_size,)),
            pltpu.VMEM((self.out_wide, self.half), BF16),
        ] + line_sems(self.ctx_size)

    def bind(self, in_refs, out_refs, side_refs, scratch):
        pre_ref, norm_ref, gain_second_ref, out_ref = in_refs
        all_ref, out_all_ref, gains_ref = out_refs
        slabs, own_half, far_half, from_far, quarter, swaps, by_level, by_place = scratch[:8]
        all_send, all_recv, duo, lev_send, lev_recv, ctx_send, ctx_recv = scratch[8:15]
        ctx_size, levels, half, rows = self.ctx_size, self.levels, self.half, self.rows
        place = lax.axis_index("ctx")
        _, _, level, partner, others = tp_peers(self.tp_size)
        far = {"fsdp": 1 - lax.axis_index("fsdp")}
        tile = min(512, half)
        line_begin, line_stage, line_drain = line_gather(quarter, all_ref, ctx_size, scratch[15:18])
        out_slots, out_send, out_recv, out_quarter = scratch[18:22]
        out_wide = self.out_wide
        out_begin, out_stage, out_drain = line_gather(
            out_quarter, out_all_ref, ctx_size, scratch[22:25]
        )

        def out_slab(step):
            peer = lax.rem(place + step, ctx_size)
            return remote(
                rows_at(out_ref, peer * out_wide, out_wide), out_slots.at[place],
                out_send.at[step], out_recv.at[step], {"ctx": peer},
            )

        def out_arrival(step):
            src = lax.rem(place + ctx_size - step, ctx_size)
            where = out_slots.at[src]
            return remote(where, where, out_send.at[step], out_recv.at[step], {"ctx": src})

        def slab(step):
            peer = lax.rem(place + step, ctx_size)
            return remote(
                pre_ref.at[peer], slabs.at[place], all_send.at[step], all_recv.at[step], {"ctx": peer}
            )

        def slab_arrival(step):
            src = lax.rem(place + ctx_size - step, ctx_size)
            return remote(
                slabs.at[src], slabs.at[src], all_send.at[step], all_recv.at[step], {"ctx": src}
            )

        grads = remote(far_half, from_far, duo.at[0], duo.at[1], far)
        gain_x = remote(swaps.at[0], swaps.at[1], duo.at[2], duo.at[3], far)
        gain_core = remote(swaps.at[2], swaps.at[3], duo.at[4], duo.at[5], {"tp": partner})

        def gain_level(index):
            return remote(
                by_level.at[level], by_level.at[level], lev_send.at[index],
                lev_recv.at[levels - 2 - index], {"tp": others[index]},
            )

        def gain_level_arrival(index):
            where = by_level.at[lax.rem(level + 1 + index, levels)]
            return remote(where, where, lev_send.at[index], lev_recv.at[index], {"tp": others[index]})

        def gain_place(step):
            peer = lax.rem(place + step, ctx_size)
            return remote(
                by_place.at[place], by_place.at[place], ctx_send.at[step], ctx_recv.at[step],
                {"ctx": peer},
            )

        def gain_place_arrival(step):
            src = lax.rem(place + ctx_size - step, ctx_size)
            where = by_place.at[src]
            return remote(where, where, ctx_send.at[step], ctx_recv.at[step], {"ctx": src})

        def product(at):
            columns = pl.ds(pl.multiple_of(at, tile), tile)
            total = jnp.dot(
                slabs[0], norm_ref[0:rows, columns], preferred_element_type=F32
            )
            for z in range(1, ctx_size):
                total += jnp.dot(
                    slabs[z], norm_ref[z * rows : (z + 1) * rows, columns],
                    preferred_element_type=F32,
                )
            return total

        def begin():
            for step in range(1, ctx_size):
                slab(step).start()
            slabs[place] = pre_ref[place]
            out_slots[place] = out_ref[pl.ds(pl.multiple_of(place * out_wide, out_wide), out_wide), :]

        def middle():
            for step in range(1, ctx_size):
                slab_arrival(step).wait_recv()
            for step in range(1, ctx_size):
                out_slab(step).start()

            @pl.loop(0, half // tile)
            def _(i):
                far_half[:, pl.ds(pl.multiple_of(i * tile, tile), tile)] = product(
                    half + i * tile
                ).astype(BF16)

            grads.start()

            @pl.loop(0, half // tile)
            def _(i):
                own_half[:, pl.ds(pl.multiple_of(i * tile, tile), tile)] = product(i * tile)

        def end():
            gain_first = side_refs[0]
            swaps[0, 0:1, :] = gain_first[:, half:]
            swaps[0, 1:2, :] = gain_second_ref[:, half:]
            gain_x.start()
            grads.wait_recv()
            quarter[...] = (own_half[...] + from_far[...].astype(F32)).astype(BF16)
            line_begin()
            gain_x.wait_recv()
            swaps[2, 0:1, :] = gain_first[:, :half] + swaps[1, 0:1, :]
            swaps[2, 1:2, :] = gain_second_ref[:, :half] + swaps[1, 1:2, :]
            gain_core.start()
            for step in range(1, ctx_size):
                out_arrival(step).wait_recv()
            total = out_slots[0].astype(F32)
            for z in range(1, ctx_size):
                total += out_slots[z].astype(F32)
            out_quarter[...] = total.astype(BF16)
            out_begin()
            gain_core.wait_recv()
            by_level[level] = swaps[2] + swaps[3]
            for index in range(levels - 1):
                gain_level(index).start()
            line_stage(1)
            for index in range(levels - 1):
                gain_level_arrival(index).wait_recv()
            total = by_level[0]
            for lev in range(1, levels):
                total += by_level[lev]
            by_place[place] = total
            for step in range(1, ctx_size):
                gain_place(step).start()
            out_stage(1)
            for step in range(2, ctx_size):
                line_stage(step)
                out_stage(step)
            for step in range(1, ctx_size):
                gain_place_arrival(step).wait_recv()
            total = by_place[0]
            for z in range(1, ctx_size):
                total += by_place[z]
            gains_ref[...] = total
            line_drain()
            out_drain()
            for step in range(1, ctx_size):
                slab(step).wait_send()
                out_slab(step).wait_send()
                gain_place(step).wait_send()
            for index in range(levels - 1):
                gain_level(index).wait_send()
            grads.wait_send()
            gain_x.wait_send()
            gain_core.wait_send()

        return begin, middle, end


def reduce_gather(term, extras, finish, side_shapes, mesh_shape, identity, blocks, across, aside=None):
    ctx_size, tp_size = mesh_shape
    levels = tp_size // 2
    width = term.shape[1]
    block_rows = term.shape[0] // blocks
    rows = block_rows // tp_size
    reach = ctx_size if across else 1
    beside = aside is not None
    aside_inputs = aside.inputs if beside else ()
    aside_outs = aside.outs if beside else ()
    aside_scratch = aside.scratch if beside else []

    def kernel(term_ref, *refs):
        extra_refs = refs[: len(extras)]
        refs = refs[len(extras) :]
        aside_in = refs[: len(aside_inputs)]
        refs = refs[len(aside_inputs) :]
        all_ref = refs[0]
        side_refs = refs[1 : 1 + len(side_shapes)]
        refs = refs[1 + len(side_shapes) :]
        aside_out = refs[: len(aside_outs)]
        refs = refs[len(aside_outs) :]
        from_core, stage, from_chip, mine = refs[:4]
        refs = refs[4:]
        if blocks == 2:
            pair_stage, from_pair = refs[:2]
            refs = refs[2:]
        sems = refs[:7]
        core_send, core_recv, chip_send, chip_recv, pair_sems = refs[7:12]
        place = lax.axis_index("ctx")
        me, core, level, partner, others = tp_peers(tp_size)
        enter(
            ctx_size, tp_size, along=across, pair=blocks == 2 and not beside,
            side=beside and aside.side, line=beside,
        )
        if beside:
            aside_begin, aside_middle, aside_end = aside.bind(
                aside_in, aside_out, side_refs, refs[12:]
            )
            aside_begin()

        def to_core(block, lev):
            slot = block * levels + lev
            return remote(
                rows_at(term_ref, block * block_rows + (2 * lev + 1 - core) * rows, rows),
                from_core.at[slot], core_send.at[slot], core_recv.at[slot], {"tp": partner},
            )

        def to_chip(index):
            return remote(
                stage.at[index], from_chip.at[levels - 2 - index], chip_send.at[index],
                chip_recv.at[levels - 2 - index], {"tp": others[index]},
            )

        def chip_sum(block, lev):
            own = term_ref[
                pl.ds(pl.multiple_of(block * block_rows + (2 * lev + core) * rows, rows), rows), :
            ]
            return own.astype(F32) + from_core[block * levels + lev].astype(F32)

        for lev in range(levels):
            for block in range(blocks):
                to_core(block, lev).start()
        for lev in range(levels):
            for block in range(blocks):
                to_core(block, lev).wait_recv()
        for index in range(levels - 1):
            lev = lax.rem(level + 1 + index, levels)
            for block in range(blocks):
                stage[index, block * rows : (block + 1) * rows, :] = chip_sum(block, lev).astype(
                    BF16
                )
            to_chip(index).start()
        if beside:
            aside_middle()
        for index in range(levels - 1):
            to_chip(index).wait_recv()

        def tp_sum(block):
            total = chip_sum(block, level)
            for index in range(levels - 1):
                total += from_chip[
                    index, pl.ds(pl.multiple_of(block * rows, rows), rows), :
                ].astype(F32)
            return total

        if blocks == 2:
            low = lax.rem(place, 2)
            pair_stage[...] = tp_sum(1 - low).astype(BF16)
            swap = remote(
                pair_stage, from_pair, pair_sems.at[0], pair_sems.at[1], {"ctx": place + 1 - 2 * low}
            )
            swap.start()
            total = tp_sum(low)
            swap.wait_recv()
            total += from_pair[...].astype(F32)
        else:
            total = tp_sum(0)
        start = pl.multiple_of(me * rows, rows)
        mine[...] = finish(total, start, *extra_refs, *side_refs)
        gather_rows(mine, all_ref, reach, tp_size, sems)
        if beside:
            aside_end()
        for lev in range(levels):
            for block in range(blocks):
                to_core(block, lev).wait_send()
        for index in range(levels - 1):
            to_chip(index).wait_send()
        if blocks == 2:
            swap.wait_send()

    chips = max(levels - 1, 1)
    scratch = [
        pltpu.VMEM((blocks * levels, rows, width), BF16),
        pltpu.VMEM((chips, blocks * rows, width), BF16),
        pltpu.VMEM((chips, blocks * rows, width), BF16),
        pltpu.VMEM((rows, width), BF16),
    ]
    if blocks == 2:
        scratch += [pltpu.VMEM((rows, width), BF16)] * 2
    scratch += gather_sems(reach, tp_size)
    scratch += [
        DMA((blocks * levels,)), DMA((blocks * levels,)), DMA((chips,)), DMA((chips,)), DMA((2,)),
    ]
    scratch += aside_scratch
    return pl.pallas_call(
        kernel,
        out_shape=(
            jax.ShapeDtypeStruct((reach * block_rows, width), BF16),
            *(jax.ShapeDtypeStruct(shape, F32) for shape in side_shapes),
            *aside_outs,
        ),
        in_specs=[VMEM_SPEC] * (1 + len(extras) + len(aside_inputs)),
        out_specs=(HBM_SPEC,) + (VMEM_SPEC,) * len(side_shapes)
        + (aside.out_specs if beside else ()),
        scratch_shapes=scratch,
        compiler_params=pltpu.CompilerParams(
            collective_id=identity, has_side_effects=True, vmem_limit_bytes=32 << 20
        ),
    )(term, *extras, *aside_inputs)


def unit_places(place):
    low = place % 2
    part = ((place + 1) // 2) % 2
    base = 2 + 3 * part
    return [base, low, base + 1, base + 2, 1 - low], part


def opening(cot_rows, groups, gains, hidden_weights, mesh_shape, identity):
    ctx_size, tp_size = mesh_shape
    block_rows, width = cot_rows.shape
    rows = block_rows // tp_size
    weights = [w for group in groups for w in group]
    depth = weights[0].shape[0]
    places = []
    for g, group in enumerate(groups):
        at = 0
        for w in group:
            places.append((g, at, w.shape[1]))
            at += w.shape[1]
    wholes = [
        jax.ShapeDtypeStruct((2 * depth, sum(w.shape[1] for w in group)), BF16) for group in groups
    ]

    unit = hidden_weights[0].shape[1] // 8
    kinds = len(hidden_weights)

    def kernel(cot_ref, *refs):
        weight_refs = refs[: len(weights)]
        gain_ref = refs[len(weights)]
        refs = refs[len(weights) + 1 :]
        hidden_refs = refs[:kinds]
        refs = refs[kinds:]
        all_ref, gain_far_ref = refs[:2]
        whole_refs = refs[2 : 2 + len(groups)]
        refs = refs[2 + len(groups) :]
        pack_refs = refs[:5]
        refs = refs[5:]
        sems = refs[:7]
        send, recv, pack_sems = refs[7:]
        units, _ = unit_places(lax.axis_index("ctx"))
        packs = [
            pltpu.make_async_copy(
                hidden_refs[k].at[:, pl.ds(pl.multiple_of(at * unit, unit), unit)],
                pack_refs[c].at[:, pl.ds(k * unit, unit)], pack_sems.at[c * kinds + k],
            )
            for c, at in enumerate(units) for k in range(kinds)
        ]
        enter(ctx_size, tp_size, along=True, side=True)
        far = {"fsdp": 1 - lax.axis_index("fsdp")}
        last = len(weights)
        swaps = [remote(gain_ref, gain_far_ref, send.at[last], recv.at[last], far)]
        for i, (g, at, wide) in enumerate(places):
            swaps.append(
                remote(
                    weight_refs[i], whole_refs[g].at[pl.ds(depth, depth), pl.ds(at, wide)],
                    send.at[i], recv.at[i], far,
                )
            )
        for swap in swaps:
            swap.start()
        for pack in packs:
            pack.start()
        for i, (g, at, wide) in enumerate(places):
            whole_refs[g][0:depth, at : at + wide] = weight_refs[i][...]
        mine = rows_at(cot_ref, lax.axis_index("tp") * rows, rows)
        gather_rows(mine, all_ref, ctx_size, tp_size, sems, block=cot_ref)
        for pack in packs:
            pack.wait()
        for swap in swaps:
            swap.wait()

    return pl.pallas_call(
        kernel,
        out_shape=(
            jax.ShapeDtypeStruct((ctx_size * block_rows, width), BF16),
            jax.ShapeDtypeStruct(gains.shape, F32),
            *wholes,
            *[jax.ShapeDtypeStruct((depth, kinds * unit), BF16)] * 5,
        ),
        in_specs=[VMEM_SPEC] * (2 + len(weights)) + [HBM_SPEC] * kinds,
        out_specs=(HBM_SPEC,) + (VMEM_SPEC,) * (6 + len(groups)),
        scratch_shapes=gather_sems(ctx_size, tp_size)
        + [DMA((len(weights) + 1,)), DMA((len(weights) + 1,)), DMA((5 * kinds,))],
        compiler_params=pltpu.CompilerParams(
            collective_id=identity, has_side_effects=True, vmem_limit_bytes=40 << 20
        ),
    )(cot_rows, *weights, gains, *hidden_weights)


def place_blocks(table, pieces, wide, blocks, bases=None):
    count = len(pieces)
    depth, width = pieces[0].shape
    outs = width // wide

    def kernel(table_ref, *refs):
        which, step = pl.program_id(0), pl.program_id(1)
        for o in range(outs):
            for k in range(count):
                @pl.when(jnp.logical_and(which == o, step == k))
                def _(o=o, k=k):
                    refs[len(refs) - outs + o][...] = refs[k][...].astype(F32)

    def target(o):
        def index(which, step, table_ref):
            now = jnp.where(which < o, 0, jnp.where(which > o, count - 1, step))
            return 0, table_ref[now]

        return index

    shape = jax.ShapeDtypeStruct((depth, blocks * wide), F32)
    return pl.pallas_call(
        kernel,
        grid_spec=pltpu.PrefetchScalarGridSpec(
            num_scalar_prefetch=1,
            grid=(outs, count),
            in_specs=[
                pl.BlockSpec((depth, wide), lambda which, step, table_ref: (0, which))
            ] * count
            + [HBM_SPEC] * (0 if bases is None else outs),
            out_specs=tuple(pl.BlockSpec((depth, wide), target(o)) for o in range(outs)),
        ),
        out_shape=(shape,) * outs,
        input_output_aliases={} if bases is None else {1 + count + o: o for o in range(outs)},
        compiler_params=pltpu.CompilerParams(vmem_limit_bytes=32 << 20),
    )(table, *pieces, *(() if bases is None else bases))


def transposed_grads(columns, widths, last):
    depth = columns.shape[1]
    tile = min(depth, 256)
    widths = list(widths) + [last.shape[0]]

    def kernel(in_ref, last_ref, *out_refs):
        head = in_ref[...].astype(F32).T
        at = 0
        for out_ref, wide in zip(out_refs[:-1], widths[:-1]):
            out_ref[...] = head[:, at : at + wide]
            at += wide
        out_refs[-1][...] = last_ref[...].astype(F32).T

    return pl.pallas_call(
        kernel,
        grid=(depth // tile,),
        in_specs=[
            pl.BlockSpec((array.shape[0], tile), lambda i: (0, i)) for array in (columns, last)
        ],
        out_specs=tuple(pl.BlockSpec((tile, wide), lambda i: (i, 0)) for wide in widths),
        out_shape=tuple(jax.ShapeDtypeStruct((depth, wide), F32) for wide in widths),
    )(columns, last)


def mean_square(rows):
    return jnp.mean(rows * rows, axis=-1, keepdims=True)


def normalize_rows(rows, gain):
    count, width = rows.shape[0], rows.shape[1] // 2
    tile = min(count, 256)

    def kernel(row_ref, gain_ref, out_ref):
        values = row_ref[...].astype(F32)
        out_ref[...] = (
            values * lax.rsqrt(mean_square(values) + EPSILON) * gain_ref[...]
        ).astype(BF16)

    return pl.pallas_call(
        kernel,
        grid=(count // tile,),
        in_specs=[
            pl.BlockSpec((tile, width), lambda i: (i, 1)),
            pl.BlockSpec((1, width), lambda i: (0, 0)),
        ],
        out_specs=pl.BlockSpec((tile, width), lambda i: (i, 0)),
        out_shape=jax.ShapeDtypeStruct((count, width), BF16),
    )(rows, gain)


def finish_middle(total, start, resid_ref, gain_ref, middle_ref):
    rows = total.shape[0]
    middle = resid_ref[pl.ds(start, rows), :].astype(F32) + total
    middle_ref[...] = middle
    return (middle * lax.rsqrt(mean_square(middle) + EPSILON) * gain_ref[...]).astype(BF16)


def norm_back(grad, base, values, gain):
    rms = lax.rsqrt(mean_square(values) + EPSILON)
    scaled = grad * gain
    gain_grad = jnp.sum(grad * values * rms, axis=0, keepdims=True)
    cube = rms * rms * rms
    full = base + rms * scaled - values * cube * jnp.mean(scaled * values, axis=-1, keepdims=True)
    return full, gain_grad


def finish_grad_middle(total, start, middle_ref, cot_ref, gain_ref, grad_ref, gain_grad_ref):
    base = cot_ref[pl.ds(start, total.shape[0]), :].astype(F32)
    full, gain_grad = norm_back(total, base, middle_ref[...], gain_ref[...])
    grad_ref[...] = full
    gain_grad_ref[...] = gain_grad
    return full.astype(BF16)


def finish_grad_input(total, start, grad_ref, resid_ref, gain_ref, gain_grad_ref):
    values = resid_ref[pl.ds(start, total.shape[0]), :].astype(F32)
    full, gain_grad = norm_back(total, grad_ref[...], values, gain_ref[...])
    gain_grad_ref[...] = gain_grad
    return full.astype(BF16)


def finish_output(total, start, middle_ref):
    return (middle_ref[...] + total).astype(BF16)


def make_local(ctx_size, tp_size):
    mesh_shape = (ctx_size, tp_size)
    swap_x = [(0, 1), (1, 0)]
    swap_z = [(i, i ^ 1) for i in range(ctx_size)]

    def swap_rows(array):
        return lax.ppermute(array, "fsdp", swap_x)

    def local(
        inputs, cotangent, prefix, attn_gain, w_query, key_projection, value_projection, w_out,
        ffn_gain, w_gate, w_up, w_down,
    ):
        side = lax.axis_index("fsdp")
        place = lax.axis_index("ctx")
        units, part = unit_places(place)
        row_count, model_width = inputs.shape[1:]
        half_width = model_width // 2
        query_width = w_query.shape[1]
        key_width = key_projection.shape[1]
        ffn_width = w_gate.shape[1]
        unit = ffn_width // 8
        query_heads = query_width // HEAD_SIZE
        kv_heads = key_width // HEAD_SIZE
        row_start = place * row_count
        pair_start = (place // 2) * 2 * row_count

        def own_first(rows):
            a = lax.dynamic_slice_in_dim(rows, side * half_width, half_width, 1)
            b = lax.dynamic_slice_in_dim(rows, (1 - side) * half_width, half_width, 1)
            return jnp.concatenate([a, b], axis=1)

        gains = jnp.stack([attn_gain, ffn_gain]).astype(F32)
        residual_low = own_first(inputs[0])
        cot_low = own_first(cotangent[0])
        rows_all, gains_far, qkv_weight, out_weight, *owns = opening(
            jnp.concatenate([cot_low, residual_low], axis=1),
            ((w_query, jnp.concatenate([key_projection, value_projection], axis=1)), (w_out,)),
            gains, (w_gate, w_up, w_down), mesh_shape, 0,
        )
        cot_all = rows_all[:, :model_width]
        gains = jnp.concatenate([gains, gains_far], axis=1)
        gain_first, gain_second = gains[0], gains[1]
        others = [swap_rows(owns[0]), swap_rows(owns[1]), None, None, None]

        cosine_lookup, sine_lookup = (table.T for table in rope_tables(row_start, row_count))
        residual = residual_low.astype(F32)
        rms_first = lax.rsqrt(jnp.mean(residual * residual, axis=-1, keepdims=True) + EPSILON)
        normalized_rows = (residual * rms_first * gain_first).astype(BF16)
        qkv = contract(qkv_weight, normalized_rows, 0, 1)
        queries = apply_rotary(
            qkv[:query_width].reshape(query_heads, HEAD_SIZE, row_count),
            cosine_lookup, sine_lookup, 1.0,
        ).astype(BF16)
        key_rot = apply_rotary(
            qkv[query_width : query_width + key_width].reshape(kv_heads, HEAD_SIZE, row_count),
            cosine_lookup, sine_lookup, 1.0,
        ).astype(BF16)
        value_rows = qkv[query_width + key_width :].astype(BF16)
        kv_own = jnp.concatenate([key_rot, value_rows.reshape(kv_heads, HEAD_SIZE, row_count)], axis=0)
        kv_whole = lax.all_gather(
            kv_own.reshape(2 * key_width, row_count).T, "ctx", axis=0, tiled=True
        )
        length_total = kv_whole.shape[0]
        by_place = kv_whole.reshape(length_total, 2 * kv_heads, HEAD_SIZE).transpose(1, 0, 2)
        by_feature = kv_whole.T.reshape(2 * kv_heads, HEAD_SIZE, length_total)
        bounds = jnp.stack([prefix[0], row_start.astype(jnp.int32)])
        attended, log_total = attend(
            bounds, queries, by_place[:kv_heads], by_feature[kv_heads:]
        )
        attended_flat = attended.reshape(query_width, row_count)
        attn_term = contract(attended_flat, out_weight, 0, 1).astype(BF16)
        attn_term, owns[2], others[0] = lax.optimization_barrier((attn_term, owns[2], others[0]))
        others[2] = swap_rows(owns[2])
        slice_shape = (row_count // tp_size, model_width)
        normed_all, middle = reduce_gather(
            attn_term, (residual_low, gain_second[None]), finish_middle,
            (slice_shape,), mesh_shape, 1, 1, True,
        )

        ffn_term = 0.0
        mid_term = 0.0
        sides = []
        fars = []
        received = []

        def pair(rows):
            return lax.dynamic_slice_in_dim(rows, pair_start, 2 * row_count, 0)

        def outer(sides_of, part_of):
            return [contract(part_of(rows), cols, 0, 0) for rows, cols in sides_of]

        def near_of(c):
            return jnp.concatenate(outer(sides[c], lambda rows: rows[:, :half_width]), axis=1)

        def summed(c, near=None):
            near = near_of(c) if near is None else near
            return (near + received[c].astype(F32)).astype(BF16)

        def forward(c):
            both_w = jnp.concatenate([owns[c], others[c]], axis=0)
            pair_w, down_w = both_w[:, : 2 * unit], both_w[:, 2 * unit :]
            both = jnp.dot(normed_all, pair_w, preferred_element_type=F32)
            gating, upward = both[:, :unit], both[:, unit:]
            grad_hidden = jnp.dot(cot_all, down_w, preferred_element_type=F32)
            sigmoid_gate = jax.nn.sigmoid(gating)
            hidden = (gating * sigmoid_gate * upward).astype(BF16)
            grad_gating = (
                grad_hidden * upward * sigmoid_gate * (1.0 + gating * (1.0 - sigmoid_gate))
            ).astype(BF16)
            grad_upward = (grad_hidden * gating * sigmoid_gate).astype(BF16)
            grad_both = jnp.concatenate([grad_gating, grad_upward], axis=1)
            sides.append(((normed_all, grad_both), (cot_all, hidden)))
            far = outer(sides[c], lambda rows: rows[:, half_width:])
            fars.append(jnp.concatenate([f.astype(BF16) for f in far], axis=1))
            return pair_w, down_w, grad_both, hidden

        for c in range(4):
            if c:
                others[c], fars[-1] = lax.optimization_barrier((others[c], fars[-1]))
            if c == 1:
                owns[3], others[1] = lax.optimization_barrier((owns[3], others[1]))
                others[3] = swap_rows(owns[3])
                others[4] = lax.ppermute(others[1], "ctx", swap_z)
            if c == 3:
                others[3], others[4] = lax.optimization_barrier((others[3], others[4]))
            pair_w, down_w, grad_both, hidden = forward(c)
            ffn_term += contract(pair(hidden), down_w, 1, 1)
            mid_term += contract(pair(grad_both), pair_w, 1, 1)

        def swap_ctx(total):
            return lax.ppermute(total, "ctx", swap_z)

        received = {0: swap_rows(fars[0]), 2: swap_rows(fars[2])}
        totals, swapped = {}, {}
        mid_low, fars[1], fars[3], received[0] = lax.optimization_barrier(
            (mid_term.astype(BF16), fars[1], fars[3], received[0])
        )
        received[3] = swap_rows(fars[3])
        totals[0] = summed(0)
        mid_low, totals[0] = lax.optimization_barrier((mid_low, totals[0]))
        swapped[0] = swap_ctx(totals[0])
        branch_low, grad_middle, gain_grad_second = reduce_gather(
            mid_low, (middle, cot_low, gain_second[None]), finish_grad_middle,
            (slice_shape, (1, model_width)), mesh_shape, 2, 2, False,
        )
        branch_low, received[2], fars[1], swapped[0], rows_all = lax.optimization_barrier(
            (branch_low, received[2], fars[1], swapped[0], rows_all)
        )
        received[1] = swap_rows(fars[1])
        totals[2] = summed(2)
        near_one = near_of(1)
        branch_low, totals[2], near_one = lax.optimization_barrier(
            (branch_low, totals[2], near_one)
        )
        swapped[2] = swap_ctx(totals[2])
        grad_out = jnp.dot(attended_flat, branch_low, preferred_element_type=F32)
        grad_out_half = grad_out[:, half_width:].astype(BF16)
        grad_attended = contract(out_weight, branch_low, 0, 1).astype(BF16)
        grad_query_rot, grad_kv = attend_back(
            bounds, queries, by_place[:kv_heads], by_feature[:kv_heads], by_place[kv_heads:],
            grad_attended.reshape(query_heads, HEAD_SIZE, row_count), log_total,
        )
        grad_kv = grad_kv.reshape(2 * key_width, length_total)
        far_base = 2 + 3 * (1 - part)
        table = jnp.stack(units + [far_base, far_base + 1, far_base + 2])
        grad_kv, received[3] = lax.optimization_barrier((grad_kv, received[3]))
        totals[3] = summed(3)
        grad_kv, totals[3] = lax.optimization_barrier((grad_kv, totals[3]))
        swapped[3] = swap_ctx(totals[3])
        early = [totals[0], totals[2], totals[3], swapped[0]]
        placed = place_blocks(
            jnp.stack([table[0], table[2], table[3], table[5]]), early, unit, 8
        )
        placed, rows_all = lax.optimization_barrier((placed, rows_all))
        norm_all = normalize_rows(rows_all, gain_first[None])
        placed, norm_all = lax.optimization_barrier((placed, norm_all))
        others[4], placed, swapped[2], received[1], grad_out_half = lax.optimization_barrier(
            (others[4], placed, swapped[2], received[1], grad_out_half)
        )
        grad_out_far = swap_rows(grad_out_half)
        forward(4)
        near_four = near_of(4)
        totals[1] = summed(1, near_one)
        grad_kv, near_four, fars[4], totals[1] = lax.optimization_barrier(
            (grad_kv, near_four, fars[4], totals[1])
        )
        received[4] = swap_rows(fars[4])
        output_rows, grad_kv = reduce_gather(
            ffn_term.astype(BF16), (middle,), finish_output, (), mesh_shape, 3, 2, False,
            KvSum(grad_kv, ctx_size),
        )
        output_rows, grad_kv, swapped[3], grad_out_far = lax.optimization_barrier(
            (output_rows, grad_kv, swapped[3], grad_out_far)
        )
        grad_query_pre = apply_rotary(
            grad_query_rot, cosine_lookup, sine_lookup, -1.0
        ).astype(BF16).reshape(query_width, row_count)
        grad_key_pre = apply_rotary(
            grad_kv[:key_width].reshape(kv_heads, HEAD_SIZE, row_count),
            cosine_lookup, sine_lookup, -1.0,
        ).astype(BF16).reshape(key_width, row_count)
        grad_value_pre = grad_kv[key_width:].astype(BF16)
        grad_qkv_pre = jnp.concatenate([grad_query_pre, grad_key_pre, grad_value_pre], axis=0)
        attn_width = grad_qkv_pre.shape[0]
        pre_slabs = grad_qkv_pre.reshape(ctx_size, attn_width // ctx_size, row_count)
        normed_term = contract(grad_qkv_pre, qkv_weight, 0, 1).astype(BF16)
        grad_out_rows = (grad_out[:, :half_width] + grad_out_far.astype(F32)).astype(BF16)
        input_rows, _, grad_attn, grad_out, gain_grads = reduce_gather(
            normed_term,
            (grad_middle, residual_low, gain_first[None]), finish_grad_input,
            ((1, model_width),), mesh_shape, 4, 1, False,
            AttnTail(pre_slabs, norm_all, gain_grad_second, grad_out_rows, mesh_shape),
        )
        grad_attn, received[4] = lax.optimization_barrier((grad_attn, received[4]))
        grad_query, grad_key, grad_value, grad_out = transposed_grads(
            grad_attn, (query_width, key_width, key_width), grad_out
        )
        totals[4] = summed(4, near_four)

        late = jnp.stack([table[1], table[4], table[6], table[7]])
        result = place_blocks(
            late, [totals[1], totals[4], swapped[2], swapped[3]], unit, 8, placed
        )

        return (
            own_first(output_rows)[None],
            own_first(input_rows)[None],
            gain_grads[0],
            grad_query,
            grad_key,
            grad_value,
            grad_out,
            gain_grads[1],
            result[0],
            result[1],
            result[2],
        )

    return local


def solution(mesh):
    return jax.shard_map(
        make_local(mesh.shape["ctx"], mesh.shape["tp"]),
        mesh=mesh,
        in_specs=(
            P("fsdp", "ctx", None), P("fsdp", "ctx", None), P("fsdp"), P("fsdp"),
            P("fsdp", "tp"), P("fsdp", "tp"), P("fsdp", "tp"), P("fsdp", "tp"),
            P("fsdp"), P("fsdp", "tp"), P("fsdp", "tp"), P("fsdp", "tp"),
        ),
        out_specs=(
            P("fsdp", "ctx", None), P("fsdp", "ctx", None), P("fsdp"), P("fsdp", "tp"),
            P("fsdp", "tp"), P("fsdp", "tp"), P("fsdp", "tp"), P("fsdp"),
            P("fsdp", "tp"), P("fsdp", "tp"), P("fsdp", "tp"),
        ),
        check_vma=False,
    )
```
